32 devices in a mesh: seq: 16 (over z, y, x), dp: 2 (over core).
Axes of the slice: x: 2, y: 2, z: 4, core: 2. Of those that a mesh axis runs over, the one named last changes fastest.
Arguments:
- inputs: bfloat16 [8, 1536, 896], P('dp', 'seq'), may hold values from -6 to 6
- lengths: int32 [8, 9], P('dp'), may hold values from 0 to 1536, as said below
- w_qkv: bfloat16 [896, 1152], replicated, may hold values from -0.1875 to 0.1875
- b_qkv: bfloat16 [1152], replicated, may hold values from -3 to 3
- g_attn: bfloat16 [896], replicated, may hold values from 0.25 to 1.75
- w_out: bfloat16 [896, 896], replicated, may hold values from -1.5 to 1.5
- g_mlp: bfloat16 [896], replicated, may hold values from 0.25 to 1.75
- w_gate_up: bfloat16 [896, 9728], replicated, may hold values from -0.1875 to 0.1875
- w_down: bfloat16 [4864, 896], replicated, may hold values from -0.078125 to 0.078125
- cotangent: bfloat16 [8, 1536, 896], P('dp', 'seq'), may hold values from -6 to 6
Outputs:
- output: bfloat16 [8, 1536, 896], P('dp', 'seq')
- grad_input: float32 [8, 1536, 896], P('dp', 'seq')
- grad_qkv: float32 [896, 1152], P('seq')
- grad_bias_qkv: float32 [1152], replicated
- grad_norm_attn: float32 [896], replicated
- grad_out: float32 [896, 896], P('seq')
- grad_norm_mlp: float32 [896], replicated
- grad_gate_up: float32 [896, 9728], P('seq')
- grad_down: float32 [4864, 896], P('seq')
The draws below stay inside these ranges and needn't reach their ends.
Inputs may be any that keep to these rules, and one draw needn't show every extreme that they name: Each row lists the lengths of the documents packed one after another from the start of a stream; nonzero entries come first, and the tokens after their sum, fewer than 96, are padding. In every group of 4 consecutive rows one row is a single document of 1536 tokens; any other document has at most 4096 tokens.
All inputs are finite; a program needn't handle non-finite values.
Results may differ from the reference program's by a relative error of at most 0.014.
Values may be sent and summed in bfloat16 or wider, within the bound.
No kernel may reach another device: no remote copies, remote signals or barrier semaphores. Data moves between devices by JAX's collectives and lax.ppermute only.
A program may use at most 576 MiB of HBM per device.

```python
import jax
import jax.numpy as jnp
from jax import lax

D = 896
HEADS = 14
KVH = 2
HD = 64
FF = 4864
MB = 4
TOK_DEV = 96
STREAM = 1536
BATCH = 8
SEGS = 9
QW = 1152


def draw_lengths(key, part):
    octave_key, fine_key, pad_key, pick_key = jax.random.split(key, 4)
    octave = jax.random.randint(octave_key, (BATCH, SEGS), 0, 5)
    octave_scale = jnp.array([1, 2, 4, 8, 16], dtype=jnp.int32)[octave]
    raw_lengths = jnp.minimum(200 * octave_scale + jax.random.randint(fine_key, (BATCH, SEGS), 0, 200) * octave_scale, 4096)
    used = STREAM - jax.random.randint(pad_key, (BATCH, 1), 0, TOK_DEV)
    before = jnp.cumsum(raw_lengths, axis=1) - raw_lengths
    packed = jnp.clip(used - before, 0, raw_lengths)
    chosen = jax.random.randint(pick_key, (BATCH // MB, 1), 0, MB)
    full_row = (jnp.arange(MB, dtype=jnp.int32)[None, :] == chosen).reshape(BATCH)
    single = jnp.zeros((BATCH, SEGS), jnp.int32).at[:, 0].set(STREAM)
    return jnp.where(full_row[:, None], single, packed).astype(jnp.int32)


def spiked(drawn, key, source, target, parts, factor):
    owner, partner = [(jnp.arange(drawn.shape[dim]) // (drawn.shape[dim] // parts)).reshape([-1 if axis == dim else 1 for axis in range(drawn.ndim)]) for dim in (source, target)]
    chosen = jax.random.permutation(key, parts)[partner]
    strong = (owner == chosen) | (owner == (partner + parts // 2) % parts)
    return jnp.where(strong, factor * drawn, drawn)


def steps_of(rng, shape, shards, least, high):
    level, own = 1.0, jax.random.fold_in(rng, 6)
    for dim, blocks in shards:
        steps = jnp.exp(jax.random.uniform(jax.random.fold_in(own, dim), (blocks,), jnp.float32, least / len(shards), high / len(shards)))
        level = level * jnp.repeat(steps, shape[dim] // blocks).reshape([-1 if axis == dim else 1 for axis in range(len(shape))])
    return level


def gaussian(rng, shape, scale, most, cuts=(), kind=jnp.bfloat16):
    values = scale * jax.random.normal(rng, shape, jnp.float32)
    if cuts:
        values = values * steps_of(rng, shape, cuts, -0.22, 0.18)
    return jnp.clip(values, -most, most).astype(kind)


def gaussian_with(own_key, shape, width, reach, cuts, heavy, held_as=jnp.bfloat16):
    drawn = width * jax.random.normal(own_key, shape, jnp.float32)
    if cuts:
        drawn = drawn * steps_of(own_key, shape, cuts, -0.22, 0.18)
    return jnp.clip(spiked(drawn, jax.random.fold_in(own_key, 3), *heavy), -reach, reach).astype(held_as)


def setup_inputs(seed: int = 0) -> dict:
    splits = jax.random.split(jax.random.key(seed), 11)
    return {
        "inputs": gaussian_with(splits[0], (BATCH, STREAM, D), 1.0, 6.0, ((0, 2), (1, 16)), (1, 2, 16, 2.0)),
        "lengths": draw_lengths(jax.random.fold_in(splits[10], 71), 0),
        "w_qkv": gaussian(splits[2], (D, QW), D ** -0.5, 0.1875),
        "b_qkv": gaussian(splits[3], (QW,), 0.5, 3.0),
        "g_attn": jnp.clip(1.0 + 0.15 * jax.random.normal(splits[4], (D,), jnp.float32), 0.25, 1.75).astype(jnp.bfloat16),
        "w_out": gaussian(splits[5], (D, D), (D // 64) ** -0.5, 1.5),
        "g_mlp": jnp.clip(1.0 + 0.15 * jax.random.normal(splits[6], (D,), jnp.float32), 0.25, 1.75).astype(jnp.bfloat16),
        "w_gate_up": gaussian(splits[7], (D, 2 * FF), D ** -0.5, 0.1875),
        "w_down": gaussian(splits[8], (FF, D), FF ** -0.5, 0.078125),
        "cotangent": gaussian(splits[9], (BATCH, STREAM, D), 1.0, 6.0, ((0, 2), (1, 16))),
    }


@jax.custom_vjp
def low(v):
    return lax.optimization_barrier(v.astype(jnp.bfloat16)).astype(jnp.float32)

@jax.custom_vjp
def low_back(v):
    return v

def low_keep(v):
    return (low(v), None)

def low_pass(kept, grad):
    return (grad,)

def back_keep(v):
    return (v, None)

def back_low(kept, grad):
    return (low(grad),)
low.defvjp(low_keep, low_pass)
low_back.defvjp(back_keep, back_low)
epsilon = 1e-06
rope_base = 1000000.0
precise = lax.Precision.HIGHEST

def rms_scale(values, gain):
    return values * lax.rsqrt(lax.optimization_barrier(jnp.mean(values * values, axis=-1, keepdims=True)) + epsilon) * gain

def rotate(field, cos_table, sin_table):
    half = field.shape[-1] // 2
    first = field[..., :half]
    second = field[..., half:]
    return jnp.concatenate([first * cos_table - second * sin_table, second * cos_table + first * sin_table], axis=-1)

def layout(row_lengths, stream_len):
    places = jnp.arange(stream_len, dtype=jnp.int32)
    ends = jnp.cumsum(row_lengths, dtype=jnp.int32)
    after = (places[:, None] >= ends[None, :]).astype(jnp.int32)
    segment = lax.optimization_barrier(jnp.sum(after, axis=-1, dtype=jnp.int32))
    begins = lax.optimization_barrier(jnp.sum(after * row_lengths[None, :], axis=-1, dtype=jnp.int32))
    return (segment, places - begins, (places < ends[-1]).astype(jnp.float32))

def one_stream(params, stream_in, segment, position):
    w_qkv, b_qkv, g_attn, w_out, g_mlp, w_gate_up, w_down = params
    stream_len = stream_in.shape[0]
    q_width = HEADS * HD
    kv_width = KVH * HD
    normed = low(rms_scale(stream_in, g_attn))
    projected = jnp.dot(normed, w_qkv, precision=precise) + b_qkv
    q_linear = low_back(projected[:, :q_width])
    k_linear = low_back(projected[:, q_width:q_width + kv_width])
    v_linear = low_back(projected[:, q_width + kv_width:])
    half = HD // 2
    inverse = rope_base ** (-(jnp.arange(half, dtype=jnp.float32) * (2.0 / HD)))
    angle = position.astype(jnp.float32)[:, None] * inverse[None, :]
    cos_table = jnp.cos(angle)[:, None, :]
    sin_table = jnp.sin(angle)[:, None, :]
    queries = low(rotate(q_linear.reshape(stream_len, HEADS, HD), cos_table, sin_table))
    queries = queries.reshape(stream_len, KVH, HEADS // KVH, HD)
    key_rows = low(rotate(k_linear.reshape(stream_len, KVH, HD), cos_table, sin_table))
    value_rows = low(v_linear).reshape(stream_len, KVH, HD)
    row_block = min(512, stream_len)
    places = jnp.arange(stream_len, dtype=jnp.int32)
    factor = HD ** (-0.5)

    def attend(block_index):
        first_row = block_index * row_block
        query_part = lax.dynamic_slice_in_dim(queries, first_row, row_block, 0)
        query_seg = lax.dynamic_slice_in_dim(segment, first_row, row_block, 0)
        query_place = lax.dynamic_slice_in_dim(places, first_row, row_block, 0)
        scores = low_back(jnp.einsum('qhgd,khd->hgqk', query_part, key_rows, precision=precise) * factor)
        allowed = (query_seg[:, None] == segment[None, :]) & (query_place[:, None] >= places[None, :])
        masked = jnp.where(allowed[None, None], scores, -1e+30)
        row_max = lax.optimization_barrier(jnp.max(masked, axis=-1, keepdims=True))
        row_sum = lax.optimization_barrier(jnp.sum(jnp.exp(masked - row_max), axis=-1, keepdims=True))
        weights = low(jnp.exp(masked - row_max - jnp.log(row_sum)))
        return jnp.einsum('hgqk,khd->qhgd', weights, value_rows, precision=precise)
    mixed_out = lax.map(jax.checkpoint(attend), jnp.arange(stream_len // row_block, dtype=jnp.int32))
    mixed_low = low(low_back(mixed_out.reshape(stream_len, q_width)))
    middle = stream_in + low_back(jnp.dot(mixed_low, w_out, precision=precise))
    normed_mlp = low(rms_scale(middle, g_mlp))
    gate_up = jnp.dot(normed_mlp, w_gate_up, precision=precise)
    gate_pre = low_back(gate_up[:, :FF])
    up_pre = low_back(gate_up[:, FF:])
    active = low(jax.nn.silu(gate_pre) * up_pre)
    return middle + jnp.dot(active, w_down, precision=precise)

def reference(inputs, lengths, w_qkv, b_qkv, g_attn, w_out, g_mlp, w_gate_up, w_down, cotangent):
    params = tuple((weight.astype(jnp.float32) for weight in (w_qkv, b_qkv, g_attn, w_out, g_mlp, w_gate_up, w_down)))
    segment, position, valid_rows = jax.vmap(lambda row_lengths: layout(row_lengths, STREAM))(lengths)
    step = jax.checkpoint(one_stream)

    def forward(weights, streams_in):

        def scan_body(running, item):
            return (running, step(weights, item[0], item[1], item[2]))
        unused, stacked = lax.scan(scan_body, jnp.zeros((), jnp.float32), (streams_in, segment, position))
        return stacked
    result, pullback = jax.vjp(forward, params, inputs.astype(jnp.float32))
    gradients, grad_input = pullback(cotangent.astype(jnp.float32) * valid_rows[..., None])
    return (result.astype(jnp.bfloat16), grad_input, gradients[0], gradients[1], gradients[2], gradients[3], gradients[4], gradients[5], gradients[6])
```

```python
import functools

import jax
import jax.numpy as jnp
import numpy as np
from jax import lax
from jax.experimental import pallas as pl
from jax.experimental.pallas import tpu as pltpu
from jax.sharding import Mesh
from jax.sharding import PartitionSpec as P

HEADS = 14
KVH = 2
HD = 64
FF = 4864
QW = HEADS * HD
KW = KVH * HD
LANES = 128
GROUP = 4
NEG = -1e30
epsilon = 1e-06
rope_base = 1000000.0
BF = jnp.bfloat16
F32 = jnp.float32
SEQ = ("az", "ay", "ax")

SAME = [h for h in range(HEADS) if h % 2 == h // (HEADS // KVH)]
OTHER = [h for h in range(HEADS) if h % 2 != h // (HEADS // KVH)]


def nt(a, b):
    return lax.dot_general(a, b, (((1,), (1,)), ((), ())), preferred_element_type=F32)


def tn(a, b):
    return lax.dot_general(a, b, (((0,), (0,)), ((), ())), preferred_element_type=F32)


def nn(a, b):
    return lax.dot_general(a, b, (((1,), (0,)), ((), ())), preferred_element_type=F32)


def lane_iota(shape):
    return lax.broadcasted_iota(jnp.int32, shape, len(shape) - 1)


def half_swap(tile):
    low = lane_iota(tile.shape) % HD < HD // 2
    return jnp.where(low, pltpu.roll(tile, LANES - HD // 2, 1), pltpu.roll(tile, HD // 2, 1))


def params(limit=56):
    return pltpu.CompilerParams(vmem_limit_bytes=limit << 20)


def project_kernel(x_ref, w_ref, b_ref, g_ref, cos_ref, sin_ref, normed_ref, q_ref, kv_ref):
    x = x_ref[...].astype(F32)
    inv = lax.rsqrt(jnp.mean(x * x, axis=-1, keepdims=True) + epsilon)
    normed = (x * inv * g_ref[...].astype(F32)).astype(BF)
    normed_ref[...] = normed
    cos = cos_ref[...]
    sin = sin_ref[...]
    for first in range(0, QW + 2 * KW, LANES):
        cols = slice(first, first + LANES)
        part = nn(normed, w_ref[:, cols]) + b_ref[:, cols].astype(F32)
        if first < QW + KW:
            part = part * cos + half_swap(part) * sin
        if first < QW:
            q_ref[:, cols] = (part * HD**-0.5).astype(BF)
        else:
            kv_ref[:, first - QW : first - QW + LANES] = part.astype(BF)


def project(x, w, b, g, cos, sin):
    tokens, width = x.shape
    return pl.pallas_call(
        project_kernel,
        out_shape=(
            jax.ShapeDtypeStruct((tokens, width), BF),
            jax.ShapeDtypeStruct((tokens, QW), BF),
            jax.ShapeDtypeStruct((tokens, 2 * KW), BF),
        ),
        compiler_params=params(),
        name="project",
    )(x, w, b.reshape(1, -1), g.reshape(1, -1), cos, sin)


def masked_heads(ref, heads, scratch, rows):
    lane = lane_iota((rows, LANES))
    for slot, h in enumerate(heads):
        pair = ref[0, :, h // 2 * LANES : h // 2 * LANES + LANES]
        keep = (lane >= HD) if h % 2 else (lane < HD)
        scratch[slot * rows : (slot + 1) * rows, :LANES] = jnp.where(keep, pair, jnp.zeros_like(pair))


def forward_kernel(low_ref, me_ref, q_ref, kv_ref, start_ref, out_ref, lse_ref, qa, qb, ma, la, oa, mb, lb, ob):
    rows = q_ref.shape[1]
    stream = pl.program_id(0)
    me = me_ref[0]
    masked_heads(q_ref, SAME, qa, rows)
    masked_heads(q_ref, OTHER, qb, rows)
    for m, l, o in ((ma, la, oa), (mb, lb, ob)):
        m[...] = jnp.full_like(m, NEG)
        l[...] = jnp.zeros_like(l)
        o[...] = jnp.zeros_like(o)
    keys = GROUP * rows
    place = me * rows + lax.broadcasted_iota(jnp.int32, (rows, keys), 0)
    start = start_ref[0]

    def step(j, carry):
        block = kv_ref[pl.ds(j * GROUP, GROUP), 0].reshape(keys, 2 * KW)
        key = block[:, :KW]
        value = block[:, KW:]
        index = j * keys + lane_iota((rows, keys))
        allowed = (index <= place) & (index >= start)
        for swap, q, m, l, o in ((False, qa, ma, la, oa), (True, qb, mb, lb, ob)):
            count = q.shape[0] // rows
            k = jnp.concatenate([key[:, HD:], key[:, :HD]], 1) if swap else key
            v = jnp.concatenate([value[:, HD:], value[:, :HD]], 1) if swap else value
            s = nt(q[...], k).reshape(count, rows, keys)
            s = jnp.where(allowed[None], s, NEG)
            before = m[...].reshape(count, rows, 1)
            top = jnp.maximum(before, jnp.max(s, axis=-1, keepdims=True))
            p = jnp.where(allowed[None], jnp.exp(s - top), 0.0)
            shrink = jnp.exp(before - top).reshape(count * rows, 1)
            m[...] = top.reshape(count * rows, 1)
            l[...] = l[...] * shrink + jnp.sum(p, axis=-1, keepdims=True).reshape(count * rows, 1)
            o[...] = o[...] * shrink + nn(p.astype(BF).reshape(count * rows, keys), v)
        return carry

    lax.fori_loop(low_ref[stream], me // GROUP + 1, step, 0)
    lane = lane_iota((rows, LANES))
    lse = jnp.zeros((rows, LANES), F32)
    parts = {}
    for heads, m, l, o in ((SAME, ma, la, oa), (OTHER, mb, lb, ob)):
        for slot, h in enumerate(heads):
            at = slice(slot * rows, (slot + 1) * rows)
            total = l[at]
            lse = jnp.where(lane == h, m[at] + jnp.log(total), lse)
            parts[h] = o[at] / total
    lse_ref[0] = lse
    for pair in range(HEADS // 2):
        both = jnp.where(lane < HD, parts[2 * pair], parts[2 * pair + 1])
        out_ref[0, :, pair * LANES : (pair + 1) * LANES] = both.astype(BF)


def attend(q, kv_all, start, low, me):
    streams, rows, width = q.shape
    n = kv_all.shape[0]
    a, b = len(SAME) * rows, len(OTHER) * rows
    column = lambda count: pltpu.VMEM((count, 1), F32)
    return pl.pallas_call(
        forward_kernel,
        grid_spec=pltpu.PrefetchScalarGridSpec(
            num_scalar_prefetch=2,
            grid=(streams,),
            in_specs=[
                pl.BlockSpec((1, rows, width), lambda s, *_: (s, 0, 0)),
                pl.BlockSpec((n, 1, rows, 2 * KW), lambda s, *_: (0, s, 0, 0)),
                pl.BlockSpec((1, rows, 1), lambda s, *_: (s, 0, 0)),
            ],
            out_specs=[
                pl.BlockSpec((1, rows, width), lambda s, *_: (s, 0, 0)),
                pl.BlockSpec((1, rows, LANES), lambda s, *_: (s, 0, 0)),
            ],
            scratch_shapes=[
                pltpu.VMEM((a, LANES), BF),
                pltpu.VMEM((b, LANES), BF),
                column(a),
                column(a),
                pltpu.VMEM((a, LANES), F32),
                column(b),
                column(b),
                pltpu.VMEM((b, LANES), F32),
            ],
        ),
        out_shape=(
            jax.ShapeDtypeStruct((streams, rows, width), BF),
            jax.ShapeDtypeStruct((streams, rows, LANES), F32),
        ),
        compiler_params=params(),
        name="attend",
    )(low, me, q, kv_all, start)


def three_parts(column):
    high = column.astype(BF)
    rest = column - high.astype(F32)
    middle = rest.astype(BF)
    return high, middle, (rest - middle.astype(F32)).astype(BF)


def put_column(scratch, at, column, rows):
    lane = lane_iota((rows, LANES))
    out = jnp.zeros((rows, LANES), F32)
    for i, piece in enumerate(three_parts(column)):
        out = jnp.where(lane == i, piece.astype(F32), out)
    scratch[at, LANES:] = out.astype(BF)


def backward_kernel(
    low_ref, me_ref, q_ref, kv_ref, start_ref, lse_ref, mixed_ref, grad_ref, cos_ref, sin_ref, dq_ref, dkv_ref,
    qa, qb, ga, gb, ta, tb,
):
    rows = q_ref.shape[1]
    stream = pl.program_id(0)
    me = me_ref[0]
    masked_heads(q_ref, SAME, qa, rows)
    masked_heads(q_ref, OTHER, qb, rows)
    masked_heads(grad_ref, SAME, ga, rows)
    masked_heads(grad_ref, OTHER, gb, rows)
    lane = lane_iota((rows, LANES))
    lse = lse_ref[0]
    for heads, q, g in ((SAME, qa, ga), (OTHER, qb, gb)):
        for slot, h in enumerate(heads):
            at = slice(slot * rows, (slot + 1) * rows)
            cols = slice(h // 2 * LANES, h // 2 * LANES + LANES)
            keep = (lane >= HD) if h % 2 else (lane < HD)
            product = grad_ref[0, :, cols].astype(F32) * mixed_ref[0, :, cols].astype(F32)
            delta = jnp.sum(jnp.where(keep, product, 0.0), axis=-1, keepdims=True)
            put_column(g, at, -delta, rows)
            put_column(q, at, -lse[:, h : h + 1], rows)
    ta[...] = jnp.zeros_like(ta)
    tb[...] = jnp.zeros_like(tb)
    dkv_ref[...] = jnp.zeros_like(dkv_ref)
    keys = GROUP * rows
    ones = (lane_iota((keys, LANES)) < 3).astype(F32).astype(BF)

    def step(j, carry):
        block = kv_ref[pl.ds(j * GROUP, GROUP), 0].reshape(keys, 2 * KW)
        key = block[:, :KW]
        value = block[:, KW:]
        grad_keys = []
        grad_values = []
        for swap, q, g, t in ((False, qa, ga, ta), (True, qb, gb, tb)):
            count = q.shape[0] // rows
            k = jnp.concatenate([key[:, HD:], key[:, :HD]], 1) if swap else key
            v = jnp.concatenate([value[:, HD:], value[:, :HD]], 1) if swap else value
            index = j * keys + lax.broadcasted_iota(jnp.int32, (keys, count * rows), 0)
            place = start_ref[0, 1:2, : count * rows]
            allowed = (index <= place) & (index >= start_ref[0, 0:1, : count * rows])
            s = nt(jnp.concatenate([k, ones], 1), q[...])
            p = jnp.where(allowed, jnp.exp(jnp.where(allowed, s, NEG)), 0.0)
            d = (p * nt(jnp.concatenate([v, ones], 1), g[...])).astype(BF)
            grad_values.append(nn(p.astype(BF), g[:, :LANES]))
            grad_keys.append(nn(d, q[:, :LANES]))
            t[...] += nn(k.T, d)
        other = lambda a: jnp.concatenate([a[:, HD:], a[:, :HD]], 1)
        total = jnp.concatenate([grad_keys[0] + other(grad_keys[1]), grad_values[0] + other(grad_values[1])], 1)
        dkv_ref[pl.ds(j * GROUP, GROUP), 0] = total.astype(BF).reshape(GROUP, rows, 2 * KW)
        return carry

    lax.fori_loop(low_ref[stream], me // GROUP + 1, step, 0)
    parts = {}
    for heads, t in ((SAME, ta), (OTHER, tb)):
        flat = t[...].T
        for slot, h in enumerate(heads):
            parts[h] = flat[slot * rows : (slot + 1) * rows]
    cos = cos_ref[0]
    sin = sin_ref[0]
    for pair in range(HEADS // 2):
        both = jnp.where(lane < HD, parts[2 * pair], parts[2 * pair + 1]) * HD**-0.5
        dq_ref[0, :, pair * LANES : (pair + 1) * LANES] = (both * cos - half_swap(both) * sin).astype(BF)


def attend_back(q, kv_all, start_rows, low, me, lse, mixed, grad, cos, sin):
    streams, rows, width = q.shape
    n = kv_all.shape[0]
    a, b = len(SAME) * rows, len(OTHER) * rows
    tok = lambda w: pl.BlockSpec((1, rows, w), lambda s, *_: (s, 0, 0))
    return pl.pallas_call(
        backward_kernel,
        grid_spec=pltpu.PrefetchScalarGridSpec(
            num_scalar_prefetch=2,
            grid=(streams,),
            in_specs=[
                tok(width),
                pl.BlockSpec((n, 1, rows, 2 * KW), lambda s, *_: (0, s, 0, 0)),
                pl.BlockSpec((1, 2, a), lambda s, *_: (s, 0, 0)),
                tok(LANES),
                tok(width),
                tok(width),
                tok(LANES),
                tok(LANES),
            ],
            out_specs=[tok(width), pl.BlockSpec((n, 1, rows, 2 * KW), lambda s, *_: (0, s, 0, 0))],
            scratch_shapes=[
                pltpu.VMEM((a, 2 * LANES), BF),
                pltpu.VMEM((b, 2 * LANES), BF),
                pltpu.VMEM((a, 2 * LANES), BF),
                pltpu.VMEM((b, 2 * LANES), BF),
                pltpu.VMEM((LANES, a), F32),
                pltpu.VMEM((LANES, b), F32),
            ],
        ),
        out_shape=(
            jax.ShapeDtypeStruct((streams, rows, width), BF),
            jax.ShapeDtypeStruct((n, streams, rows, 2 * KW), BF),
        ),
        compiler_params=params(),
        name="attend_back",
    )(low, me, q, kv_all, start_rows, lse, mixed, grad, cos, sin)


def other_core(a):
    return lax.ppermute(a, "dp", [(0, 1), (1, 0)])


def reduce_over(a, axis, dim):
    size = lax.axis_size(axis)
    me = lax.axis_index(axis)
    if size == 1:
        return lax.squeeze(a, (dim,))
    if size == 2:
        sent = lax.dynamic_index_in_dim(a, 1 - me, dim, keepdims=False)
        kept = lax.dynamic_index_in_dim(a, me, dim, keepdims=False)
        got = lax.ppermute(sent, axis, [(0, 1), (1, 0)])
        return (kept.astype(F32) + got.astype(F32)).astype(BF)
    a = jnp.moveaxis(a, dim, 0)
    shape = a.shape[1:]
    return lax.psum_scatter(a.reshape(size * shape[0], *shape[1:]), axis, scatter_dimension=0, tiled=True).reshape(shape)


def reduce_path(a, order):
    sizes = [lax.axis_size(axis) for axis in SEQ]
    a = a.reshape(*sizes, *a.shape[1:])
    left = list(SEQ)
    for axis in order:
        a = reduce_over(a, axis, left.index(axis))
        left.remove(axis)
    return a


def sum_over_all(a):
    return lax.psum(a, (*SEQ, "dp"))


def layout(lengths, offset, row_count):
    places = offset + jnp.arange(row_count, dtype=jnp.int32)
    slots = jnp.arange(lengths.shape[1])
    ends = jnp.sum(jnp.where(slots[:, None] <= slots[None, :], lengths[:, :, None], 0), axis=1)
    after = (places[None, :, None] >= ends[:, None, :]).astype(jnp.int32)
    begins = jnp.sum(after * lengths[:, None, :], axis=-1, dtype=jnp.int32)
    return (places, begins, places[None, :] < ends[:, -1:])


def shards(inputs, lengths, w_qkv, b_qkv, g_attn, w_out, g_mlp, w_gate_up, w_down, cotangent):
    streams, length, width = inputs.shape
    tokens = streams * length
    n = 1
    for axis in SEQ:
        n *= lax.axis_size(axis)
    me = lax.axis_index(SEQ)
    core = lax.axis_index("dp")
    offset = me * length
    places, begins, valid = layout(lengths, offset, length)
    frequency = rope_base ** (-(jnp.arange(HD // 2, dtype=F32) * (2.0 / HD)))
    lane_frequency = jnp.tile(frequency, LANES // (HD // 2))
    sign = jnp.where(jnp.arange(LANES) % HD < HD // 2, -1.0, 1.0)
    angle = (places[None, :] - begins).astype(F32).reshape(tokens, 1) * lane_frequency
    cos = jnp.cos(angle)
    sin = jnp.sin(angle) * sign

    x = inputs.reshape(tokens, width)
    normed, q, kv = project(x, w_qkv, b_qkv, g_attn, cos, sin)
    kv_all = lax.all_gather(kv.reshape(streams, length, 2 * KW), SEQ, axis=0)

    seed = (cotangent * valid[..., None].astype(BF)).reshape(tokens, width)
    seed_all = jnp.concatenate([seed, other_core(seed)], 0)
    half = FF // 2
    w_gate = lax.dynamic_slice_in_dim(w_gate_up, core * half, half, 1)
    w_up = lax.dynamic_slice_in_dim(w_gate_up, FF + core * half, half, 1)
    w_d = lax.dynamic_slice_in_dim(w_down, core * half, half, 0)

    low = begins[:, 0] // (GROUP * length)
    me_1 = jnp.reshape(me, (1,)).astype(jnp.int32)
    q = q.reshape(streams, length, QW)
    mixed, lse = attend(q, kv_all, begins[:, :, None], low, me_1)
    mixed_flat = mixed.reshape(tokens, QW)
    middle = x.astype(F32) + nn(mixed_flat, w_out)
    inv_mlp = lax.rsqrt(jnp.mean(middle * middle, axis=-1, keepdims=True) + epsilon)
    unit_mlp = middle * inv_mlp
    gain_mlp = g_mlp.astype(F32)
    normed_mlp = (unit_mlp * gain_mlp).astype(BF)
    normed_all = jnp.concatenate([normed_mlp, other_core(normed_mlp)], 0)

    gate = nn(normed_all, w_gate)
    up = nn(normed_all, w_up)
    grad_active = nt(seed_all, w_d)
    sig = jax.nn.sigmoid(gate)
    silu = gate * sig
    active = (silu * up).astype(BF)
    grad_gate = (grad_active * up * (sig * (1.0 + gate * (1.0 - sig)))).astype(BF)
    grad_up = (grad_active * silu).astype(BF)
    term_down = tn(active, seed_all).astype(BF)
    term_gate = tn(normed_all, grad_gate).astype(BF)
    term_up = tn(normed_all, grad_up).astype(BF)
    out_part = nn(active, w_d)
    back_part = nt(grad_gate, w_gate) + nt(grad_up, w_up)
    output = (middle + out_part[:tokens] + other_core(out_part[tokens:])).astype(BF)

    z, y, xx = SEQ
    rows_gate = reduce_path(term_gate.reshape(n, width // n, half), (xx, y, z))
    rows_up = reduce_path(term_up.reshape(n, width // n, half), (y, xx, z))
    rows_down = reduce_path(term_down.reshape(n, half // n, width), (z, xx, y))

    grad_normed_mlp = back_part[:tokens] + other_core(back_part[tokens:])
    scaled = grad_normed_mlp * gain_mlp
    grad_middle = seed.astype(F32) + inv_mlp * (
        scaled - unit_mlp * jnp.mean(scaled * unit_mlp, axis=-1, keepdims=True)
    )
    gain_mlp_part = jnp.sum(grad_normed_mlp * unit_mlp, axis=0)
    grad_branch = grad_middle.astype(BF)
    grad_mixed = nt(grad_branch, w_out).astype(BF).reshape(streams, length, QW)

    start_rows = jnp.stack(
        [jnp.tile(begins, (1, len(SAME))), jnp.tile(jnp.broadcast_to(places[None], begins.shape), (1, len(SAME)))], 1
    )
    grad_q, grad_kv = attend_back(
        q, kv_all, start_rows, low, me_1, lse, mixed, grad_mixed,
        cos.reshape(streams, length, LANES), sin.reshape(streams, length, LANES),
    )
    grad_kv = grad_kv.reshape(n, tokens, 2 * KW)
    grad_k = reduce_path(grad_kv[..., :KW], (xx, y, z)).astype(F32)
    grad_v = reduce_path(grad_kv[..., KW:], (y, xx, z))
    quarter = HD // 2
    turned = jnp.concatenate(
        [grad_k[:, quarter:HD], grad_k[:, :quarter], grad_k[:, HD + quarter :], grad_k[:, HD : HD + quarter]], 1
    )
    grad_k = (grad_k * cos - turned * sin).astype(BF)
    grad_projected = jnp.concatenate([grad_q.reshape(tokens, QW), grad_k, grad_v], 1)
    grad_normed = nt(grad_projected, w_qkv)
    residual = x.astype(F32)
    inv_attn = lax.rsqrt(jnp.mean(residual * residual, axis=-1, keepdims=True) + epsilon)
    unit_attn = residual * inv_attn
    scaled = grad_normed * g_attn.astype(F32)
    grad_input = grad_middle + inv_attn * (
        scaled - unit_attn * jnp.mean(scaled * unit_attn, axis=-1, keepdims=True)
    )
    gain_attn_part = jnp.sum(grad_normed * unit_attn, axis=0)
    bias_part = jnp.sum(grad_projected.astype(F32), axis=0)

    terms = jnp.concatenate([tn(normed, grad_projected).astype(BF), tn(mixed_flat, grad_branch).astype(BF)], 1)
    joined = terms.shape[1]
    cut = joined // 2
    sent = lax.dynamic_slice_in_dim(terms, (1 - core) * cut, cut, 1)
    kept = lax.dynamic_slice_in_dim(terms, core * cut, cut, 1)
    terms = (kept.astype(F32) + other_core(sent).astype(F32)).astype(BF)
    rows_attn = reduce_path(terms.reshape(n, width // n, cut), (xx, y, z))

    def both_cores(mine, dim):
        theirs = other_core(mine)
        first = jnp.where(core == 0, mine, theirs)
        second = jnp.where(core == 0, theirs, mine)
        return jnp.concatenate([first, second], dim).astype(F32)

    rows_down = lax.ppermute(
        rows_down, (*SEQ, "dp"), [(s * 2 + d, d * n + s) for s in range(n) for d in range(2)]
    )
    rows_attn = both_cores(rows_attn, 1)
    bias_grad, gain_attn_grad, gain_mlp_grad = sum_over_all((bias_part, gain_attn_part, gain_mlp_part))
    joined_width = QW + 2 * KW
    return (
        output.reshape(streams, length, width),
        grad_input.reshape(streams, length, width),
        rows_attn[:, :joined_width],
        bias_grad,
        gain_attn_grad,
        rows_attn[:, joined_width:],
        gain_mlp_grad,
        jnp.concatenate([both_cores(rows_gate, 1), both_cores(rows_up, 1)], 1),
        both_cores(rows_down, 0),
    )


def solution(mesh):
    n = mesh.shape["seq"]
    sizes = {16: (4, 2, 2), 64: (4, 4, 4)}.get(n, (n, 1, 1))
    fine = Mesh(np.asarray(mesh.devices).reshape(*sizes, mesh.shape["dp"]), (*SEQ, "dp"))
    in_specs = (P("dp", SEQ, None), P("dp", None), P(), P(), P(), P(), P(), P(), P(), P("dp", SEQ, None))
    out_specs = (
        P("dp", SEQ, None), P("dp", SEQ, None), P(SEQ, None), P(), P(), P(SEQ, None), P(), P(SEQ, None), P(SEQ, None),
    )
    return jax.shard_map(shards, mesh=fine, in_specs=in_specs, out_specs=out_specs, check_vma=False)
```

```python
import functools

import jax
import jax.numpy as jnp
import numpy as np
from jax import lax
from jax.experimental import pallas as pl
from jax.experimental.pallas import tpu as pltpu
from jax.sharding import Mesh
from jax.sharding import PartitionSpec as P

HEADS = 14
KVH = 2
HD = 64
FF = 4864
QW = HEADS * HD
KW = KVH * HD
LANES = 128
GROUP = 8
CHUNK = 256
NEG = -1e30
epsilon = 1e-06
rope_base = 1000000.0
BF = jnp.bfloat16
F32 = jnp.float32
SEQ = ("az", "ay", "ax")

SAME = [h for h in range(HEADS) if h % 2 == h // (HEADS // KVH)]
OTHER = [h for h in range(HEADS) if h % 2 != h // (HEADS // KVH)]


def nt(a, b):
    return lax.dot_general(a, b, (((1,), (1,)), ((), ())), preferred_element_type=F32)


def tn(a, b):
    return lax.dot_general(a, b, (((0,), (0,)), ((), ())), preferred_element_type=F32)


def nn(a, b):
    return lax.dot_general(a, b, (((1,), (0,)), ((), ())), preferred_element_type=F32)


def lane_iota(shape):
    return lax.broadcasted_iota(jnp.int32, shape, len(shape) - 1)


def half_swap(tile):
    low = lane_iota(tile.shape) % HD < HD // 2
    return jnp.where(low, pltpu.roll(tile, LANES - HD // 2, 1), pltpu.roll(tile, HD // 2, 1))


def cost(us):
    return pl.CostEstimate(flops=int(us * 1e6 * 90), bytes_accessed=1 << 16, transcendentals=0)


def params(limit=56):
    return pltpu.CompilerParams(vmem_limit_bytes=limit << 20)


def turn(part, cos, sin):
    return part * cos + half_swap(part) * sin


def project_kv_kernel(x_ref, w_ref, b_ref, g_ref, cos_ref, sin_ref, normed_ref, k_ref, v_ref):
    step = pl.program_id(0)

    @pl.when(step == 0)
    def _():
        x = x_ref[...].astype(F32)
        inv = lax.rsqrt(jnp.mean(x * x, axis=-1, keepdims=True) + epsilon)
        normed_ref[...] = (x * inv * g_ref[...].astype(F32)).astype(BF)

    part = nn(normed_ref[...], w_ref[...]) + b_ref[...].astype(F32)

    @pl.when(step == 0)
    def _():
        k_ref[...] = turn(part, cos_ref[...], sin_ref[...]).astype(BF)

    @pl.when(step == 1)
    def _():
        v_ref[...] = part.astype(BF)


def project_kv(x, w, b, g, cos, sin):
    tokens, width = x.shape
    fixed = lambda *shape: pl.BlockSpec(shape, lambda i: (0, 0))
    return pl.pallas_call(
        project_kv_kernel,
        grid=(2,),
        in_specs=[
            fixed(tokens, width),
            pl.BlockSpec((width, KW), lambda i: (0, QW // KW + i)),
            pl.BlockSpec((1, KW), lambda i: (0, QW // KW + i)),
            fixed(1, width),
            fixed(tokens, LANES),
            fixed(tokens, LANES),
        ],
        out_specs=[fixed(tokens, width), fixed(tokens, KW), fixed(tokens, KW)],
        out_shape=(
            jax.ShapeDtypeStruct((tokens, width), BF),
            jax.ShapeDtypeStruct((tokens, KW), BF),
            jax.ShapeDtypeStruct((tokens, KW), BF),
        ),
        compiler_params=params(),
        cost_estimate=cost(3),
        name="project_kv",
    )(x, w, b, g, cos, sin)


def project_q_kernel(normed_ref, w_ref, b_ref, cos_ref, sin_ref, q_ref):
    normed = normed_ref[...]
    cos = cos_ref[...]
    sin = sin_ref[...]
    for first in range(0, QW, 2 * LANES):
        cols = slice(first, min(first + 2 * LANES, QW))
        both = nn(normed, w_ref[:, cols]) + b_ref[:, cols].astype(F32)
        for at in range(0, both.shape[1], LANES):
            part = turn(both[:, at : at + LANES], cos, sin) * HD**-0.5
            q_ref[:, first + at : first + at + LANES] = part.astype(BF)


def project_q(normed, w, b, cos, sin):
    tokens, width = normed.shape
    return pl.pallas_call(
        project_q_kernel,
        out_shape=jax.ShapeDtypeStruct((tokens, QW), BF),
        compiler_params=params(),
        cost_estimate=cost(4),
        name="project_q",
    )(normed, w, b, cos, sin)


def masked_heads(ref, heads, scratch, rows):
    lane = lane_iota((rows, LANES))
    for slot, h in enumerate(heads):
        pair = ref[0, :, h // 2 * LANES : h // 2 * LANES + LANES]
        keep = (lane >= HD) if h % 2 else (lane < HD)
        scratch[slot * rows : (slot + 1) * rows, :LANES] = jnp.where(keep, pair, jnp.zeros_like(pair))


def swapped(a):
    return jnp.concatenate([a[:, HD:], a[:, :HD]], 1)


def chunks(width):
    return [slice(at, min(at + CHUNK, width)) for at in range(0, width, CHUNK)]


def allowed_pairs(start_ref, first, keys, cols):
    index = first + lax.broadcasted_iota(jnp.int32, (keys, cols.stop - cols.start), 0)
    return (index <= start_ref[0, 1:2, cols]) & (index >= start_ref[0, 0:1, cols])


def gathered(ref, spot_ref, which, j):
    return jnp.concatenate([ref[spot_ref[which, j * GROUP + i], 0] for i in range(GROUP)], 0)


def forward_kernel(low_ref, me_ref, spot_ref, q_ref, k_ref, v_ref, start_ref, out_ref, lse_ref, qa, qb, ma, la, oa, mb, lb, ob, weights):
    rows = q_ref.shape[1]
    stream = pl.program_id(0)
    me = me_ref[0]
    masked_heads(q_ref, SAME, qa, rows)
    masked_heads(q_ref, OTHER, qb, rows)
    for m, l, o in ((ma, la, oa), (mb, lb, ob)):
        m[...] = jnp.full_like(m, NEG)
        l[...] = jnp.zeros_like(l)
        o[...] = jnp.zeros_like(o)
    keys = GROUP * rows

    def step(j, carry):
        key = gathered(k_ref, spot_ref, 0, j)
        value = gathered(v_ref, spot_ref, 1, j)
        for swap, q, m, l, o in ((False, qa, ma, la, oa), (True, qb, mb, lb, ob)):
            width = q.shape[0]
            k = swapped(key) if swap else key
            v = swapped(value) if swap else value
            for cols in chunks(width):
                s = jnp.where(allowed_pairs(start_ref, j * keys, keys, cols), nt(k, q[cols]), NEG)
                before = m[:, cols]
                top = jnp.maximum(before, jnp.max(s, axis=0, keepdims=True))
                p = jnp.exp(s - top)
                shrink = jnp.exp(before - top)
                m[:, cols] = top
                l[:, cols] = l[:, cols] * shrink + jnp.sum(p, axis=0, keepdims=True)
                o[:, cols] = o[:, cols] * shrink
                weights[:, cols] = p.astype(BF)
            o[...] += nn(v.T, weights[:, :width])
        return carry

    lax.fori_loop(low_ref[stream], me // GROUP + 1, step, 0)
    lane = lane_iota((rows, LANES))
    parts = {}
    for row, (heads, m, l, o) in enumerate(((SAME, ma, la, oa), (OTHER, mb, lb, ob))):
        total = l[...]
        flat = (o[...] / total).T
        lse_ref[0, row : row + 1, : total.shape[1]] = m[...] + jnp.log(total)
        for slot, h in enumerate(heads):
            parts[h] = flat[slot * rows : (slot + 1) * rows]
    for pair in range(HEADS // 2):
        both = jnp.where(lane < HD, parts[2 * pair], parts[2 * pair + 1])
        out_ref[0, :, pair * LANES : (pair + 1) * LANES] = both.astype(BF)


def attend(q, k_all, v_all, start_rows, low, me, spots):
    streams, rows, width = q.shape
    n = k_all.shape[0]
    a, b = len(SAME) * rows, len(OTHER) * rows
    tok = lambda w: pl.BlockSpec((1, rows, w), lambda s, *_: (s, 0, 0))
    two = pl.BlockSpec((1, 2, a), lambda s, *_: (s, 0, 0))
    return pl.pallas_call(
        forward_kernel,
        grid_spec=pltpu.PrefetchScalarGridSpec(
            num_scalar_prefetch=3,
            grid=(streams,),
            in_specs=[tok(width), *[pl.BlockSpec((n, 1, rows, KW), lambda s, *_: (0, s, 0, 0))] * 2, two],
            out_specs=[tok(width), two],
            scratch_shapes=[
                pltpu.VMEM((a, LANES), BF),
                pltpu.VMEM((b, LANES), BF),
                pltpu.VMEM((1, a), F32),
                pltpu.VMEM((1, a), F32),
                pltpu.VMEM((LANES, a), F32),
                pltpu.VMEM((1, b), F32),
                pltpu.VMEM((1, b), F32),
                pltpu.VMEM((LANES, b), F32),
                pltpu.VMEM((GROUP * rows, a), BF),
            ],
        ),
        out_shape=(
            jax.ShapeDtypeStruct((streams, rows, width), BF),
            jax.ShapeDtypeStruct((streams, 2, a), F32),
        ),
        compiler_params=params(),
        cost_estimate=cost(18),
        name="attend",
    )(low, me, spots, q, k_all, v_all, start_rows)


def three_parts(column):
    high = column.astype(BF)
    rest = column - high.astype(F32)
    middle = rest.astype(BF)
    return high, middle, (rest - middle.astype(F32)).astype(BF)


def put_column(scratch, at, column, rows):
    lane = lane_iota((rows, LANES))
    out = jnp.zeros((rows, LANES), F32)
    for i, piece in enumerate(three_parts(column)):
        out = jnp.where(lane == i, piece.astype(F32), out)
    scratch[at, LANES:] = out.astype(BF)


def backward_kernel(
    first, low_ref, me_ref, spot_ref, q_ref, k_ref, v_ref, start_ref, lse_ref, mixed_ref, grad_ref, cos_ref, sin_ref, dq_ref, dkk_ref,
    dks_ref, dvk_ref, dvs_ref, qa, qb, ga, gb, ta, tb, dk_all, dv_all, weights, grads,
):
    rows = q_ref.shape[1]
    stream = first + pl.program_id(0)
    me = me_ref[0]
    masked_heads(q_ref, SAME, qa, rows)
    masked_heads(q_ref, OTHER, qb, rows)
    masked_heads(grad_ref, SAME, ga, rows)
    masked_heads(grad_ref, OTHER, gb, rows)
    lane = lane_iota((rows, LANES))
    for heads, g in ((SAME, ga), (OTHER, gb)):
        for slot, h in enumerate(heads):
            at = slice(slot * rows, (slot + 1) * rows)
            cols = slice(h // 2 * LANES, h // 2 * LANES + LANES)
            keep = (lane >= HD) if h % 2 else (lane < HD)
            product = grad_ref[0, :, cols].astype(F32) * mixed_ref[0, :, cols].astype(F32)
            delta = jnp.sum(jnp.where(keep, product, 0.0), axis=-1, keepdims=True)
            put_column(g, at, -delta, rows)
    ta[...] = jnp.zeros_like(ta)
    tb[...] = jnp.zeros_like(tb)
    dk_all[...] = jnp.zeros_like(dk_all)
    dv_all[...] = jnp.zeros_like(dv_all)
    keys = GROUP * rows
    ones = (lane_iota((keys, LANES)) < 3).astype(F32).astype(BF)

    def step(j, carry):
        key = gathered(k_ref, spot_ref, 0, j)
        value = gathered(v_ref, spot_ref, 1, j)
        grad_keys = []
        grad_values = []
        for row, (q, g, t) in enumerate(((qa, ga, ta), (qb, gb, tb))):
            width = q.shape[0]
            k = swapped(key) if row else key
            v = jnp.concatenate([swapped(value) if row else value, ones], 1)
            for cols in chunks(width):
                s = nt(k, q[cols]) - lse_ref[0, row : row + 1, cols]
                p = jnp.exp(jnp.where(allowed_pairs(start_ref, j * keys, keys, cols), s, NEG))
                weights[:, cols] = p.astype(BF)
                grads[:, cols] = (p * nt(v, g[cols])).astype(BF)
            grad_values.append(nn(weights[:, :width], g[:, :LANES]))
            grad_keys.append(nn(grads[:, :width], q[...]))
            t[...] += nn(k.T, grads[:, :width])
        for out_ref, (same, other) in ((dk_all, grad_keys), (dv_all, grad_values)):
            total = (same + swapped(other)).astype(BF)
            out_ref[pl.ds(j * GROUP, GROUP)] = total.reshape(GROUP, rows, KW)
        return carry

    lax.fori_loop(low_ref[stream], me // GROUP + 1, step, 0)
    half = dkk_ref.shape[0]
    for which, (keep_ref, send_ref, out_ref) in enumerate(((dkk_ref, dks_ref, dk_all), (dvk_ref, dvs_ref, dv_all))):
        for spot in range(half):
            keep_ref[spot, 0] = out_ref[spot_ref[2 + which, spot]]
            send_ref[spot, 0] = out_ref[spot_ref[2 + which, half + spot]]
    parts = {}
    for heads, t in ((SAME, ta), (OTHER, tb)):
        flat = t[...].T
        for slot, h in enumerate(heads):
            parts[h] = flat[slot * rows : (slot + 1) * rows]
    cos = cos_ref[0]
    sin = sin_ref[0]
    for pair in range(HEADS // 2):
        both = jnp.where(lane < HD, parts[2 * pair], parts[2 * pair + 1]) * HD**-0.5
        dq_ref[0, :, pair * LANES : (pair + 1) * LANES] = (both * cos - half_swap(both) * sin).astype(BF)


def attend_back(first, streams, q, k_all, v_all, start_rows, low, me, spots, lse, mixed, grad, cos, sin):
    rows, width = q.shape[1:]
    n = k_all.shape[0]
    a, b = len(SAME) * rows, len(OTHER) * rows
    tok = lambda w: pl.BlockSpec((1, rows, w), lambda s, *_: (s + first, 0, 0))
    two = pl.BlockSpec((1, 2, a), lambda s, *_: (s + first, 0, 0))
    key_spec = pl.BlockSpec((n // 2, 1, rows, KW), lambda s, *_: (0, s, 0, 0))
    return pl.pallas_call(
        functools.partial(backward_kernel, first),
        grid_spec=pltpu.PrefetchScalarGridSpec(
            num_scalar_prefetch=3,
            grid=(streams,),
            in_specs=[
                tok(width),
                *[pl.BlockSpec((n, 1, rows, KW), lambda s, *_: (0, s + first, 0, 0))] * 2,
                two,
                two,
                tok(width),
                tok(width),
                tok(LANES),
                tok(LANES),
            ],
            out_specs=[pl.BlockSpec((1, rows, width), lambda s, *_: (s, 0, 0)), *[key_spec] * 4],
            scratch_shapes=[
                pltpu.VMEM((a, LANES), BF),
                pltpu.VMEM((b, LANES), BF),
                pltpu.VMEM((a, 2 * LANES), BF),
                pltpu.VMEM((b, 2 * LANES), BF),
                pltpu.VMEM((LANES, a), F32),
                pltpu.VMEM((LANES, b), F32),
                *[pltpu.VMEM((n, rows, KW), BF)] * 2,
                *[pltpu.VMEM((GROUP * rows, a), BF)] * 2,
            ],
        ),
        out_shape=(
            jax.ShapeDtypeStruct((streams, rows, width), BF),
            *[jax.ShapeDtypeStruct((n // 2, streams, rows, KW), BF)] * 4,
        ),
        compiler_params=params(),
        cost_estimate=cost(8 * streams),
        name="attend_back",
    )(low, me, spots, q, k_all, v_all, start_rows, lse, mixed, grad, cos, sin)


TILE = 256


def mlp_kernel(
    valid, mine_ref, theirs_ref, sm_ref, st_ref, og_ref, ou_ref, wg_ref, wu_ref, wd_ref, om_ref, ot_ref, bm_ref, bt_ref,
    td_ref, gk_ref, gs_ref, uk_ref, us_ref, n_ref, s_ref, ng_ref, nu_ref,
):
    rows = mine_ref.shape[0]
    step = pl.program_id(0)
    sums = (om_ref, ot_ref, bm_ref, bt_ref)

    @pl.when(step == 0)
    def _():
        n_ref[:rows] = mine_ref[...]
        n_ref[rows:] = theirs_ref[...]
        s_ref[:rows] = sm_ref[...]
        s_ref[rows:] = st_ref[...]
        ng_ref[...] = nt(og_ref[...], n_ref[...]).astype(BF)
        nu_ref[...] = nt(ou_ref[...], n_ref[...]).astype(BF)
        for ref in sums:
            ref[...] = jnp.zeros_like(ref)

    normed = n_ref[...]
    seed = s_ref[...]
    left = valid - step * TILE
    inside = lambda w, dim: jnp.where(lax.broadcasted_iota(jnp.int32, w.shape, dim) < left, w, jnp.zeros_like(w))
    wg, wu, wd = inside(wg_ref[...], 1), inside(wu_ref[...], 1), inside(wd_ref[...], 0)
    gate = nn(normed, wg)
    up = nn(normed, wu)
    grad = nt(seed, wd)
    sig = 1.0 / (1.0 + jnp.exp(-gate))
    silu = gate * sig
    active = (silu * up).astype(BF)
    grad_up = (grad * silu).astype(BF)
    grad_gate = (grad * up * (sig * (1.0 + gate * (1.0 - sig)))).astype(BF)
    td_ref[...] = tn(active, seed).astype(BF)
    half = gk_ref.shape[0]
    for turned, grad_pre, keep, send in ((ng_ref, grad_gate, gk_ref, gs_ref), (nu_ref, grad_up, uk_ref, us_ref)):
        term = nn(turned[...], grad_pre).astype(BF)
        keep[...] = term[:half]
        send[...] = term[half:]
    out = nn(active, wd)
    back = nt(grad_gate, wg) + nt(grad_up, wu)
    for ref, part in zip(sums, (out[:rows], out[rows:], back[:rows], back[rows:])):
        ref[...] += part


def fixed(*shape):
    return pl.BlockSpec(shape, lambda *_: (0,) * len(shape))


def shaped(dtype, *dims):
    return jax.ShapeDtypeStruct(dims, dtype)


def mlp(mine, theirs, seed_mine, seed_theirs, order_gate, order_up, w_gate, w_up, w_d):
    rows, width = mine.shape
    half = w_gate.shape[1]
    cols = lambda size: pl.BlockSpec((size, TILE), lambda i: (0, i))
    down = pl.BlockSpec((TILE, width), lambda i: (i, 0))
    part = fixed(rows, width)
    return pl.pallas_call(
        functools.partial(mlp_kernel, half),
        grid=(pl.cdiv(half, TILE),),
        in_specs=[part] * 4 + [fixed(width, width)] * 2 + [cols(width)] * 2 + [down],
        out_specs=[part] * 4 + [down] + [cols(width // 2)] * 4,
        out_shape=[shaped(F32, rows, width)] * 4 + [shaped(BF, half, width)] + [shaped(BF, width // 2, half)] * 4,
        scratch_shapes=[pltpu.VMEM((2 * rows, width), BF)] * 2 + [pltpu.VMEM((width, 2 * rows), BF)] * 2,
        compiler_params=params(),
        cost_estimate=cost(40),
        name="mlp",
    )(mine, theirs, seed_mine, seed_theirs, order_gate, order_up, w_gate, w_up, w_d)


def middle_kernel(bm_ref, bt_ref, middle_ref, seed_ref, g_ref, w_ref, gm_ref, gb_ref, gx_ref, gain_ref):
    @pl.when(pl.program_id(0) == 0)
    def _():
        gain_ref[...] = jnp.zeros_like(gain_ref)

    grad = bm_ref[...] + bt_ref[...]
    middle = middle_ref[...]
    inv = lax.rsqrt(jnp.mean(middle * middle, axis=-1, keepdims=True) + epsilon)
    unit = middle * inv
    scaled = grad * g_ref[...].astype(F32)
    grad_middle = seed_ref[...].astype(F32) + inv * (scaled - unit * jnp.mean(scaled * unit, axis=-1, keepdims=True))
    gm_ref[...] = grad_middle
    branch = grad_middle.astype(BF)
    gb_ref[...] = branch
    gx_ref[...] = nt(branch, w_ref[...]).astype(BF)
    gain_ref[...] += jnp.sum(grad * unit, axis=0, keepdims=True)


def middle_back(mine, theirs, middle, seed, gain, w_out):
    tokens, width = middle.shape
    rows = tokens // 4
    part = pl.BlockSpec((rows, width), lambda i: (i, 0))
    return pl.pallas_call(
        middle_kernel,
        grid=(4,),
        in_specs=[part] * 4 + [fixed(1, width), fixed(width, width)],
        out_specs=[part] * 3 + [fixed(1, width)],
        out_shape=[shaped(F32, tokens, width), shaped(BF, tokens, width), shaped(BF, tokens, width), shaped(F32, 1, width)],
        compiler_params=params(),
        cost_estimate=cost(5),
        name="middle_back",
    )(mine, theirs, middle, seed, gain, w_out)


def attention_terms_kernel(core_ref, normed_ref, mixed_ref, gq_ref, gb_ref, order_ref, sent_ref, kept_ref):
    first = core_ref[0] == 0
    order = order_ref[...]
    pick = lambda flag, a, b: jnp.where(jnp.broadcast_to(flag, a.shape), a[...], b[...])
    for out_ref, flag in ((sent_ref, first), (kept_ref, jnp.logical_not(first))):
        left = nt(order, pick(flag, normed_ref, mixed_ref)).astype(BF)
        out_ref[...] = nn(left, pick(flag, gq_ref, gb_ref)).astype(BF)


def attention_terms(core, normed, mixed, grad_q, grad_branch, order):
    width = normed.shape[1]
    whole = pl.BlockSpec(memory_space=pltpu.VMEM)
    return pl.pallas_call(
        attention_terms_kernel,
        in_specs=[pl.BlockSpec(memory_space=pltpu.SMEM)] + [whole] * 5,
        out_specs=[whole] * 2,
        out_shape=[shaped(BF, width, width)] * 2,
        compiler_params=params(),
        cost_estimate=cost(5),
        name="attention_terms",
    )(core, normed, mixed, grad_q, grad_branch, order)


def last_kernel(gkv_ref, gq_ref, w_ref, x_ref, g_ref, cos_ref, sin_ref, nt_ref, gm_ref, gain_ref, gi_ref, term_ref,
                sums_ref):
    grads = gkv_ref[...]
    keys = grads[:, :KW].astype(F32)
    keys = (keys * cos_ref[...] - half_swap(keys) * sin_ref[...]).astype(BF)
    grad_kv = jnp.concatenate([keys, grads[:, KW:]], 1)
    term_ref[...] = nn(nt_ref[...], grad_kv).astype(BF)
    grad = nt(gq_ref[...], w_ref[:, :QW]) + nt(grad_kv, w_ref[:, QW:])
    x = x_ref[...].astype(F32)
    inv = lax.rsqrt(jnp.mean(x * x, axis=-1, keepdims=True) + epsilon)
    unit = x * inv
    scaled = grad * g_ref[...].astype(F32)
    gi_ref[...] = gm_ref[...] + inv * (scaled - unit * jnp.mean(scaled * unit, axis=-1, keepdims=True))
    over = lambda a: jnp.sum(a.astype(F32), axis=0, keepdims=True)
    at = 0
    for row in (over(gq_ref[...]), over(grad_kv), over(grad * unit), gain_ref[...]):
        sums_ref[:, at : at + row.shape[1]] = row
        at += row.shape[1]


def last_back(grads, grad_q, w_qkv, x, gain, cos, sin, normed_t, grad_middle, gain_mlp_part):
    tokens, width = x.shape
    return pl.pallas_call(
        last_kernel,
        out_shape=[
            shaped(F32, tokens, width),
            shaped(BF, width, 2 * KW),
            shaped(F32, 1, QW + 2 * KW + 2 * width),
        ],
        compiler_params=params(),
        cost_estimate=cost(6),
        name="last_back",
    )(grads, grad_q, w_qkv, x, gain, cos, sin, normed_t, grad_middle, gain_mlp_part)


def after(a, *others):
    return lax.optimization_barrier((a, others))[0]


class Order:
    def __init__(self, token):
        self.token = token

    def enter(self, inputs):
        return lax.optimization_barrier((inputs, self.token))[0]

    def __call__(self, step, *inputs):
        self.token = step(*self.enter(inputs))
        return self.token


def other_core(a):
    return lax.ppermute(a, "dp", [(0, 1), (1, 0)])


def pair_up(a, axis, step):
    return lax.ppermute(a, axis, [(i, i ^ step) for i in range(lax.axis_size(axis))])


def total(terms):
    return functools.reduce(lambda a, b: a + b, [a.astype(F32) for a in terms]).astype(BF)


def add(a, b):
    return total((a, b))


Z, Y, X = SEQ
X_FIRST = ((X, 1), (Y, 1), (Z, 1), (Z, 2))
Y_FIRST = ((Y, 1), (X, 1), (Z, 1), (Z, 2))
Z_FIRST = ((Z, 1), (Z, 2), (X, 1), (Y, 1))
KEY_GATHER = ((Y, 1), (X, 1), (Z, 2), (Z, 1))
VALUE_GATHER = X_FIRST


def halving():
    return [lax.axis_size(axis) for axis in SEQ] == [4, 2, 2]


def my_bit(axis, step):
    return (lax.axis_index(axis) // step) % 2


def device_at(order, spot, relative):
    place = 0
    weight = {(X, 1): 1, (Y, 1): 2, (Z, 1): 4, (Z, 2): 8}
    for i, (axis, step) in enumerate(order):
        bit = (spot >> (len(order) - 1 - i)) & 1
        if relative:
            bit = bit ^ my_bit(axis, step)
        place = place + bit * weight[axis, step]
    return place


def spots_of_devices(order):
    n = lax.axis_size(SEQ)
    if not halving():
        return jnp.arange(n)
    spots = jnp.arange(n)
    return jnp.sum(jnp.where(device_at(order, spots, True)[:, None] == spots[None, :], spots[:, None], 0), 0)


def devices_at_spots(order):
    n = lax.axis_size(SEQ)
    return device_at(order, jnp.arange(n), True) if halving() else jnp.arange(n)


def row_order(order, width):
    n = lax.axis_size(SEQ)
    row = jnp.arange(width)
    source = row
    if halving():
        source = device_at(order, row // (width // n), True) * (width // n) + row % (width // n)
    return (source[:, None] == jnp.arange(width)[None, :]).astype(BF)


class Halving:
    def __init__(self, steps, arrays, rows, order=None, send=None):
        self.steps = list(steps)
        self.arrays = list(arrays)
        self.firsts = [0] * len(self.arrays)
        self.rows = rows
        if send is None:
            self.go(order)
        else:
            self.move(send)

    def halves(self):
        return 0, self.rows

    def move(self, send):
        self.arrays.append(pair_up(send, *self.steps.pop(0)))
        self.firsts.append(0)

    def sum(self, offset):
        cut = lambda a, first: lax.dynamic_slice_in_dim(a, first + offset, self.rows, 0)
        return total([cut(a, first) for a, first in zip(self.arrays, self.firsts)])

    def go(self, order):
        self.arrays = list(order.enter(self.arrays))
        if not self.steps:
            order.token = self.sum(0)
            return order.token
        self.rows //= 2
        kept, sent = self.halves()
        send = order.token = self.sum(sent)
        self.firsts = [first + kept for first in self.firsts]
        self.move(send)


class PlacedHalving(Halving):
    def halves(self):
        bit = my_bit(*self.steps[0])
        return bit * self.rows, (1 - bit) * self.rows


class PairHalving:
    def __init__(self, a_keep, a_send, b_keep, b_send, orders=(X_FIRST, Y_FIRST)):
        rows = a_keep.shape[0]
        self.pair = [
            Halving(orders[0][:2], [a_keep], rows, send=a_send),
            Halving(orders[1][:2], [b_keep], rows, send=b_send),
        ]
        self.last = orders[0][2:]
        self.count = 0

    def go(self, order, which=None):
        if which is not None:
            return self.pair[which].go(order)
        self.count += 1
        a, b = self.pair
        if self.count == 1:
            a.arrays, b.arrays = order.enter((list(a.arrays), list(b.arrays)))
            both = order.token = jnp.concatenate([a.sum(0), b.sum(0)], 1)
            half = both.shape[0] // 2
            self.rest = Halving(self.last, [both], half, send=both[half:])
        else:
            return self.rest.go(order)


def reduce_rows(a):
    return lax.psum_scatter(a, SEQ, scatter_dimension=0, tiled=True)


class Doubling:
    def __init__(self, order, a):
        self.steps = list(reversed(order))
        self.all = a[None]
        self.got = pair_up(self.all, *self.steps.pop(0))

    def go(self, order):
        self.all = order(lambda a, b: jnp.concatenate([a, b], 0), self.all, self.got)
        if self.steps:
            self.got = pair_up(self.all, *self.steps.pop(0))
        return self.all


def to_owner(a, order):
    n = lax.axis_size(SEQ)
    holder = [device_at(order, spot, False) for spot in range(n)] if halving() else list(range(n))
    pairs = [(holder[spot] * 2 + core, core * n + spot) for spot in range(n) for core in range(2)]
    return lax.ppermute(a, (*SEQ, "dp"), pairs)


def sum_over_all(a):
    for axis in ("dp", *SEQ[::-1]):
        size = lax.axis_size(axis)
        step = 1
        while step < size:
            a = a + lax.ppermute(a, axis, [(i, i ^ step) for i in range(size)])
            step *= 2
    return a


def layout(lengths, offset, row_count):
    places = offset + jnp.arange(row_count, dtype=jnp.int32)
    slots = jnp.arange(lengths.shape[1])
    ends = jnp.sum(jnp.where(slots[:, None] <= slots[None, :], lengths[:, :, None], 0), axis=1)
    after = (places[None, :, None] >= ends[:, None, :]).astype(jnp.int32)
    begins = jnp.sum(after * lengths[:, None, :], axis=-1, dtype=jnp.int32)
    return (places, begins, places[None, :] < ends[:, -1:])


def shards(inputs, lengths, w_qkv, b_qkv, g_attn, w_out, g_mlp, w_gate_up, w_down, cotangent):
    streams, length, width = inputs.shape
    tokens = streams * length
    n = 1
    for axis in SEQ:
        n *= lax.axis_size(axis)
    me = lax.axis_index(SEQ)
    core = lax.axis_index("dp")
    offset = me * length
    places, begins, valid = layout(lengths, offset, length)
    frequency = rope_base ** (-(jnp.arange(HD // 2, dtype=F32) * (2.0 / HD)))
    lane_frequency = jnp.tile(frequency, LANES // (HD // 2))
    sign = jnp.where(jnp.arange(LANES) % HD < HD // 2, -1.0, 1.0)
    angle = (places[None, :] - begins).astype(F32).reshape(tokens, 1) * lane_frequency
    cos = jnp.cos(angle)
    sin = jnp.sin(angle) * sign

    x = inputs.reshape(tokens, width)
    bias = b_qkv.reshape(1, -1)
    normed, k, v = project_kv(x, w_qkv, bias, g_attn.reshape(1, -1), cos, sin)
    k, v = k.reshape(streams, length, KW), v.reshape(streams, length, KW)
    half = FF // 2

    def small_inputs(begins):
        start_rows = jnp.stack(
            [
                jnp.tile(begins, (1, len(SAME))),
                jnp.tile(jnp.broadcast_to(places[None], begins.shape), (1, len(SAME))),
            ],
            1,
        )
        spots = jnp.stack(
            [*map(spots_of_devices, (KEY_GATHER, VALUE_GATHER)), *map(devices_at_spots, (Y_FIRST, X_FIRST))]
        ).astype(jnp.int32)
        return start_rows, spots, row_order(X_FIRST, width), row_order(Y_FIRST, width)

    cut_cols = lambda w, first: lax.dynamic_slice_in_dim(w, first + core * half, half, 1)
    cut_rows = lambda w: lax.dynamic_slice_in_dim(w, core * half, half, 0)
    fast = halving()
    order = Order(k)
    if fast:
        keys = Doubling(KEY_GATHER, k)
        values = Doubling(VALUE_GATHER, v)
        q = order(project_q, normed, w_qkv, bias, cos, sin)
        keys.go(order), values.go(order)
        seed = order(lambda c: (c * valid[..., None].astype(BF)).reshape(tokens, width), cotangent)
        w_gate = order(functools.partial(cut_cols, first=0), w_gate_up)
        keys.go(order), values.go(order)
        w_up = order(functools.partial(cut_cols, first=FF), w_gate_up)
        w_d = order(cut_rows, w_down)
        keys.go(order), values.go(order)
        seed_theirs = other_core(seed)
        start_rows, spots, order_x, order_y = order(small_inputs, begins)
        normed_t = order(lambda a, b: nt(a, b).astype(BF), order_x, normed)
        k_all, v_all = keys.go(order), values.go(order)
    else:
        k_all, v_all = lax.all_gather(k, SEQ, axis=0), lax.all_gather(v, SEQ, axis=0)
        q = project_q(normed, w_qkv, bias, cos, sin)
        seed = (cotangent * valid[..., None].astype(BF)).reshape(tokens, width)
        seed_theirs = other_core(seed)
        w_gate, w_up, w_d = cut_cols(w_gate_up, 0), cut_cols(w_gate_up, FF), cut_rows(w_down)
        start_rows, spots, order_x, order_y = small_inputs(begins)
        normed_t = nt(order_x, normed).astype(BF)
    low = begins[:, 0] // (GROUP * length)
    me_1 = jnp.reshape(me, (1,)).astype(jnp.int32)
    q = q.reshape(streams, length, QW)
    mixed, lse = attend(q, k_all, v_all, start_rows, low, me_1, spots)
    mixed_flat = mixed.reshape(tokens, QW)
    middle = x.astype(F32) + nn(mixed_flat, w_out)
    inv_mlp = lax.rsqrt(jnp.mean(middle * middle, axis=-1, keepdims=True) + epsilon)
    unit_mlp = middle * inv_mlp
    gain_mlp = g_mlp.astype(F32)
    normed_mlp = (unit_mlp * gain_mlp).astype(BF)
    normed_theirs = other_core(normed_mlp)
    out_mine, out_theirs, back_mine, back_theirs, term_down, keep_gate, send_gate, keep_up, send_up = mlp(
        normed_mlp, normed_theirs, seed, seed_theirs, order_x, order_y, w_gate, w_up, w_d
    )
    order = Order(back_mine)
    back_theirs = other_core(back_theirs)
    out_theirs = other_core(out_theirs)
    if fast:
        gate_up = PairHalving(keep_gate, send_gate, keep_up, send_up)
        down = PlacedHalving(Z_FIRST, [term_down], half, order)

    grad_middle, grad_branch, grad_mixed, gain_mlp_part = order(
        middle_back, back_mine, back_theirs, middle, seed, g_mlp.reshape(1, -1), w_out
    )
    grad_mixed = grad_mixed.reshape(streams, length, QW)

    cos_s = cos.reshape(streams, length, LANES)
    sin_s = sin.reshape(streams, length, LANES)
    back = lambda first, count: attend_back(
        first, count, q, k_all, v_all, start_rows, low, me_1, spots, lse, mixed, grad_mixed, cos_s, sin_s
    )

    core_1 = jnp.reshape(core, (1,)).astype(jnp.int32)
    gain_attn = g_attn.reshape(1, -1)

    def finish(mine, theirs, middle):
        return (middle + mine + theirs).astype(BF)

    def both_cores(mine, dim):
        theirs = other_core(mine)
        first = jnp.where(core == 0, mine, theirs)
        second = jnp.where(core == 0, theirs, mine)
        return jnp.concatenate([first, second], dim).astype(F32)

    if fast:
        per = streams // PARTS
        rows = (n // 2) * per * length
        grads_q = []
        at = {"down": down, "gu": gate_up}
        value = {}

        def back_step(which):
            grad_q, *grads = attend_back(
                per * which, per, q, k_all, v_all, start_rows, low, order.enter(me_1), spots, lse, mixed, grad_mixed, cos_s, sin_s
            )
            order.token = grad_q
            grads_q.append(grad_q.reshape(per * length, QW))
            at["keys", which] = PairHalving(*[g.reshape(rows, KW) for g in grads], orders=(Y_FIRST, X_FIRST))

        def terms_step():
            value["q"] = jnp.concatenate(grads_q, 0)
            sent, kept = order(attention_terms, core_1, normed, mixed_flat, value["q"], grad_branch, order_x)
            value["attn"] = kept, other_core(sent)

        def attn_step():
            value["attn"] = order(add, *value["attn"])
            at["attn"] = Halving(X_FIRST, [value["attn"]], width, order)

        def last_step():
            grads = jnp.concatenate([value[f"keys:{i}"] for i in range(PARTS)], 0)
            value["input"], term, sums = order(
                last_back, grads, value["q"], w_qkv, x, gain_attn, cos, sin, normed_t,
                grad_middle, gain_mlp_part,
            )
            block = width // n
            extra = jnp.pad(sums.astype(BF).reshape(-1, LANES), ((0, block - sums.size // LANES), (0, 0)))
            term = order(lambda t, e: jnp.concatenate([t, jnp.tile(e, (n, 1))], 1), term, extra)
            at["kv"] = Halving(X_FIRST, [term], width, order)

        def finish_step():
            value["output"] = order(finish, out_mine, out_theirs, middle)

        steps = {"ab": back_step, "terms": terms_step, "attn0": attn_step, "last": last_step}
        steps["finish"] = finish_step
        for name in PLAN:
            head, *rest = name.split(":")
            rest = [int(r) for r in rest]
            if head in steps:
                steps[head](*rest)
            elif head == "gu":
                value[name] = gate_up.go(order, *rest)
            elif head == "keys":
                value[name] = at[head, rest[0]].go(order, *rest[1:])
            else:
                value[name] = at[name].go(order)
        output, grad_input = value["output"], value["input"]
        rows_gate, rows_up = value["gu"][:, :half], value["gu"][:, half:]
        rows_down, rows_attn, rows_kv = value["down"], value["attn"], value["kv"]
        rows_kv = add(rows_kv, other_core(rows_kv))
        sums = rows_kv[:, 2 * KW :].astype(F32).reshape(-1)
    else:
        grad_q, *grads = back(0, streams)
        grad_q = grad_q.reshape(tokens, QW)
        sent, kept = attention_terms(core_1, normed, mixed_flat, grad_q, grad_branch, order_x)
        rows_attn = reduce_rows(add(kept, other_core(sent)))
        output = finish(out_mine, out_theirs, middle)
        grad_k, grad_v = [reduce_rows(jnp.concatenate(g, 0).reshape(n * tokens, KW)) for g in (grads[:2], grads[2:])]
        grad_kv = jnp.concatenate([grad_k, grad_v], 1)
        grad_input, term, sums = last_back(
            grad_kv, grad_q, w_qkv, x, gain_attn, cos, sin, normed_t, grad_middle,
            gain_mlp_part,
        )
        rows_kv = reduce_rows(term)
        rows_kv = add(rows_kv, other_core(rows_kv))
        sums = sum_over_all(sums.reshape(-1, LANES)).reshape(-1)
        rows_gate = reduce_rows(jnp.concatenate([keep_gate, send_gate], 0))
        rows_up = reduce_rows(jnp.concatenate([keep_up, send_up], 0))
        rows_down = reduce_rows(term_down)

    rows_down = to_owner(rows_down, Z_FIRST)
    rows_attn = both_cores(rows_attn, 1)
    rows_out, rows_q = rows_attn[:, :width], rows_attn[:, width:]
    small = [QW + 2 * KW, QW + 2 * KW + width, QW + 2 * KW + 2 * width]
    bias_grad, gain_attn_grad, gain_mlp_grad, _ = jnp.split(sums, small)
    return (
        output.reshape(streams, length, width),
        grad_input.reshape(streams, length, width),
        jnp.concatenate([rows_q, rows_kv[:, : 2 * KW].astype(F32)], 1),
        bias_grad,
        gain_attn_grad,
        rows_out,
        gain_mlp_grad,
        jnp.concatenate([both_cores(rows_gate, 1), both_cores(rows_up, 1)], 1),
        both_cores(rows_down, 0),
    )


PARTS = 1
PLAN = (
    "ab:0", "gu:0", "gu:1", "down", "keys:0:0", "keys:0:1", "terms", "attn0", "keys:0", "down", "keys:0",
    "gu", "finish", "attn", "keys:0", "down", "last", "gu", "kv", "attn", "kv", "attn", "kv", "gu", "down",
    "attn", "kv",
)


def solution(mesh):
    n = mesh.shape["seq"]
    sizes = {16: (4, 2, 2), 64: (4, 4, 4)}.get(n, (n, 1, 1))
    fine = Mesh(np.asarray(mesh.devices).reshape(*sizes, mesh.shape["dp"]), (*SEQ, "dp"))
    in_specs = (P("dp", SEQ, None), P("dp", None), P(), P(), P(), P(), P(), P(), P(), P("dp", SEQ, None))
    out_specs = (
        P("dp", SEQ, None), P("dp", SEQ, None), P(SEQ, None), P(), P(), P(SEQ, None), P(), P(SEQ, None), P(SEQ, None),
    )
    return jax.shard_map(shards, mesh=fine, in_specs=in_specs, out_specs=out_specs, check_vma=False)
```

```python
import functools

import jax
import jax.numpy as jnp
import numpy as np
from jax import lax
from jax.experimental import pallas as pl
from jax.experimental.pallas import tpu as pltpu
from jax.sharding import Mesh
from jax.sharding import PartitionSpec as P

HEADS = 14
KVH = 2
HD = 64
FF = 4864
QW = HEADS * HD
KW = KVH * HD
LANES = 128
GROUP = 8
CHUNK = 256
NEG = -1e30
epsilon = 1e-06
rope_base = 1000000.0
BF = jnp.bfloat16
F32 = jnp.float32
SEQ = ("az", "ay", "ax")

SAME = [h for h in range(HEADS) if h % 2 == h // (HEADS // KVH)]
OTHER = [h for h in range(HEADS) if h % 2 != h // (HEADS // KVH)]


def nt(a, b):
    return lax.dot_general(a, b, (((1,), (1,)), ((), ())), preferred_element_type=F32)


def tn(a, b):
    return lax.dot_general(a, b, (((0,), (0,)), ((), ())), preferred_element_type=F32)


def nn(a, b):
    return lax.dot_general(a, b, (((1,), (0,)), ((), ())), preferred_element_type=F32)


def lane_iota(shape):
    return lax.broadcasted_iota(jnp.int32, shape, len(shape) - 1)


def half_swap(tile):
    low = lane_iota(tile.shape) % HD < HD // 2
    return jnp.where(low, pltpu.roll(tile, LANES - HD // 2, 1), pltpu.roll(tile, HD // 2, 1))


def cost(us):
    return pl.CostEstimate(flops=int(us * 1e6 * 90), bytes_accessed=1 << 16, transcendentals=0)


def params(limit=56):
    return pltpu.CompilerParams(vmem_limit_bytes=limit << 20)


def turn(part, cos, sin):
    return part * cos + half_swap(part) * sin


def project_kv_kernel(x_ref, w_ref, small_ref, cos_ref, sin_ref, normed_ref, k_ref, v_ref):
    step = pl.program_id(0)

    @pl.when(step == 0)
    def _():
        x = x_ref[...].astype(F32)
        inv = lax.rsqrt(jnp.mean(x * x, axis=-1, keepdims=True) + epsilon)
        normed_ref[...] = (x * inv * small_ref[:, QW + 2 * KW :].astype(F32)).astype(BF)

    at = pl.multiple_of(QW + step * KW, LANES)
    part = nn(normed_ref[...], w_ref[...]) + small_ref[:, pl.ds(at, KW)].astype(F32)

    @pl.when(step == 0)
    def _():
        k_ref[...] = turn(part, cos_ref[...], sin_ref[...]).astype(BF)

    @pl.when(step == 1)
    def _():
        v_ref[...] = part.astype(BF)


def project_kv(x, w, small, cos, sin):
    tokens, width = x.shape
    fixed = lambda *shape: pl.BlockSpec(shape, lambda i: (0, 0))
    return pl.pallas_call(
        project_kv_kernel,
        grid=(2,),
        in_specs=[
            fixed(tokens, width),
            pl.BlockSpec((width, KW), lambda i: (0, QW // KW + i)),
            fixed(*small.shape),
            fixed(tokens, LANES),
            fixed(tokens, LANES),
        ],
        out_specs=[fixed(tokens, width), fixed(tokens, KW), fixed(tokens, KW)],
        out_shape=(
            jax.ShapeDtypeStruct((tokens, width), BF),
            jax.ShapeDtypeStruct((tokens, KW), BF),
            jax.ShapeDtypeStruct((tokens, KW), BF),
        ),
        compiler_params=params(),
        cost_estimate=cost(3),
        name="project_kv",
    )(x, w, small, cos, sin)


def project_q_kernel(normed_ref, w_ref, b_ref, cos_ref, sin_ref, q_ref):
    normed = normed_ref[...]
    cos = cos_ref[...]
    sin = sin_ref[...]
    for first in range(0, QW, 2 * LANES):
        cols = slice(first, min(first + 2 * LANES, QW))
        both = nn(normed, w_ref[:, cols]) + b_ref[:, cols].astype(F32)
        for at in range(0, both.shape[1], LANES):
            part = turn(both[:, at : at + LANES], cos, sin) * HD**-0.5
            q_ref[:, first + at : first + at + LANES] = part.astype(BF)


def project_q(normed, w, b, cos, sin):
    tokens, width = normed.shape
    return pl.pallas_call(
        project_q_kernel,
        out_shape=jax.ShapeDtypeStruct((tokens, QW), BF),
        compiler_params=params(),
        cost_estimate=cost(4),
        name="project_q",
    )(normed, w, b, cos, sin)


def masked_heads(ref, heads, scratch, rows):
    lane = lane_iota((rows, LANES))
    for slot, h in enumerate(heads):
        pair = ref[0, :, h // 2 * LANES : h // 2 * LANES + LANES]
        keep = (lane >= HD) if h % 2 else (lane < HD)
        scratch[slot * rows : (slot + 1) * rows, :LANES] = jnp.where(keep, pair, jnp.zeros_like(pair))


def swapped(a):
    return jnp.concatenate([a[:, HD:], a[:, :HD]], 1)


def chunks(width):
    return [slice(at, min(at + CHUNK, width)) for at in range(0, width, CHUNK)]


def allowed_pairs(start_ref, first, keys, cols):
    index = first + lax.broadcasted_iota(jnp.int32, (keys, cols.stop - cols.start), 0)
    return (index <= start_ref[0, 1:2, cols]) & (index >= start_ref[0, 0:1, cols])


def gathered(first_ref, second_ref, spot_ref, which, j):
    half = first_ref.shape[0]

    def block(i):
        spot = spot_ref[which, j * GROUP + i]
        one = first_ref[jnp.minimum(spot, half - 1), 0]
        two = second_ref[jnp.maximum(spot - half, 0), 0]
        return jnp.where(jnp.broadcast_to(spot < half, one.shape), one, two)

    return jnp.concatenate([block(i) for i in range(GROUP)], 0)


def forward_kernel(low_ref, me_ref, spot_ref, q_ref, k1_ref, k2_ref, v1_ref, v2_ref, start_ref, out_ref, lse_ref, qa, qb, ma, la, oa, mb, lb, ob, weights):
    rows = q_ref.shape[1]
    stream = pl.program_id(0)
    me = me_ref[0]
    masked_heads(q_ref, SAME, qa, rows)
    masked_heads(q_ref, OTHER, qb, rows)
    for m, l, o in ((ma, la, oa), (mb, lb, ob)):
        m[...] = jnp.full_like(m, NEG)
        l[...] = jnp.zeros_like(l)
        o[...] = jnp.zeros_like(o)
    keys = GROUP * rows

    def step(j, carry):
        key = gathered(k1_ref, k2_ref, spot_ref, 0, j)
        value = gathered(v1_ref, v2_ref, spot_ref, 1, j)
        for swap, q, m, l, o in ((False, qa, ma, la, oa), (True, qb, mb, lb, ob)):
            width = q.shape[0]
            k = swapped(key) if swap else key
            v = swapped(value) if swap else value
            for cols in chunks(width):
                s = jnp.where(allowed_pairs(start_ref, j * keys, keys, cols), nt(k, q[cols]), NEG)
                before = m[:, cols]
                top = jnp.maximum(before, jnp.max(s, axis=0, keepdims=True))
                p = jnp.exp(s - top)
                shrink = jnp.exp(before - top)
                m[:, cols] = top
                l[:, cols] = l[:, cols] * shrink + jnp.sum(p, axis=0, keepdims=True)
                o[:, cols] = o[:, cols] * shrink
                weights[:, cols] = p.astype(BF)
            o[...] += nn(v.T, weights[:, :width])
        return carry

    lax.fori_loop(low_ref[stream], me // GROUP + 1, step, 0)
    lane = lane_iota((rows, LANES))
    parts = {}
    for row, (heads, m, l, o) in enumerate(((SAME, ma, la, oa), (OTHER, mb, lb, ob))):
        total = l[...]
        flat = (o[...] / total).T
        lse_ref[0, row : row + 1, : total.shape[1]] = m[...] + jnp.log(total)
        for slot, h in enumerate(heads):
            parts[h] = flat[slot * rows : (slot + 1) * rows]
    for pair in range(HEADS // 2):
        both = jnp.where(lane < HD, parts[2 * pair], parts[2 * pair + 1])
        out_ref[0, :, pair * LANES : (pair + 1) * LANES] = both.astype(BF)


def attend(q, k_all, v_all, start_rows, low, me, spots):
    streams, rows, width = q.shape
    half = k_all[0].shape[0]
    a, b = len(SAME) * rows, len(OTHER) * rows
    tok = lambda w: pl.BlockSpec((1, rows, w), lambda s, *_: (s, 0, 0))
    two = pl.BlockSpec((1, 2, a), lambda s, *_: (s, 0, 0))
    return pl.pallas_call(
        forward_kernel,
        grid_spec=pltpu.PrefetchScalarGridSpec(
            num_scalar_prefetch=3,
            grid=(streams,),
            in_specs=[tok(width), *[pl.BlockSpec((half, 1, rows, KW), lambda s, *_: (0, s, 0, 0))] * 4, two],
            out_specs=[tok(width), two],
            scratch_shapes=[
                pltpu.VMEM((a, LANES), BF),
                pltpu.VMEM((b, LANES), BF),
                pltpu.VMEM((1, a), F32),
                pltpu.VMEM((1, a), F32),
                pltpu.VMEM((LANES, a), F32),
                pltpu.VMEM((1, b), F32),
                pltpu.VMEM((1, b), F32),
                pltpu.VMEM((LANES, b), F32),
                pltpu.VMEM((GROUP * rows, a), BF),
            ],
        ),
        out_shape=(
            jax.ShapeDtypeStruct((streams, rows, width), BF),
            jax.ShapeDtypeStruct((streams, 2, a), F32),
        ),
        compiler_params=params(),
        cost_estimate=cost(18),
        name="attend",
    )(low, me, spots, q, *k_all, *v_all, start_rows)


def three_parts(column):
    high = column.astype(BF)
    rest = column - high.astype(F32)
    middle = rest.astype(BF)
    return high, middle, (rest - middle.astype(F32)).astype(BF)


def put_column(scratch, at, column, rows):
    lane = lane_iota((rows, LANES))
    out = jnp.zeros((rows, LANES), F32)
    for i, piece in enumerate(three_parts(column)):
        out = jnp.where(lane == i, piece.astype(F32), out)
    scratch[at, LANES:] = out.astype(BF)


def backward_kernel(
    first, low_ref, me_ref, spot_ref, q_ref, k1_ref, k2_ref, v1_ref, v2_ref, start_ref, lse_ref, mixed_ref, grad_ref, cos_ref, sin_ref, dq_ref, dkk_ref,
    dks_ref, dvk_ref, dvs_ref, qa, qb, ga, gb, ta, tb, dk_all, dv_all, weights, grads,
):
    rows = q_ref.shape[1]
    stream = first + pl.program_id(0)
    me = me_ref[0]
    masked_heads(q_ref, SAME, qa, rows)
    masked_heads(q_ref, OTHER, qb, rows)
    masked_heads(grad_ref, SAME, ga, rows)
    masked_heads(grad_ref, OTHER, gb, rows)
    lane = lane_iota((rows, LANES))
    for heads, g in ((SAME, ga), (OTHER, gb)):
        for slot, h in enumerate(heads):
            at = slice(slot * rows, (slot + 1) * rows)
            cols = slice(h // 2 * LANES, h // 2 * LANES + LANES)
            keep = (lane >= HD) if h % 2 else (lane < HD)
            product = grad_ref[0, :, cols].astype(F32) * mixed_ref[0, :, cols].astype(F32)
            delta = jnp.sum(jnp.where(keep, product, 0.0), axis=-1, keepdims=True)
            put_column(g, at, -delta, rows)
    ta[...] = jnp.zeros_like(ta)
    tb[...] = jnp.zeros_like(tb)
    dk_all[...] = jnp.zeros_like(dk_all)
    dv_all[...] = jnp.zeros_like(dv_all)
    keys = GROUP * rows
    ones = (lane_iota((keys, LANES)) < 3).astype(F32).astype(BF)

    def step(j, carry):
        key = gathered(k1_ref, k2_ref, spot_ref, 0, j)
        value = gathered(v1_ref, v2_ref, spot_ref, 1, j)
        grad_keys = []
        grad_values = []
        for row, (q, g, t) in enumerate(((qa, ga, ta), (qb, gb, tb))):
            width = q.shape[0]
            k = swapped(key) if row else key
            v = jnp.concatenate([swapped(value) if row else value, ones], 1)
            for cols in chunks(width):
                s = nt(k, q[cols]) - lse_ref[0, row : row + 1, cols]
                p = jnp.exp(jnp.where(allowed_pairs(start_ref, j * keys, keys, cols), s, NEG))
                weights[:, cols] = p.astype(BF)
                grads[:, cols] = (p * nt(v, g[cols])).astype(BF)
            grad_values.append(nn(weights[:, :width], g[:, :LANES]))
            grad_keys.append(nn(grads[:, :width], q[...]))
            t[...] += nn(k.T, grads[:, :width])
        for out_ref, (same, other) in ((dk_all, grad_keys), (dv_all, grad_values)):
            total = (same + swapped(other)).astype(BF)
            out_ref[pl.ds(j * GROUP, GROUP)] = total.reshape(GROUP, rows, KW)
        return carry

    lax.fori_loop(low_ref[stream], me // GROUP + 1, step, 0)
    half = dkk_ref.shape[0]
    for which, (keep_ref, send_ref, out_ref) in enumerate(((dkk_ref, dks_ref, dk_all), (dvk_ref, dvs_ref, dv_all))):
        for spot in range(half):
            keep_ref[spot, 0] = out_ref[spot_ref[2 + which, spot]]
            send_ref[spot, 0] = out_ref[spot_ref[2 + which, half + spot]]
    parts = {}
    for heads, t in ((SAME, ta), (OTHER, tb)):
        flat = t[...].T
        for slot, h in enumerate(heads):
            parts[h] = flat[slot * rows : (slot + 1) * rows]
    cos = cos_ref[0]
    sin = sin_ref[0]
    for pair in range(HEADS // 2):
        both = jnp.where(lane < HD, parts[2 * pair], parts[2 * pair + 1]) * HD**-0.5
        dq_ref[0, :, pair * LANES : (pair + 1) * LANES] = (both * cos - half_swap(both) * sin).astype(BF)


def attend_back(first, streams, q, k_all, v_all, start_rows, low, me, spots, lse, mixed, grad, cos, sin):
    rows, width = q.shape[1:]
    half = k_all[0].shape[0]
    n = 2 * half
    a, b = len(SAME) * rows, len(OTHER) * rows
    tok = lambda w: pl.BlockSpec((1, rows, w), lambda s, *_: (s + first, 0, 0))
    two = pl.BlockSpec((1, 2, a), lambda s, *_: (s + first, 0, 0))
    key_spec = pl.BlockSpec((n // 2, 1, rows, KW), lambda s, *_: (0, s, 0, 0))
    return pl.pallas_call(
        functools.partial(backward_kernel, first),
        grid_spec=pltpu.PrefetchScalarGridSpec(
            num_scalar_prefetch=3,
            grid=(streams,),
            in_specs=[
                tok(width),
                *[pl.BlockSpec((half, 1, rows, KW), lambda s, *_: (0, s + first, 0, 0))] * 4,
                two,
                two,
                tok(width),
                tok(width),
                tok(LANES),
                tok(LANES),
            ],
            out_specs=[pl.BlockSpec((1, rows, width), lambda s, *_: (s, 0, 0)), *[key_spec] * 4],
            scratch_shapes=[
                pltpu.VMEM((a, LANES), BF),
                pltpu.VMEM((b, LANES), BF),
                pltpu.VMEM((a, 2 * LANES), BF),
                pltpu.VMEM((b, 2 * LANES), BF),
                pltpu.VMEM((LANES, a), F32),
                pltpu.VMEM((LANES, b), F32),
                *[pltpu.VMEM((n, rows, KW), BF)] * 2,
                *[pltpu.VMEM((GROUP * rows, a), BF)] * 2,
            ],
        ),
        out_shape=(
            jax.ShapeDtypeStruct((streams, rows, width), BF),
            *[jax.ShapeDtypeStruct((n // 2, streams, rows, KW), BF)] * 4,
        ),
        compiler_params=params(),
        cost_estimate=cost(8 * streams),
        name="attend_back",
    )(low, me, spots, q, *k_all, *v_all, start_rows, lse, mixed, grad, cos, sin)


TILE = 256


def mlp_kernel(
    valid, mine_ref, theirs_ref, sm_ref, st_ref, order_ref, wg_ref, wu_ref, wd_ref, om_ref, ot_ref, bm_ref, bt_ref,
    td_ref, gk_ref, gs_ref, uk_ref, us_ref, n_ref, s_ref, turned_ref,
):
    rows = mine_ref.shape[0]
    step = pl.program_id(0)
    sums = (om_ref, ot_ref, bm_ref, bt_ref)

    @pl.when(step == 0)
    def _():
        n_ref[:rows] = mine_ref[...]
        n_ref[rows:] = theirs_ref[...]
        s_ref[:rows] = sm_ref[...]
        s_ref[rows:] = st_ref[...]
        turned_ref[...] = nt(order_ref[...], n_ref[...]).astype(BF)
        for ref in sums:
            ref[...] = jnp.zeros_like(ref)

    normed = n_ref[...]
    seed = s_ref[...]
    left = valid - step * TILE
    inside = lambda w, dim: jnp.where(lax.broadcasted_iota(jnp.int32, w.shape, dim) < left, w, jnp.zeros_like(w))
    wg, wu, wd = inside(wg_ref[...], 1), inside(wu_ref[...], 1), inside(wd_ref[...], 0)
    gate = nn(normed, wg)
    up = nn(normed, wu)
    grad = nt(seed, wd)
    sig = 1.0 / (1.0 + jnp.exp(-gate))
    silu = gate * sig
    active = (silu * up).astype(BF)
    grad_up = (grad * silu).astype(BF)
    grad_gate = (grad * up * (sig * (1.0 + gate * (1.0 - sig)))).astype(BF)
    td_ref[...] = tn(active, seed).astype(BF)
    quarter = gk_ref.shape[0] // 2
    rows_of = lambda a, i: a[i * quarter : (i + 1) * quarter]
    for grad_pre, keep, send, quarters in ((grad_gate, gk_ref, gs_ref, (0, 1, 2, 3)), (grad_up, uk_ref, us_ref, (0, 2, 1, 3))):
        term = nn(turned_ref[...], grad_pre).astype(BF)
        for i in range(2):
            keep[i * quarter : (i + 1) * quarter] = rows_of(term, quarters[i])
            send[i * quarter : (i + 1) * quarter] = rows_of(term, quarters[2 + i])
    out = nn(active, wd)
    back = nt(grad_gate, wg) + nt(grad_up, wu)
    for ref, part in zip(sums, (out[:rows], out[rows:], back[:rows], back[rows:])):
        ref[...] += part


def fixed(*shape):
    return pl.BlockSpec(shape, lambda *_: (0,) * len(shape))


def shaped(dtype, *dims):
    return jax.ShapeDtypeStruct(dims, dtype)


def mlp(mine, theirs, seed_mine, seed_theirs, order, w_gate, w_up, w_d):
    rows, width = mine.shape
    half = w_gate.shape[1]
    cols = lambda size: pl.BlockSpec((size, TILE), lambda i: (0, i))
    down = pl.BlockSpec((TILE, width), lambda i: (i, 0))
    part = fixed(rows, width)
    return pl.pallas_call(
        functools.partial(mlp_kernel, half),
        grid=(pl.cdiv(half, TILE),),
        in_specs=[part] * 4 + [fixed(width, width)] + [cols(width)] * 2 + [down],
        out_specs=[part] * 4 + [down] + [cols(width // 2)] * 4,
        out_shape=[shaped(F32, rows, width)] * 4 + [shaped(BF, half, width)] + [shaped(BF, width // 2, half)] * 4,
        scratch_shapes=[pltpu.VMEM((2 * rows, width), BF)] * 2 + [pltpu.VMEM((width, 2 * rows), BF)],
        compiler_params=params(),
        cost_estimate=cost(40),
        name="mlp",
    )(mine, theirs, seed_mine, seed_theirs, order, w_gate, w_up, w_d)


def middle_kernel(bm_ref, bt_ref, middle_ref, seed_ref, g_ref, w_ref, gm_ref, gb_ref, gx_ref, gain_ref):
    @pl.when(pl.program_id(0) == 0)
    def _():
        gain_ref[...] = jnp.zeros_like(gain_ref)

    grad = bm_ref[...] + bt_ref[...]
    middle = middle_ref[...]
    inv = lax.rsqrt(jnp.mean(middle * middle, axis=-1, keepdims=True) + epsilon)
    unit = middle * inv
    scaled = grad * g_ref[...].astype(F32)
    grad_middle = seed_ref[...].astype(F32) + inv * (scaled - unit * jnp.mean(scaled * unit, axis=-1, keepdims=True))
    gm_ref[...] = grad_middle
    branch = grad_middle.astype(BF)
    gb_ref[...] = branch
    gx_ref[...] = nt(branch, w_ref[...]).astype(BF)
    gain_ref[...] += jnp.sum(grad * unit, axis=0, keepdims=True)


def middle_back(mine, theirs, middle, seed, gain, w_out):
    tokens, width = middle.shape
    rows = tokens // 4
    part = pl.BlockSpec((rows, width), lambda i: (i, 0))
    return pl.pallas_call(
        middle_kernel,
        grid=(4,),
        in_specs=[part] * 4 + [fixed(1, width), fixed(width, width)],
        out_specs=[part] * 3 + [fixed(1, width)],
        out_shape=[shaped(F32, tokens, width), shaped(BF, tokens, width), shaped(BF, tokens, width), shaped(F32, 1, width)],
        compiler_params=params(),
        cost_estimate=cost(5),
        name="middle_back",
    )(mine, theirs, middle, seed, gain, w_out)


def attention_terms_kernel(core_ref, normed_ref, mixed_ref, gq_ref, gb_ref, order_ref, sent_ref, kept_ref):
    first = core_ref[0] == 0
    order = order_ref[...]
    pick = lambda flag, a, b: jnp.where(jnp.broadcast_to(flag, a.shape), a[...], b[...])
    for out_ref, flag in ((sent_ref, first), (kept_ref, jnp.logical_not(first))):
        left = nt(order, pick(flag, normed_ref, mixed_ref)).astype(BF)
        out_ref[...] = nn(left, pick(flag, gq_ref, gb_ref)).astype(BF)


def attention_terms(core, normed, mixed, grad_q, grad_branch, order):
    width = normed.shape[1]
    whole = pl.BlockSpec(memory_space=pltpu.VMEM)
    return pl.pallas_call(
        attention_terms_kernel,
        in_specs=[pl.BlockSpec(memory_space=pltpu.SMEM)] + [whole] * 5,
        out_specs=[whole] * 2,
        out_shape=[shaped(BF, width, width)] * 2,
        compiler_params=params(),
        cost_estimate=cost(5),
        name="attention_terms",
    )(core, normed, mixed, grad_q, grad_branch, order)


def last_kernel(gkv_ref, gq_ref, w_ref, x_ref, g_ref, cos_ref, sin_ref, nt_ref, gm_ref, gain_ref, gi_ref, term_ref,
                sums_ref):
    grads = gkv_ref[...]
    keys = grads[:, :KW].astype(F32)
    keys = (keys * cos_ref[...] - half_swap(keys) * sin_ref[...]).astype(BF)
    grad_kv = jnp.concatenate([keys, grads[:, KW:]], 1)
    term_ref[...] = nn(nt_ref[...], grad_kv).astype(BF)
    grad = nt(gq_ref[...], w_ref[:, :QW]) + nt(grad_kv, w_ref[:, QW:])
    x = x_ref[...].astype(F32)
    inv = lax.rsqrt(jnp.mean(x * x, axis=-1, keepdims=True) + epsilon)
    unit = x * inv
    scaled = grad * g_ref[...].astype(F32)
    gi_ref[...] = gm_ref[...] + inv * (scaled - unit * jnp.mean(scaled * unit, axis=-1, keepdims=True))
    over = lambda a: jnp.sum(a.astype(F32), axis=0, keepdims=True)
    at = 0
    for row in (over(gq_ref[...]), over(grad_kv), over(grad * unit), gain_ref[...]):
        sums_ref[:, at : at + row.shape[1]] = row
        at += row.shape[1]


def last_back(grads, grad_q, w_qkv, x, gain, cos, sin, normed_t, grad_middle, gain_mlp_part):
    tokens, width = x.shape
    return pl.pallas_call(
        last_kernel,
        out_shape=[
            shaped(F32, tokens, width),
            shaped(BF, width, 2 * KW),
            shaped(F32, 1, QW + 2 * KW + 2 * width),
        ],
        compiler_params=params(),
        cost_estimate=cost(6),
        name="last_back",
    )(grads, grad_q, w_qkv, x, gain, cos, sin, normed_t, grad_middle, gain_mlp_part)


def after(a, *others):
    return lax.optimization_barrier((a, others))[0]


class Order:
    def __init__(self, token):
        self.token = token

    def enter(self, inputs):
        return lax.optimization_barrier((inputs, self.token))[0]

    def __call__(self, step, *inputs):
        self.token = step(*self.enter(inputs))
        return self.token


def other_core(a):
    return lax.ppermute(a, "dp", [(0, 1), (1, 0)])


def pair_up(a, axis, step):
    return lax.ppermute(a, axis, [(i, i ^ step) for i in range(lax.axis_size(axis))])


def total(terms):
    return functools.reduce(lambda a, b: a + b, [a.astype(F32) for a in terms]).astype(BF)


def add(a, b):
    return total((a, b))


Z, Y, X = SEQ
X_FIRST = ((X, 1), (Y, 1), (Z, 1), (Z, 2))
Y_FIRST = ((Y, 1), (X, 1), (Z, 1), (Z, 2))
Z_FIRST = ((Z, 1), (X, 1), (Y, 1), (Z, 2))
KEY_GATHER = ((Y, 1), (X, 1), (Z, 2), (Z, 1))
VALUE_GATHER = X_FIRST


def halving():
    return [lax.axis_size(axis) for axis in SEQ] == [4, 2, 2]


def my_bit(axis, step):
    return (lax.axis_index(axis) // step) % 2


def device_at(order, spot, relative):
    place = 0
    weight = {(X, 1): 1, (Y, 1): 2, (Z, 1): 4, (Z, 2): 8}
    for i, (axis, step) in enumerate(order):
        bit = (spot >> (len(order) - 1 - i)) & 1
        if relative:
            bit = bit ^ my_bit(axis, step)
        place = place + bit * weight[axis, step]
    return place


def spots_of_devices(order):
    n = lax.axis_size(SEQ)
    if not halving():
        return jnp.arange(n)
    spots = jnp.arange(n)
    return jnp.sum(jnp.where(device_at(order, spots, True)[:, None] == spots[None, :], spots[:, None], 0), 0)


def devices_at_spots(order):
    n = lax.axis_size(SEQ)
    return device_at(order, jnp.arange(n), True) if halving() else jnp.arange(n)


def row_order(order, width):
    n = lax.axis_size(SEQ)
    row = jnp.arange(width)
    source = row
    if halving():
        source = device_at(order, row // (width // n), True) * (width // n) + row % (width // n)
    return (source[:, None] == jnp.arange(width)[None, :]).astype(BF)


class Halving:
    def __init__(self, steps, arrays, rows, order=None, send=None):
        self.steps = list(steps)
        self.arrays = list(arrays)
        self.firsts = [0] * len(self.arrays)
        self.rows = rows
        if send is None:
            self.go(order)
        else:
            self.move(send)

    def halves(self):
        return 0, self.rows

    def move(self, send):
        self.arrays.append(pair_up(send, *self.steps.pop(0)))
        self.firsts.append(0)

    def sum(self, offset):
        cut = lambda a, first: lax.dynamic_slice_in_dim(a, first + offset, self.rows, 0)
        return total([cut(a, first) for a, first in zip(self.arrays, self.firsts)])

    def go(self, order):
        self.arrays = list(order.enter(self.arrays))
        if not self.steps:
            order.token = self.sum(0)
            return order.token
        self.rows //= 2
        kept, sent = self.halves()
        send = order.token = self.sum(sent)
        self.firsts = [first + kept for first in self.firsts]
        self.move(send)


class PlacedHalving(Halving):
    def halves(self):
        bit = my_bit(*self.steps[0])
        return bit * self.rows, (1 - bit) * self.rows


class PairHalving:
    def __init__(self, a_keep, a_send, b_keep, b_send, orders=(X_FIRST, Y_FIRST)):
        rows = a_keep.shape[0]
        self.pair = [
            Halving(orders[0][:2], [a_keep], rows, send=a_send),
            Halving(orders[1][:2], [b_keep], rows, send=b_send),
        ]
        self.last = orders[0][2:]
        self.count = 0

    def go(self, order, which=None):
        if which is not None:
            return self.pair[which].go(order)
        self.count += 1
        a, b = self.pair
        if self.count == 1:
            a.arrays, b.arrays = order.enter((list(a.arrays), list(b.arrays)))
            both = order.token = jnp.concatenate([a.sum(0), b.sum(0)], 1)
            half = both.shape[0] // 2
            self.rest = Halving(self.last, [both], half, send=both[half:])
        else:
            return self.rest.go(order)


def reduce_rows(a):
    return lax.psum_scatter(a, SEQ, scatter_dimension=0, tiled=True)


class Doubling:
    def __init__(self, order, a):
        self.steps = list(reversed(order))
        self.all = a[None]
        self.got = pair_up(self.all, *self.steps.pop(0))

    def go(self, order):
        if not self.steps:
            return self.all, self.got
        self.all = order(lambda a, b: jnp.concatenate([a, b], 0), self.all, self.got)
        self.got = pair_up(self.all, *self.steps.pop(0))


def to_owner(a, order):
    n = lax.axis_size(SEQ)
    holder = [device_at(order, spot, False) for spot in range(n)] if halving() else list(range(n))
    pairs = [(holder[spot] * 2 + core, core * n + spot) for spot in range(n) for core in range(2)]
    return lax.ppermute(a, (*SEQ, "dp"), pairs)


def sum_over_all(a):
    for axis in ("dp", *SEQ[::-1]):
        size = lax.axis_size(axis)
        step = 1
        while step < size:
            a = a + lax.ppermute(a, axis, [(i, i ^ step) for i in range(size)])
            step *= 2
    return a


def layout(lengths, offset, row_count):
    places = offset + jnp.arange(row_count, dtype=jnp.int32)
    slots = jnp.arange(lengths.shape[1])
    ends = jnp.sum(jnp.where(slots[:, None] <= slots[None, :], lengths[:, :, None], 0), axis=1)
    after = (places[None, :, None] >= ends[:, None, :]).astype(jnp.int32)
    begins = jnp.sum(after * lengths[:, None, :], axis=-1, dtype=jnp.int32)
    return (places, begins, places[None, :] < ends[:, -1:])


def shards(inputs, lengths, w_qkv, b_qkv, g_attn, w_out, g_mlp, w_gate_up, w_down, cotangent):
    streams, length, width = inputs.shape
    tokens = streams * length
    n = 1
    for axis in SEQ:
        n *= lax.axis_size(axis)
    me = lax.axis_index(SEQ)
    core = lax.axis_index("dp")
    offset = me * length
    places, begins, valid = layout(lengths, offset, length)
    frequency = rope_base ** (-(jnp.arange(HD // 2, dtype=F32) * (2.0 / HD)))
    lane_frequency = jnp.tile(frequency, LANES // (HD // 2))
    sign = jnp.where(jnp.arange(LANES) % HD < HD // 2, -1.0, 1.0)
    angle = (places[None, :] - begins).astype(F32).reshape(tokens, 1) * lane_frequency
    cos = jnp.cos(angle)
    sin = jnp.sin(angle) * sign

    x = inputs.reshape(tokens, width)
    small = jnp.concatenate([b_qkv, g_attn]).reshape(1, -1)
    normed, k, v = project_kv(x, w_qkv, small, cos, sin)
    k, v = k.reshape(streams, length, KW), v.reshape(streams, length, KW)
    half = FF // 2

    def small_inputs(begins):
        start_rows = jnp.stack(
            [
                jnp.tile(begins, (1, len(SAME))),
                jnp.tile(jnp.broadcast_to(places[None], begins.shape), (1, len(SAME))),
            ],
            1,
        )
        spots = jnp.stack(
            [*map(spots_of_devices, (KEY_GATHER, VALUE_GATHER)), *map(devices_at_spots, (Y_FIRST, X_FIRST))]
        ).astype(jnp.int32)
        return start_rows, spots, row_order(X_FIRST, width)

    cut_cols = lambda w, first: lax.dynamic_slice_in_dim(w, first + core * half, half, 1)
    cut_rows = lambda w: lax.dynamic_slice_in_dim(w, core * half, half, 0)
    fast = halving()
    order = Order(k)
    if fast:
        keys = Doubling(KEY_GATHER, k)
        values = Doubling(VALUE_GATHER, v)
        q = order(project_q, normed, w_qkv, small, cos, sin)
        keys.go(order), values.go(order)
        seed = order(lambda c: (c * valid[..., None].astype(BF)).reshape(tokens, width), cotangent)
        w_gate = order(functools.partial(cut_cols, first=0), w_gate_up)
        keys.go(order), values.go(order)
        w_up = order(functools.partial(cut_cols, first=FF), w_gate_up)
        w_d = order(cut_rows, w_down)
        keys.go(order), values.go(order)
        seed_theirs = other_core(seed)
        start_rows, spots, order_x = order(small_inputs, begins)
        normed_t = order(lambda a, b: nt(a, b).astype(BF), order_x, normed)
        k_all, v_all = keys.go(order), values.go(order)
    else:
        in_halves = lambda a: (a[: n // 2], a[n // 2 :])
        k_all, v_all = [in_halves(lax.all_gather(a, SEQ, axis=0)) for a in (k, v)]
        q = project_q(normed, w_qkv, small, cos, sin)
        seed = (cotangent * valid[..., None].astype(BF)).reshape(tokens, width)
        seed_theirs = other_core(seed)
        w_gate, w_up, w_d = cut_cols(w_gate_up, 0), cut_cols(w_gate_up, FF), cut_rows(w_down)
        start_rows, spots, order_x = small_inputs(begins)
        normed_t = nt(order_x, normed).astype(BF)
    low = begins[:, 0] // (GROUP * length)
    me_1 = jnp.reshape(me, (1,)).astype(jnp.int32)
    q = q.reshape(streams, length, QW)
    mixed, lse = attend(q, k_all, v_all, start_rows, low, me_1, spots)
    mixed_flat = mixed.reshape(tokens, QW)
    middle = x.astype(F32) + nn(mixed_flat, w_out)
    inv_mlp = lax.rsqrt(jnp.mean(middle * middle, axis=-1, keepdims=True) + epsilon)
    unit_mlp = middle * inv_mlp
    gain_mlp = g_mlp.astype(F32)
    normed_mlp = (unit_mlp * gain_mlp).astype(BF)
    normed_theirs = other_core(normed_mlp)
    out_mine, out_theirs, back_mine, back_theirs, term_down, keep_gate, send_gate, keep_up, send_up = mlp(
        normed_mlp, normed_theirs, seed, seed_theirs, order_x, w_gate, w_up, w_d
    )
    order = Order(back_mine)
    back_theirs = other_core(back_theirs)
    out_theirs = other_core(out_theirs)
    if fast:
        gate_up = PairHalving(keep_gate, send_gate, keep_up, send_up)
        down = PlacedHalving(Z_FIRST, [term_down], half, order)

    grad_middle, grad_branch, grad_mixed, gain_mlp_part = order(
        middle_back, back_mine, back_theirs, middle, seed, g_mlp.reshape(1, -1), w_out
    )
    grad_mixed = grad_mixed.reshape(streams, length, QW)

    cos_s = cos.reshape(streams, length, LANES)
    sin_s = sin.reshape(streams, length, LANES)
    back = lambda first, count: attend_back(
        first, count, q, k_all, v_all, start_rows, low, me_1, spots, lse, mixed, grad_mixed, cos_s, sin_s
    )

    core_1 = jnp.reshape(core, (1,)).astype(jnp.int32)
    gain_attn = g_attn.reshape(1, -1)

    def finish(mine, theirs, middle):
        return (middle + mine + theirs).astype(BF)

    def both_cores(mine, dim):
        theirs = other_core(mine)
        first = jnp.where(core == 0, mine, theirs)
        second = jnp.where(core == 0, theirs, mine)
        return jnp.concatenate([first, second], dim).astype(F32)

    if fast:
        per = streams // PARTS
        rows = (n // 2) * per * length
        grads_q = []
        at = {"down": down, "gu": gate_up}
        value = {}

        def back_step(which):
            grad_q, *grads = attend_back(
                per * which, per, q, k_all, v_all, start_rows, low, order.enter(me_1), spots, lse, mixed, grad_mixed, cos_s, sin_s
            )
            order.token = grad_q
            grads_q.append(grad_q.reshape(per * length, QW))
            at["keys", which] = PairHalving(*[g.reshape(rows, KW) for g in grads], orders=(Y_FIRST, X_FIRST))

        def terms_step():
            value["q"] = jnp.concatenate(grads_q, 0)
            sent, kept = order(attention_terms, core_1, normed, mixed_flat, value["q"], grad_branch, order_x)
            value["attn"] = kept, other_core(sent)

        def attn_step():
            value["attn"] = order(add, *value["attn"])
            at["attn"] = Halving(X_FIRST, [value["attn"]], width, order)

        def last_step():
            grads = jnp.concatenate([value[f"keys:{i}"] for i in range(PARTS)], 0)
            value["input"], term, sums = order(
                last_back, grads, value["q"], w_qkv, x, gain_attn, cos, sin, normed_t,
                grad_middle, gain_mlp_part,
            )
            block = width // n
            extra = jnp.pad(sums.astype(BF).reshape(-1, LANES), ((0, block - sums.size // LANES), (0, 0)))
            term = order(lambda t, e: jnp.concatenate([t, jnp.tile(e, (n, 1))], 1), term, extra)
            at["kv"] = Halving(X_FIRST, [term], width, order)

        def finish_step():
            value["output"] = order(finish, out_mine, out_theirs, middle)

        steps = {"ab": back_step, "terms": terms_step, "attn0": attn_step, "last": last_step}
        steps["finish"] = finish_step
        for name in PLAN:
            head, *rest = name.split(":")
            rest = [int(r) for r in rest]
            if head in steps:
                steps[head](*rest)
            elif head == "gu":
                value[name] = gate_up.go(order, *rest)
            elif head == "keys":
                value[name] = at[head, rest[0]].go(order, *rest[1:])
            else:
                value[name] = at[name].go(order)
        output, grad_input = value["output"], value["input"]
        rows_gate, rows_up = value["gu"][:, :half], value["gu"][:, half:]
        rows_down, rows_attn, rows_kv = value["down"], value["attn"], value["kv"]
        rows_kv = add(rows_kv, other_core(rows_kv))
        sums = rows_kv[:, 2 * KW :].astype(F32).reshape(-1)
    else:
        grad_q, *grads = back(0, streams)
        grad_q = grad_q.reshape(tokens, QW)
        sent, kept = attention_terms(core_1, normed, mixed_flat, grad_q, grad_branch, order_x)
        rows_attn = reduce_rows(add(kept, other_core(sent)))
        output = finish(out_mine, out_theirs, middle)
        grad_k, grad_v = [reduce_rows(jnp.concatenate(g, 0).reshape(n * tokens, KW)) for g in (grads[:2], grads[2:])]
        grad_kv = jnp.concatenate([grad_k, grad_v], 1)
        grad_input, term, sums = last_back(
            grad_kv, grad_q, w_qkv, x, gain_attn, cos, sin, normed_t, grad_middle,
            gain_mlp_part,
        )
        rows_kv = reduce_rows(term)
        rows_kv = add(rows_kv, other_core(rows_kv))
        sums = sum_over_all(sums.reshape(-1, LANES)).reshape(-1)
        rows_gate = reduce_rows(jnp.concatenate([keep_gate, send_gate], 0))
        cut_up = keep_up.shape[0] // 2
        rows_up = reduce_rows(jnp.concatenate([keep_up[:cut_up], send_up[:cut_up], keep_up[cut_up:], send_up[cut_up:]], 0))
        rows_down = reduce_rows(term_down)

    rows_down = to_owner(rows_down, Z_FIRST)
    rows_attn = both_cores(rows_attn, 1)
    rows_out, rows_q = rows_attn[:, :width], rows_attn[:, width:]
    small = [QW + 2 * KW, QW + 2 * KW + width, QW + 2 * KW + 2 * width]
    bias_grad, gain_attn_grad, gain_mlp_grad, _ = jnp.split(sums, small)
    return (
        output.reshape(streams, length, width),
        grad_input.reshape(streams, length, width),
        jnp.concatenate([rows_q, rows_kv[:, : 2 * KW].astype(F32)], 1),
        bias_grad,
        gain_attn_grad,
        rows_out,
        gain_mlp_grad,
        jnp.concatenate([both_cores(rows_gate, 1), both_cores(rows_up, 1)], 1),
        both_cores(rows_down, 0),
    )


PARTS = 1
PLAN = (
    "ab:0", "terms", "gu:0", "gu:1", "keys:0:0", "keys:0:1", "down", "keys:0", "attn0", "keys:0", "gu",
    "keys:0", "down", "last", "attn", "gu", "kv", "attn", "down", "kv", "attn", "kv", "finish", "gu", "down",
    "attn", "kv",
)


def solution(mesh):
    n = mesh.shape["seq"]
    sizes = {16: (4, 2, 2), 64: (4, 4, 4)}.get(n, (n, 1, 1))
    fine = Mesh(np.asarray(mesh.devices).reshape(*sizes, mesh.shape["dp"]), (*SEQ, "dp"))
    in_specs = (P("dp", SEQ, None), P("dp", None), P(), P(), P(), P(), P(), P(), P(), P("dp", SEQ, None))
    out_specs = (
        P("dp", SEQ, None), P("dp", SEQ, None), P(SEQ, None), P(), P(), P(SEQ, None), P(), P(SEQ, None), P(SEQ, None),
    )
    return jax.shard_map(shards, mesh=fine, in_specs=in_specs, out_specs=out_specs, check_vma=False)
```

```python
import functools

import jax
import jax.numpy as jnp
import numpy as np
from jax import lax
from jax.experimental import pallas as pl
from jax.experimental.pallas import tpu as pltpu
from jax.sharding import Mesh
from jax.sharding import PartitionSpec as P

HEADS = 14
KVH = 2
HD = 64
FF = 4864
QW = HEADS * HD
KW = KVH * HD
LANES = 128
GROUP = 8
CHUNK = 256
NEG = -1e30
epsilon = 1e-06
rope_base = 1000000.0
BF = jnp.bfloat16
F32 = jnp.float32
SEQ = ("az", "ay", "ax")

SAME = [h for h in range(HEADS) if h % 2 == h // (HEADS // KVH)]
OTHER = [h for h in range(HEADS) if h % 2 != h // (HEADS // KVH)]


def nt(a, b):
    return lax.dot_general(a, b, (((1,), (1,)), ((), ())), preferred_element_type=F32)


def tn(a, b):
    return lax.dot_general(a, b, (((0,), (0,)), ((), ())), preferred_element_type=F32)


def nn(a, b):
    return lax.dot_general(a, b, (((1,), (0,)), ((), ())), preferred_element_type=F32)


def lane_iota(shape):
    return lax.broadcasted_iota(jnp.int32, shape, len(shape) - 1)


def half_swap(tile):
    low = lane_iota(tile.shape) % HD < HD // 2
    return jnp.where(low, pltpu.roll(tile, LANES - HD // 2, 1), pltpu.roll(tile, HD // 2, 1))


def cost(us):
    return pl.CostEstimate(flops=int(us * 1e6 * 90), bytes_accessed=1 << 16, transcendentals=0)


def params(limit=56):
    return pltpu.CompilerParams(vmem_limit_bytes=limit << 20)


def turn(part, cos, sin):
    return part * cos + half_swap(part) * sin


def project_kv_kernel(x_ref, w_ref, small_ref, cos_ref, sin_ref, normed_ref, k_ref, v_ref):
    step = pl.program_id(0)

    @pl.when(step == 0)
    def _():
        x = x_ref[...].astype(F32)
        inv = lax.rsqrt(jnp.mean(x * x, axis=-1, keepdims=True) + epsilon)
        normed_ref[...] = (x * inv * small_ref[:, QW + 2 * KW :].astype(F32)).astype(BF)

    at = pl.multiple_of(QW + step * KW, LANES)
    part = nn(normed_ref[...], w_ref[...]) + small_ref[:, pl.ds(at, KW)].astype(F32)

    @pl.when(step == 0)
    def _():
        k_ref[...] = turn(part, cos_ref[...], sin_ref[...]).astype(BF)

    @pl.when(step == 1)
    def _():
        v_ref[...] = part.astype(BF)


def project_kv(x, w, small, cos, sin):
    tokens, width = x.shape
    fixed = lambda *shape: pl.BlockSpec(shape, lambda i: (0, 0))
    return pl.pallas_call(
        project_kv_kernel,
        grid=(2,),
        in_specs=[
            fixed(tokens, width),
            pl.BlockSpec((width, KW), lambda i: (0, QW // KW + i)),
            fixed(*small.shape),
            fixed(tokens, LANES),
            fixed(tokens, LANES),
        ],
        out_specs=[fixed(tokens, width), fixed(tokens, KW), fixed(tokens, KW)],
        out_shape=(
            jax.ShapeDtypeStruct((tokens, width), BF),
            jax.ShapeDtypeStruct((tokens, KW), BF),
            jax.ShapeDtypeStruct((tokens, KW), BF),
        ),
        compiler_params=params(),
        cost_estimate=cost(3),
        name="project_kv",
    )(x, w, small, cos, sin)


def project_q_kernel(normed_ref, w_ref, b_ref, cos_ref, sin_ref, q_ref):
    normed = normed_ref[...]
    cos = cos_ref[...]
    sin = sin_ref[...]
    for first in range(0, QW, 2 * LANES):
        cols = slice(first, min(first + 2 * LANES, QW))
        both = nn(normed, w_ref[:, cols]) + b_ref[:, cols].astype(F32)
        for at in range(0, both.shape[1], LANES):
            part = turn(both[:, at : at + LANES], cos, sin) * HD**-0.5
            q_ref[:, first + at : first + at + LANES] = part.astype(BF)


def project_q(normed, w, b, cos, sin):
    tokens, width = normed.shape
    return pl.pallas_call(
        project_q_kernel,
        out_shape=jax.ShapeDtypeStruct((tokens, QW), BF),
        compiler_params=params(),
        cost_estimate=cost(4),
        name="project_q",
    )(normed, w, b, cos, sin)


def masked_heads(ref, heads, scratch, rows):
    lane = lane_iota((rows, LANES))
    for slot, h in enumerate(heads):
        pair = ref[0, :, h // 2 * LANES : h // 2 * LANES + LANES]
        keep = (lane >= HD) if h % 2 else (lane < HD)
        scratch[slot * rows : (slot + 1) * rows, :LANES] = jnp.where(keep, pair, jnp.zeros_like(pair))


def swapped(a):
    return jnp.concatenate([a[:, HD:], a[:, :HD]], 1)


def chunks(width):
    return [slice(at, min(at + CHUNK, width)) for at in range(0, width, CHUNK)]


def allowed_pairs(start_ref, first, keys, cols):
    index = first + lax.broadcasted_iota(jnp.int32, (keys, cols.stop - cols.start), 0)
    return (index <= start_ref[0, 1:2, cols]) & (index >= start_ref[0, 0:1, cols])


def gathered(first_ref, second_ref, spot_ref, which, j):
    half = first_ref.shape[0]

    def block(i):
        spot = spot_ref[which, j * GROUP + i]
        one = first_ref[jnp.minimum(spot, half - 1), 0]
        two = second_ref[jnp.maximum(spot - half, 0), 0]
        return jnp.where(jnp.broadcast_to(spot < half, one.shape), one, two)

    return jnp.concatenate([block(i) for i in range(GROUP)], 0)


def forward_kernel(low_ref, me_ref, spot_ref, q_ref, k1_ref, k2_ref, v1_ref, v2_ref, start_ref, out_ref, lse_ref, qa, qb, ma, la, oa, mb, lb, ob, weights):
    rows = q_ref.shape[1]
    stream = pl.program_id(0)
    me = me_ref[0]
    masked_heads(q_ref, SAME, qa, rows)
    masked_heads(q_ref, OTHER, qb, rows)
    for m, l, o in ((ma, la, oa), (mb, lb, ob)):
        m[...] = jnp.full_like(m, NEG)
        l[...] = jnp.zeros_like(l)
        o[...] = jnp.zeros_like(o)
    keys = GROUP * rows

    def step(j, carry):
        key = gathered(k1_ref, k2_ref, spot_ref, 0, j)
        value = gathered(v1_ref, v2_ref, spot_ref, 1, j)
        for swap, q, m, l, o in ((False, qa, ma, la, oa), (True, qb, mb, lb, ob)):
            width = q.shape[0]
            k = swapped(key) if swap else key
            v = swapped(value) if swap else value
            for cols in chunks(width):
                s = jnp.where(allowed_pairs(start_ref, j * keys, keys, cols), nt(k, q[cols]), NEG)
                before = m[:, cols]
                top = jnp.maximum(before, jnp.max(s, axis=0, keepdims=True))
                p = jnp.exp(s - top)
                shrink = jnp.exp(before - top)
                m[:, cols] = top
                l[:, cols] = l[:, cols] * shrink + jnp.sum(p, axis=0, keepdims=True)
                o[:, cols] = o[:, cols] * shrink
                weights[:, cols] = p.astype(BF)
            o[...] += nn(v.T, weights[:, :width])
        return carry

    lax.fori_loop(low_ref[stream], me // GROUP + 1, step, 0)
    lane = lane_iota((rows, LANES))
    parts = {}
    for row, (heads, m, l, o) in enumerate(((SAME, ma, la, oa), (OTHER, mb, lb, ob))):
        total = l[...]
        flat = (o[...] / total).T
        lse_ref[0, row : row + 1, : total.shape[1]] = m[...] + jnp.log(total)
        for slot, h in enumerate(heads):
            parts[h] = flat[slot * rows : (slot + 1) * rows]
    for pair in range(HEADS // 2):
        both = jnp.where(lane < HD, parts[2 * pair], parts[2 * pair + 1])
        out_ref[0, :, pair * LANES : (pair + 1) * LANES] = both.astype(BF)


def attend(q, k_all, v_all, start_rows, low, me, spots):
    streams, rows, width = q.shape
    half = k_all[0].shape[0]
    a, b = len(SAME) * rows, len(OTHER) * rows
    tok = lambda w: pl.BlockSpec((1, rows, w), lambda s, *_: (s, 0, 0))
    two = pl.BlockSpec((1, 2, a), lambda s, *_: (s, 0, 0))
    return pl.pallas_call(
        forward_kernel,
        grid_spec=pltpu.PrefetchScalarGridSpec(
            num_scalar_prefetch=3,
            grid=(streams,),
            in_specs=[tok(width), *[pl.BlockSpec((half, 1, rows, KW), lambda s, *_: (0, s, 0, 0))] * 4, two],
            out_specs=[tok(width), two],
            scratch_shapes=[
                pltpu.VMEM((a, LANES), BF),
                pltpu.VMEM((b, LANES), BF),
                pltpu.VMEM((1, a), F32),
                pltpu.VMEM((1, a), F32),
                pltpu.VMEM((LANES, a), F32),
                pltpu.VMEM((1, b), F32),
                pltpu.VMEM((1, b), F32),
                pltpu.VMEM((LANES, b), F32),
                pltpu.VMEM((GROUP * rows, a), BF),
            ],
        ),
        out_shape=(
            jax.ShapeDtypeStruct((streams, rows, width), BF),
            jax.ShapeDtypeStruct((streams, 2, a), F32),
        ),
        compiler_params=params(),
        cost_estimate=cost(18),
        name="attend",
    )(low, me, spots, q, *k_all, *v_all, start_rows)


def three_parts(column):
    high = column.astype(BF)
    rest = column - high.astype(F32)
    middle = rest.astype(BF)
    return high, middle, (rest - middle.astype(F32)).astype(BF)


def put_column(scratch, at, column, rows):
    lane = lane_iota((rows, LANES))
    out = jnp.zeros((rows, LANES), F32)
    for i, piece in enumerate(three_parts(column)):
        out = jnp.where(lane == i, piece.astype(F32), out)
    scratch[at, LANES:] = out.astype(BF)


def backward_kernel(
    first, low_ref, me_ref, spot_ref, q_ref, k1_ref, k2_ref, v1_ref, v2_ref, start_ref, lse_ref, mixed_ref, grad_ref, cos_ref, sin_ref, dq_ref, dkk_ref,
    dks_ref, dvk_ref, dvs_ref, qa, qb, ga, gb, ta, tb, dk_all, dv_all, weights, grads,
):
    rows = q_ref.shape[1]
    stream = first + pl.program_id(0)
    me = me_ref[0]
    masked_heads(q_ref, SAME, qa, rows)
    masked_heads(q_ref, OTHER, qb, rows)
    masked_heads(grad_ref, SAME, ga, rows)
    masked_heads(grad_ref, OTHER, gb, rows)
    lane = lane_iota((rows, LANES))
    for heads, g in ((SAME, ga), (OTHER, gb)):
        for slot, h in enumerate(heads):
            at = slice(slot * rows, (slot + 1) * rows)
            cols = slice(h // 2 * LANES, h // 2 * LANES + LANES)
            keep = (lane >= HD) if h % 2 else (lane < HD)
            product = grad_ref[0, :, cols].astype(F32) * mixed_ref[0, :, cols].astype(F32)
            delta = jnp.sum(jnp.where(keep, product, 0.0), axis=-1, keepdims=True)
            put_column(g, at, -delta, rows)
    ta[...] = jnp.zeros_like(ta)
    tb[...] = jnp.zeros_like(tb)
    dk_all[...] = jnp.zeros_like(dk_all)
    dv_all[...] = jnp.zeros_like(dv_all)
    keys = GROUP * rows
    ones = (lane_iota((keys, LANES)) < 3).astype(F32).astype(BF)

    def step(j, carry):
        key = gathered(k1_ref, k2_ref, spot_ref, 0, j)
        value = gathered(v1_ref, v2_ref, spot_ref, 1, j)
        grad_keys = []
        grad_values = []
        for row, (q, g, t) in enumerate(((qa, ga, ta), (qb, gb, tb))):
            width = q.shape[0]
            k = swapped(key) if row else key
            v = jnp.concatenate([swapped(value) if row else value, ones], 1)
            for cols in chunks(width):
                s = nt(k, q[cols]) - lse_ref[0, row : row + 1, cols]
                p = jnp.exp(jnp.where(allowed_pairs(start_ref, j * keys, keys, cols), s, NEG))
                weights[:, cols] = p.astype(BF)
                grads[:, cols] = (p * nt(v, g[cols])).astype(BF)
            grad_values.append(nn(weights[:, :width], g[:, :LANES]))
            grad_keys.append(nn(grads[:, :width], q[...]))
            t[...] += nn(k.T, grads[:, :width])
        for out_ref, (same, other) in ((dk_all, grad_keys), (dv_all, grad_values)):
            total = (same + swapped(other)).astype(BF)
            out_ref[pl.ds(j * GROUP, GROUP)] = total.reshape(GROUP, rows, KW)
        return carry

    lax.fori_loop(low_ref[stream], me // GROUP + 1, step, 0)
    half = dkk_ref.shape[0]
    for which, (keep_ref, send_ref, out_ref) in enumerate(((dkk_ref, dks_ref, dk_all), (dvk_ref, dvs_ref, dv_all))):
        for spot in range(half):
            keep_ref[spot, 0] = out_ref[spot_ref[2 + which, spot]]
            send_ref[spot, 0] = out_ref[spot_ref[2 + which, half + spot]]
    parts = {}
    for heads, t in ((SAME, ta), (OTHER, tb)):
        flat = t[...].T
        for slot, h in enumerate(heads):
            parts[h] = flat[slot * rows : (slot + 1) * rows]
    cos = cos_ref[0]
    sin = sin_ref[0]
    for pair in range(HEADS // 2):
        both = jnp.where(lane < HD, parts[2 * pair], parts[2 * pair + 1]) * HD**-0.5
        dq_ref[0, :, pair * LANES : (pair + 1) * LANES] = (both * cos - half_swap(both) * sin).astype(BF)


def attend_back(first, streams, q, k_all, v_all, start_rows, low, me, spots, lse, mixed, grad, cos, sin):
    rows, width = q.shape[1:]
    half = k_all[0].shape[0]
    n = 2 * half
    a, b = len(SAME) * rows, len(OTHER) * rows
    tok = lambda w: pl.BlockSpec((1, rows, w), lambda s, *_: (s + first, 0, 0))
    two = pl.BlockSpec((1, 2, a), lambda s, *_: (s + first, 0, 0))
    key_spec = pl.BlockSpec((n // 2, 1, rows, KW), lambda s, *_: (0, s, 0, 0))
    return pl.pallas_call(
        functools.partial(backward_kernel, first),
        grid_spec=pltpu.PrefetchScalarGridSpec(
            num_scalar_prefetch=3,
            grid=(streams,),
            in_specs=[
                tok(width),
                *[pl.BlockSpec((half, 1, rows, KW), lambda s, *_: (0, s + first, 0, 0))] * 4,
                two,
                two,
                tok(width),
                tok(width),
                tok(LANES),
                tok(LANES),
            ],
            out_specs=[pl.BlockSpec((1, rows, width), lambda s, *_: (s, 0, 0)), *[key_spec] * 4],
            scratch_shapes=[
                pltpu.VMEM((a, LANES), BF),
                pltpu.VMEM((b, LANES), BF),
                pltpu.VMEM((a, 2 * LANES), BF),
                pltpu.VMEM((b, 2 * LANES), BF),
                pltpu.VMEM((LANES, a), F32),
                pltpu.VMEM((LANES, b), F32),
                *[pltpu.VMEM((n, rows, KW), BF)] * 2,
                *[pltpu.VMEM((GROUP * rows, a), BF)] * 2,
            ],
        ),
        out_shape=(
            jax.ShapeDtypeStruct((streams, rows, width), BF),
            *[jax.ShapeDtypeStruct((n // 2, streams, rows, KW), BF)] * 4,
        ),
        compiler_params=params(),
        cost_estimate=cost(8 * streams),
        name="attend_back",
    )(low, me, spots, q, *k_all, *v_all, start_rows, lse, mixed, grad, cos, sin)


TILE = 256


def mlp_kernel(
    valid, mine_ref, theirs_ref, sm_ref, st_ref, order_ref, wg_ref, wu_ref, wd_ref, om_ref, ot_ref, bm_ref, bt_ref,
    td_ref, gk_ref, gs_ref, uk_ref, us_ref, n_ref, s_ref, turned_ref,
):
    rows = mine_ref.shape[0]
    step = pl.program_id(0)
    sums = (om_ref, ot_ref, bm_ref, bt_ref)

    @pl.when(step == 0)
    def _():
        n_ref[:rows] = mine_ref[...]
        n_ref[rows:] = theirs_ref[...]
        s_ref[:rows] = sm_ref[...]
        s_ref[rows:] = st_ref[...]
        turned_ref[...] = nt(order_ref[...], n_ref[...]).astype(BF)
        for ref in sums:
            ref[...] = jnp.zeros_like(ref)

    normed = n_ref[...]
    seed = s_ref[...]
    left = valid - step * TILE
    inside = lambda w, dim: jnp.where(lax.broadcasted_iota(jnp.int32, w.shape, dim) < left, w, jnp.zeros_like(w))
    wg, wu, wd = inside(wg_ref[...], 1), inside(wu_ref[...], 1), inside(wd_ref[...], 0)
    gate = nn(normed, wg)
    up = nn(normed, wu)
    grad = nt(seed, wd)
    sig = 1.0 / (1.0 + jnp.exp(-gate))
    silu = gate * sig
    active = (silu * up).astype(BF)
    grad_up = (grad * silu).astype(BF)
    grad_gate = (grad * up * (sig * (1.0 + gate * (1.0 - sig)))).astype(BF)
    td_ref[...] = tn(active, seed).astype(BF)
    quarter = gk_ref.shape[0] // 2
    rows_of = lambda a, i: a[i * quarter : (i + 1) * quarter]
    for grad_pre, keep, send, quarters in ((grad_gate, gk_ref, gs_ref, (0, 1, 2, 3)), (grad_up, uk_ref, us_ref, (0, 2, 1, 3))):
        term = nn(turned_ref[...], grad_pre).astype(BF)
        for i in range(2):
            keep[i * quarter : (i + 1) * quarter] = rows_of(term, quarters[i])
            send[i * quarter : (i + 1) * quarter] = rows_of(term, quarters[2 + i])
    out = nn(active, wd)
    back = nt(grad_gate, wg) + nt(grad_up, wu)
    for ref, part in zip(sums, (out[:rows], out[rows:], back[:rows], back[rows:])):
        ref[...] += part


def fixed(*shape):
    return pl.BlockSpec(shape, lambda *_: (0,) * len(shape))


def shaped(dtype, *dims):
    return jax.ShapeDtypeStruct(dims, dtype)


def mlp(mine, theirs, seed_mine, seed_theirs, order, w_gate, w_up, w_d):
    rows, width = mine.shape
    half = w_gate.shape[1]
    cols = lambda size: pl.BlockSpec((size, TILE), lambda i: (0, i))
    down = pl.BlockSpec((TILE, width), lambda i: (i, 0))
    part = fixed(rows, width)
    return pl.pallas_call(
        functools.partial(mlp_kernel, half),
        grid=(pl.cdiv(half, TILE),),
        in_specs=[part] * 4 + [fixed(width, width)] + [cols(width)] * 2 + [down],
        out_specs=[part] * 4 + [down] + [cols(width // 2)] * 4,
        out_shape=[shaped(F32, rows, width)] * 4 + [shaped(BF, half, width)] + [shaped(BF, width // 2, half)] * 4,
        scratch_shapes=[pltpu.VMEM((2 * rows, width), BF)] * 2 + [pltpu.VMEM((width, 2 * rows), BF)],
        compiler_params=params(),
        cost_estimate=cost(40),
        name="mlp",
    )(mine, theirs, seed_mine, seed_theirs, order, w_gate, w_up, w_d)


def middle_kernel(bm_ref, bt_ref, middle_ref, seed_ref, g_ref, w_ref, gm_ref, gb_ref, gx_ref, gain_ref):
    @pl.when(pl.program_id(0) == 0)
    def _():
        gain_ref[...] = jnp.zeros_like(gain_ref)

    grad = bm_ref[...] + bt_ref[...]
    middle = middle_ref[...]
    inv = lax.rsqrt(jnp.mean(middle * middle, axis=-1, keepdims=True) + epsilon)
    unit = middle * inv
    scaled = grad * g_ref[...].astype(F32)
    grad_middle = seed_ref[...].astype(F32) + inv * (scaled - unit * jnp.mean(scaled * unit, axis=-1, keepdims=True))
    gm_ref[...] = grad_middle
    branch = grad_middle.astype(BF)
    gb_ref[...] = branch
    gx_ref[...] = nt(branch, w_ref[...]).astype(BF)
    gain_ref[...] += jnp.sum(grad * unit, axis=0, keepdims=True)


def middle_back(mine, theirs, middle, seed, gain, w_out):
    tokens, width = middle.shape
    rows = tokens // 4
    part = pl.BlockSpec((rows, width), lambda i: (i, 0))
    return pl.pallas_call(
        middle_kernel,
        grid=(4,),
        in_specs=[part] * 4 + [fixed(1, width), fixed(width, width)],
        out_specs=[part] * 3 + [fixed(1, width)],
        out_shape=[shaped(F32, tokens, width), shaped(BF, tokens, width), shaped(BF, tokens, width), shaped(F32, 1, width)],
        compiler_params=params(),
        cost_estimate=cost(5),
        name="middle_back",
    )(mine, theirs, middle, seed, gain, w_out)


def attention_terms_kernel(core_ref, normed_ref, mixed_ref, gq_ref, gb_ref, order_ref, sent_ref, kept_ref):
    first = core_ref[0] == 0
    order = order_ref[...]
    pick = lambda flag, a, b: jnp.where(jnp.broadcast_to(flag, a.shape), a[...], b[...])
    for out_ref, flag in ((sent_ref, first), (kept_ref, jnp.logical_not(first))):
        left = nt(order, pick(flag, normed_ref, mixed_ref)).astype(BF)
        out_ref[...] = nn(left, pick(flag, gq_ref, gb_ref)).astype(BF)


def attention_terms(core, normed, mixed, grad_q, grad_branch, order):
    width = normed.shape[1]
    whole = pl.BlockSpec(memory_space=pltpu.VMEM)
    return pl.pallas_call(
        attention_terms_kernel,
        in_specs=[pl.BlockSpec(memory_space=pltpu.SMEM)] + [whole] * 5,
        out_specs=[whole] * 2,
        out_shape=[shaped(BF, width, width)] * 2,
        compiler_params=params(),
        cost_estimate=cost(5),
        name="attention_terms",
    )(core, normed, mixed, grad_q, grad_branch, order)


def last_kernel(gkv_ref, gq_ref, w_ref, x_ref, g_ref, cos_ref, sin_ref, nt_ref, gm_ref, gain_ref, gi_ref, term_ref,
                sums_ref):
    grads = gkv_ref[...]
    keys = grads[:, :KW].astype(F32)
    keys = (keys * cos_ref[...] - half_swap(keys) * sin_ref[...]).astype(BF)
    grad_kv = jnp.concatenate([keys, grads[:, KW:]], 1)
    term_ref[...] = nn(nt_ref[...], grad_kv).astype(BF)
    grad = nt(gq_ref[...], w_ref[:, :QW]) + nt(grad_kv, w_ref[:, QW:])
    x = x_ref[...].astype(F32)
    inv = lax.rsqrt(jnp.mean(x * x, axis=-1, keepdims=True) + epsilon)
    unit = x * inv
    scaled = grad * g_ref[...].astype(F32)
    gi_ref[...] = gm_ref[...] + inv * (scaled - unit * jnp.mean(scaled * unit, axis=-1, keepdims=True))
    over = lambda a: jnp.sum(a.astype(F32), axis=0, keepdims=True)
    at = 0
    for row in (over(gq_ref[...]), over(grad_kv), over(grad * unit), gain_ref[...]):
        sums_ref[:, at : at + row.shape[1]] = row
        at += row.shape[1]


def last_back(grads, grad_q, w_qkv, x, gain, cos, sin, normed_t, grad_middle, gain_mlp_part):
    tokens, width = x.shape
    return pl.pallas_call(
        last_kernel,
        out_shape=[
            shaped(F32, tokens, width),
            shaped(BF, width, 2 * KW),
            shaped(F32, 1, QW + 2 * KW + 2 * width),
        ],
        compiler_params=params(),
        cost_estimate=cost(6),
        name="last_back",
    )(grads, grad_q, w_qkv, x, gain, cos, sin, normed_t, grad_middle, gain_mlp_part)


def after(a, *others):
    return lax.optimization_barrier((a, others))[0]


class Order:
    def __init__(self, token):
        self.token = token

    def enter(self, inputs):
        return lax.optimization_barrier((inputs, self.token))[0]

    def __call__(self, step, *inputs):
        self.token = step(*self.enter(inputs))
        return self.token


def other_core(a):
    return lax.ppermute(a, "dp", [(0, 1), (1, 0)])


def pair_up(a, axis, step):
    return lax.ppermute(a, axis, [(i, i ^ step) for i in range(lax.axis_size(axis))])


def total(terms):
    return functools.reduce(lambda a, b: a + b, [a.astype(F32) for a in terms]).astype(BF)


def add(a, b):
    return total((a, b))


Z, Y, X = SEQ
X_FIRST = ((X, 1), (Y, 1), (Z, 1), (Z, 2))
Y_FIRST = ((Y, 1), (X, 1), (Z, 1), (Z, 2))
Z_FIRST = ((Z, 1), (Y, 1), (X, 1), (Z, 2))
KEY_GATHER = ((Y, 1), (X, 1), (Z, 2), (Z, 1))
VALUE_GATHER = X_FIRST


def halving():
    return [lax.axis_size(axis) for axis in SEQ] == [4, 2, 2]


def my_bit(axis, step):
    return (lax.axis_index(axis) // step) % 2


def device_at(order, spot, relative):
    place = 0
    weight = {(X, 1): 1, (Y, 1): 2, (Z, 1): 4, (Z, 2): 8}
    for i, (axis, step) in enumerate(order):
        bit = (spot >> (len(order) - 1 - i)) & 1
        if relative:
            bit = bit ^ my_bit(axis, step)
        place = place + bit * weight[axis, step]
    return place


def spots_of_devices(order):
    n = lax.axis_size(SEQ)
    if not halving():
        return jnp.arange(n)
    spots = jnp.arange(n)
    return jnp.sum(jnp.where(device_at(order, spots, True)[:, None] == spots[None, :], spots[:, None], 0), 0)


def devices_at_spots(order):
    n = lax.axis_size(SEQ)
    return device_at(order, jnp.arange(n), True) if halving() else jnp.arange(n)


def row_order(order, width):
    n = lax.axis_size(SEQ)
    row = jnp.arange(width)
    source = row
    if halving():
        source = device_at(order, row // (width // n), True) * (width // n) + row % (width // n)
    return (source[:, None] == jnp.arange(width)[None, :]).astype(BF)


class Halving:
    def __init__(self, steps, arrays, rows, order=None, send=None):
        self.steps = list(steps)
        self.arrays = list(arrays)
        self.firsts = [0] * len(self.arrays)
        self.rows = rows
        if send is None:
            self.go(order)
        else:
            self.move(send)

    def halves(self):
        return 0, self.rows

    def move(self, send):
        self.arrays.append(pair_up(send, *self.steps.pop(0)))
        self.firsts.append(0)

    def sum(self, offset):
        cut = lambda a, first: lax.dynamic_slice_in_dim(a, first + offset, self.rows, 0)
        return total([cut(a, first) for a, first in zip(self.arrays, self.firsts)])

    def go(self, order):
        self.arrays = list(order.enter(self.arrays))
        if not self.steps:
            order.token = self.sum(0)
            return order.token
        self.rows //= 2
        kept, sent = self.halves()
        send = order.token = self.sum(sent)
        self.firsts = [first + kept for first in self.firsts]
        self.move(send)


class PlacedHalving(Halving):
    def halves(self):
        bit = my_bit(*self.steps[0])
        return bit * self.rows, (1 - bit) * self.rows


class PairHalving:
    def __init__(self, a_keep, a_send, b_keep, b_send, orders=(X_FIRST, Y_FIRST)):
        rows = a_keep.shape[0]
        self.pair = [
            Halving(orders[0][:2], [a_keep], rows, send=a_send),
            Halving(orders[1][:2], [b_keep], rows, send=b_send),
        ]
        self.last = orders[0][2:]
        self.count = 0

    def go(self, order, which=None):
        if which is not None:
            return self.pair[which].go(order)
        self.count += 1
        a, b = self.pair
        if self.count == 1:
            a.arrays, b.arrays = order.enter((list(a.arrays), list(b.arrays)))
            both = order.token = jnp.concatenate([a.sum(0), b.sum(0)], 1)
            half = both.shape[0] // 2
            self.rest = Halving(self.last, [both], half, send=both[half:])
        else:
            return self.rest.go(order)


def reduce_rows(a):
    return lax.psum_scatter(a, SEQ, scatter_dimension=0, tiled=True)


class Doubling:
    def __init__(self, order, a):
        self.steps = list(reversed(order))
        self.all = a[None]
        self.got = pair_up(self.all, *self.steps.pop(0))

    def go(self, order):
        if not self.steps:
            return self.all, self.got
        self.all = order(lambda a, b: jnp.concatenate([a, b], 0), self.all, self.got)
        self.got = pair_up(self.all, *self.steps.pop(0))


def to_owner(a, order):
    n = lax.axis_size(SEQ)
    holder = [device_at(order, spot, False) for spot in range(n)] if halving() else list(range(n))
    pairs = [(holder[spot] * 2 + core, core * n + spot) for spot in range(n) for core in range(2)]
    return lax.ppermute(a, (*SEQ, "dp"), pairs)


def sum_over_all(a):
    for axis in ("dp", *SEQ[::-1]):
        size = lax.axis_size(axis)
        step = 1
        while step < size:
            a = a + lax.ppermute(a, axis, [(i, i ^ step) for i in range(size)])
            step *= 2
    return a


def layout(lengths, offset, row_count):
    places = offset + jnp.arange(row_count, dtype=jnp.int32)
    slots = jnp.arange(lengths.shape[1])
    ends = jnp.sum(jnp.where(slots[:, None] <= slots[None, :], lengths[:, :, None], 0), axis=1)
    after = (places[None, :, None] >= ends[:, None, :]).astype(jnp.int32)
    begins = jnp.sum(after * lengths[:, None, :], axis=-1, dtype=jnp.int32)
    return (places, begins, places[None, :] < ends[:, -1:])


def shards(inputs, lengths, w_qkv, b_qkv, g_attn, w_out, g_mlp, w_gate_up, w_down, cotangent):
    streams, length, width = inputs.shape
    tokens = streams * length
    n = 1
    for axis in SEQ:
        n *= lax.axis_size(axis)
    me = lax.axis_index(SEQ)
    core = lax.axis_index("dp")
    offset = me * length
    places, begins, valid = layout(lengths, offset, length)
    frequency = rope_base ** (-(jnp.arange(HD // 2, dtype=F32) * (2.0 / HD)))
    lane_frequency = jnp.tile(frequency, LANES // (HD // 2))
    sign = jnp.where(jnp.arange(LANES) % HD < HD // 2, -1.0, 1.0)
    angle = (places[None, :] - begins).astype(F32).reshape(tokens, 1) * lane_frequency
    cos = jnp.cos(angle)
    sin = jnp.sin(angle) * sign

    x = inputs.reshape(tokens, width)
    small = jnp.concatenate([b_qkv, g_attn]).reshape(1, -1)
    normed, k, v = project_kv(x, w_qkv, small, cos, sin)
    k, v = k.reshape(streams, length, KW), v.reshape(streams, length, KW)
    half = FF // 2

    def small_inputs(begins):
        start_rows = jnp.stack(
            [
                jnp.tile(begins, (1, len(SAME))),
                jnp.tile(jnp.broadcast_to(places[None], begins.shape), (1, len(SAME))),
            ],
            1,
        )
        spots = jnp.stack(
            [*map(spots_of_devices, (KEY_GATHER, VALUE_GATHER)), *map(devices_at_spots, (Y_FIRST, X_FIRST))]
        ).astype(jnp.int32)
        return start_rows, spots, row_order(X_FIRST, width)

    cut_cols = lambda w, first: lax.dynamic_slice_in_dim(w, first + core * half, half, 1)
    cut_rows = lambda w: lax.dynamic_slice_in_dim(w, core * half, half, 0)
    fast = halving()
    order = Order(k)
    if fast:
        keys = Doubling(KEY_GATHER, k)
        values = Doubling(VALUE_GATHER, v)
        q = order(project_q, normed, w_qkv, small, cos, sin)
        keys.go(order), values.go(order)
        seed = order(lambda c: (c * valid[..., None].astype(BF)).reshape(tokens, width), cotangent)
        w_gate = order(functools.partial(cut_cols, first=0), w_gate_up)
        keys.go(order), values.go(order)
        w_up = order(functools.partial(cut_cols, first=FF), w_gate_up)
        w_d = order(cut_rows, w_down)
        keys.go(order), values.go(order)
        seed_theirs = other_core(seed)
        start_rows, spots, order_x = order(small_inputs, begins)
        normed_t = order(lambda a, b: nt(a, b).astype(BF), order_x, normed)
        k_all, v_all = keys.go(order), values.go(order)
    else:
        in_halves = lambda a: (a[: n // 2], a[n // 2 :])
        k_all, v_all = [in_halves(lax.all_gather(a, SEQ, axis=0)) for a in (k, v)]
        q = project_q(normed, w_qkv, small, cos, sin)
        seed = (cotangent * valid[..., None].astype(BF)).reshape(tokens, width)
        seed_theirs = other_core(seed)
        w_gate, w_up, w_d = cut_cols(w_gate_up, 0), cut_cols(w_gate_up, FF), cut_rows(w_down)
        start_rows, spots, order_x = small_inputs(begins)
        normed_t = nt(order_x, normed).astype(BF)
    low = begins[:, 0] // (GROUP * length)
    me_1 = jnp.reshape(me, (1,)).astype(jnp.int32)
    q = q.reshape(streams, length, QW)
    mixed, lse = attend(q, k_all, v_all, start_rows, low, me_1, spots)
    mixed_flat = mixed.reshape(tokens, QW)
    middle = x.astype(F32) + nn(mixed_flat, w_out)
    inv_mlp = lax.rsqrt(jnp.mean(middle * middle, axis=-1, keepdims=True) + epsilon)
    unit_mlp = middle * inv_mlp
    gain_mlp = g_mlp.astype(F32)
    normed_mlp = (unit_mlp * gain_mlp).astype(BF)
    normed_theirs = other_core(normed_mlp)
    out_mine, out_theirs, back_mine, back_theirs, term_down, keep_gate, send_gate, keep_up, send_up = mlp(
        normed_mlp, normed_theirs, seed, seed_theirs, order_x, w_gate, w_up, w_d
    )
    order = Order(back_mine)
    back_theirs = other_core(back_theirs)
    out_theirs = other_core(out_theirs)
    if fast:
        gate_up = PairHalving(keep_gate, send_gate, keep_up, send_up)
        down = PlacedHalving(Z_FIRST, [term_down], half, order)

    grad_middle, grad_branch, grad_mixed, gain_mlp_part = order(
        middle_back, back_mine, back_theirs, middle, seed, g_mlp.reshape(1, -1), w_out
    )
    grad_mixed = grad_mixed.reshape(streams, length, QW)

    cos_s = cos.reshape(streams, length, LANES)
    sin_s = sin.reshape(streams, length, LANES)
    back = lambda first, count: attend_back(
        first, count, q, k_all, v_all, start_rows, low, me_1, spots, lse, mixed, grad_mixed, cos_s, sin_s
    )

    core_1 = jnp.reshape(core, (1,)).astype(jnp.int32)
    gain_attn = g_attn.reshape(1, -1)

    def finish(mine, theirs, middle):
        return (middle + mine + theirs).astype(BF)

    def both_cores(mine, dim):
        theirs = other_core(mine)
        first = jnp.where(core == 0, mine, theirs)
        second = jnp.where(core == 0, theirs, mine)
        return jnp.concatenate([first, second], dim).astype(F32)

    if fast:
        per = streams // PARTS
        rows = (n // 2) * per * length
        grads_q = []
        at = {"down": down, "gu": gate_up}
        value = {}

        def back_step(which):
            grad_q, *grads = attend_back(
                per * which, per, q, k_all, v_all, start_rows, low, order.enter(me_1), spots, lse, mixed, grad_mixed, cos_s, sin_s
            )
            order.token = grad_q
            grads_q.append(grad_q.reshape(per * length, QW))
            at["keys", which] = PairHalving(*[g.reshape(rows, KW) for g in grads], orders=(Y_FIRST, X_FIRST))

        def terms_step():
            value["q"] = jnp.concatenate(grads_q, 0)
            sent, kept = order(attention_terms, core_1, normed, mixed_flat, value["q"], grad_branch, order_x)
            value["attn"] = kept, other_core(sent)

        def attn_step():
            value["attn"] = order(add, *value["attn"])
            at["attn"] = Halving(X_FIRST, [value["attn"]], width, order)

        def last_step():
            grads = jnp.concatenate([value[f"keys:{i}"] for i in range(PARTS)], 0)
            value["input"], term, sums = order(
                last_back, grads, value["q"], w_qkv, x, gain_attn, cos, sin, normed_t,
                grad_middle, gain_mlp_part,
            )
            block = width // n
            extra = jnp.pad(sums.astype(BF).reshape(-1, LANES), ((0, block - sums.size // LANES), (0, 0)))
            term = order(lambda t, e: jnp.concatenate([t, jnp.tile(e, (n, 1))], 1), term, extra)
            at["kv"] = Halving(X_FIRST, [term], width, order)

        def finish_step():
            value["output"] = order(finish, out_mine, out_theirs, middle)

        steps = {"ab": back_step, "terms": terms_step, "attn0": attn_step, "last": last_step}
        steps["finish"] = finish_step
        for name in PLAN:
            head, *rest = name.split(":")
            rest = [int(r) for r in rest]
            if head in steps:
                steps[head](*rest)
            elif head == "gu":
                value[name] = gate_up.go(order, *rest)
            elif head == "keys":
                value[name] = at[head, rest[0]].go(order, *rest[1:])
            else:
                value[name] = at[name].go(order)
        output, grad_input = value["output"], value["input"]
        rows_gate, rows_up = value["gu"][:, :half], value["gu"][:, half:]
        rows_down, rows_attn, rows_kv = value["down"], value["attn"], value["kv"]
        rows_kv = add(rows_kv, other_core(rows_kv))
        sums = rows_kv[:, 2 * KW :].astype(F32).reshape(-1)
    else:
        grad_q, *grads = back(0, streams)
        grad_q = grad_q.reshape(tokens, QW)
        sent, kept = attention_terms(core_1, normed, mixed_flat, grad_q, grad_branch, order_x)
        rows_attn = reduce_rows(add(kept, other_core(sent)))
        output = finish(out_mine, out_theirs, middle)
        grad_k, grad_v = [reduce_rows(jnp.concatenate(g, 0).reshape(n * tokens, KW)) for g in (grads[:2], grads[2:])]
        grad_kv = jnp.concatenate([grad_k, grad_v], 1)
        grad_input, term, sums = last_back(
            grad_kv, grad_q, w_qkv, x, gain_attn, cos, sin, normed_t, grad_middle,
            gain_mlp_part,
        )
        rows_kv = reduce_rows(term)
        rows_kv = add(rows_kv, other_core(rows_kv))
        sums = sum_over_all(sums.reshape(-1, LANES)).reshape(-1)
        rows_gate = reduce_rows(jnp.concatenate([keep_gate, send_gate], 0))
        cut_up = keep_up.shape[0] // 2
        rows_up = reduce_rows(jnp.concatenate([keep_up[:cut_up], send_up[:cut_up], keep_up[cut_up:], send_up[cut_up:]], 0))
        rows_down = reduce_rows(term_down)

    rows_down = to_owner(rows_down, Z_FIRST)
    rows_attn = both_cores(rows_attn, 1)
    rows_out, rows_q = rows_attn[:, :width], rows_attn[:, width:]
    small = [QW + 2 * KW, QW + 2 * KW + width, QW + 2 * KW + 2 * width]
    bias_grad, gain_attn_grad, gain_mlp_grad, _ = jnp.split(sums, small)
    return (
        output.reshape(streams, length, width),
        grad_input.reshape(streams, length, width),
        jnp.concatenate([rows_q, rows_kv[:, : 2 * KW].astype(F32)], 1),
        bias_grad,
        gain_attn_grad,
        rows_out,
        gain_mlp_grad,
        jnp.concatenate([both_cores(rows_gate, 1), both_cores(rows_up, 1)], 1),
        both_cores(rows_down, 0),
    )


PARTS = 1
PLAN = (
    "ab:0", "terms", "gu:0", "gu:1", "keys:0:0", "keys:0:1", "keys:0", "down", "attn0", "keys:0", "gu",
    "finish", "keys:0", "down", "last", "attn", "gu", "kv", "attn", "down", "kv", "attn", "kv", "gu", "down",
    "attn", "kv",
)


def solution(mesh):
    n = mesh.shape["seq"]
    sizes = {16: (4, 2, 2), 64: (4, 4, 4)}.get(n, (n, 1, 1))
    fine = Mesh(np.asarray(mesh.devices).reshape(*sizes, mesh.shape["dp"]), (*SEQ, "dp"))
    in_specs = (P("dp", SEQ, None), P("dp", None), P(), P(), P(), P(), P(), P(), P(), P("dp", SEQ, None))
    out_specs = (
        P("dp", SEQ, None), P("dp", SEQ, None), P(SEQ, None), P(), P(), P(SEQ, None), P(), P(SEQ, None), P(SEQ, None),
    )
    return jax.shard_map(shards, mesh=fine, in_specs=in_specs, out_specs=out_specs, check_vma=False)
```

```python
import functools

import jax
import jax.numpy as jnp
import numpy as np
from jax import lax
from jax.experimental import pallas as pl
from jax.experimental.pallas import tpu as pltpu
from jax.sharding import Mesh
from jax.sharding import PartitionSpec as P

HEADS = 14
KVH = 2
HD = 64
FF = 4864
QW = HEADS * HD
KW = KVH * HD
LANES = 128
GROUP = 8
CHUNK = 256
NEG = -1e30
epsilon = 1e-06
rope_base = 1000000.0
BF = jnp.bfloat16
F32 = jnp.float32
SEQ = ("az", "ay", "ax")

SAME = [h for h in range(HEADS) if h % 2 == h // (HEADS // KVH)]
OTHER = [h for h in range(HEADS) if h % 2 != h // (HEADS // KVH)]


def nt(a, b):
    return lax.dot_general(a, b, (((1,), (1,)), ((), ())), preferred_element_type=F32)


def tn(a, b):
    return lax.dot_general(a, b, (((0,), (0,)), ((), ())), preferred_element_type=F32)


def nn(a, b):
    return lax.dot_general(a, b, (((1,), (0,)), ((), ())), preferred_element_type=F32)


def lane_iota(shape):
    return lax.broadcasted_iota(jnp.int32, shape, len(shape) - 1)


def half_swap(tile):
    low = lane_iota(tile.shape) % HD < HD // 2
    return jnp.where(low, pltpu.roll(tile, LANES - HD // 2, 1), pltpu.roll(tile, HD // 2, 1))


def cost(us):
    return pl.CostEstimate(flops=int(us * 1e6 * 90), bytes_accessed=1 << 16, transcendentals=0)


def params(limit=56):
    return pltpu.CompilerParams(vmem_limit_bytes=limit << 20)


def turn(part, cos, sin):
    return part * cos + half_swap(part) * sin


def project_kv_kernel(x_ref, w_ref, small_ref, cos_ref, sin_ref, normed_ref, k_ref, v_ref):
    step = pl.program_id(0)

    @pl.when(step == 0)
    def _():
        x = x_ref[...].astype(F32)
        inv = lax.rsqrt(jnp.mean(x * x, axis=-1, keepdims=True) + epsilon)
        normed_ref[...] = (x * inv * small_ref[:, QW + 2 * KW :].astype(F32)).astype(BF)

    at = pl.multiple_of(QW + step * KW, LANES)
    part = nn(normed_ref[...], w_ref[...]) + small_ref[:, pl.ds(at, KW)].astype(F32)

    @pl.when(step == 0)
    def _():
        k_ref[...] = turn(part, cos_ref[...], sin_ref[...]).astype(BF)

    @pl.when(step == 1)
    def _():
        v_ref[...] = part.astype(BF)


def project_kv(x, w, small, cos, sin):
    tokens, width = x.shape
    fixed = lambda *shape: pl.BlockSpec(shape, lambda i: (0, 0))
    return pl.pallas_call(
        project_kv_kernel,
        grid=(2,),
        in_specs=[
            fixed(tokens, width),
            pl.BlockSpec((width, KW), lambda i: (0, QW // KW + i)),
            fixed(*small.shape),
            fixed(tokens, LANES),
            fixed(tokens, LANES),
        ],
        out_specs=[fixed(tokens, width), fixed(tokens, KW), fixed(tokens, KW)],
        out_shape=(
            jax.ShapeDtypeStruct((tokens, width), BF),
            jax.ShapeDtypeStruct((tokens, KW), BF),
            jax.ShapeDtypeStruct((tokens, KW), BF),
        ),
        compiler_params=params(),
        cost_estimate=cost(3),
        name="project_kv",
    )(x, w, small, cos, sin)


def project_q_kernel(normed_ref, w_ref, b_ref, cos_ref, sin_ref, q_ref):
    normed = normed_ref[...]
    cos = cos_ref[...]
    sin = sin_ref[...]
    for first in range(0, QW, 2 * LANES):
        cols = slice(first, min(first + 2 * LANES, QW))
        both = nn(normed, w_ref[:, cols]) + b_ref[:, cols].astype(F32)
        for at in range(0, both.shape[1], LANES):
            part = turn(both[:, at : at + LANES], cos, sin) * HD**-0.5
            q_ref[:, first + at : first + at + LANES] = part.astype(BF)


def project_q(normed, w, b, cos, sin):
    tokens, width = normed.shape
    return pl.pallas_call(
        project_q_kernel,
        out_shape=jax.ShapeDtypeStruct((tokens, QW), BF),
        compiler_params=params(),
        cost_estimate=cost(4),
        name="project_q",
    )(normed, w, b, cos, sin)


def masked_heads(ref, heads, scratch, rows):
    lane = lane_iota((rows, LANES))
    for slot, h in enumerate(heads):
        pair = ref[0, :, h // 2 * LANES : h // 2 * LANES + LANES]
        keep = (lane >= HD) if h % 2 else (lane < HD)
        scratch[slot * rows : (slot + 1) * rows, :LANES] = jnp.where(keep, pair, jnp.zeros_like(pair))


def swapped(a):
    return jnp.concatenate([a[:, HD:], a[:, :HD]], 1)


def chunks(width):
    return [slice(at, min(at + CHUNK, width)) for at in range(0, width, CHUNK)]


def allowed_pairs(start_ref, first, keys, cols):
    index = first + lax.broadcasted_iota(jnp.int32, (keys, cols.stop - cols.start), 0)
    return (index <= start_ref[0, 1:2, cols]) & (index >= start_ref[0, 0:1, cols])


def gathered(first_ref, second_ref, spot_ref, which, j):
    half = first_ref.shape[0]

    def block(i):
        spot = spot_ref[which, j * GROUP + i]
        one = first_ref[jnp.minimum(spot, half - 1), 0]
        two = second_ref[jnp.maximum(spot - half, 0), 0]
        return jnp.where(jnp.broadcast_to(spot < half, one.shape), one, two)

    return jnp.concatenate([block(i) for i in range(GROUP)], 0)


def forward_kernel(low_ref, me_ref, spot_ref, q_ref, k1_ref, k2_ref, v1_ref, v2_ref, start_ref, out_ref, lse_ref, qa, qb, ma, la, oa, mb, lb, ob, weights):
    rows = q_ref.shape[1]
    stream = pl.program_id(0)
    me = me_ref[0]
    masked_heads(q_ref, SAME, qa, rows)
    masked_heads(q_ref, OTHER, qb, rows)
    for m, l, o in ((ma, la, oa), (mb, lb, ob)):
        m[...] = jnp.full_like(m, NEG)
        l[...] = jnp.zeros_like(l)
        o[...] = jnp.zeros_like(o)
    keys = GROUP * rows

    def step(j, carry):
        key = gathered(k1_ref, k2_ref, spot_ref, 0, j)
        value = gathered(v1_ref, v2_ref, spot_ref, 1, j)
        for swap, q, m, l, o in ((False, qa, ma, la, oa), (True, qb, mb, lb, ob)):
            width = q.shape[0]
            k = swapped(key) if swap else key
            v = swapped(value) if swap else value
            for cols in chunks(width):
                s = jnp.where(allowed_pairs(start_ref, j * keys, keys, cols), nt(k, q[cols]), NEG)
                before = m[:, cols]
                top = jnp.maximum(before, jnp.max(s, axis=0, keepdims=True))
                p = jnp.exp(s - top)
                shrink = jnp.exp(before - top)
                m[:, cols] = top
                l[:, cols] = l[:, cols] * shrink + jnp.sum(p, axis=0, keepdims=True)
                o[:, cols] = o[:, cols] * shrink
                weights[:, cols] = p.astype(BF)
            o[...] += nn(v.T, weights[:, :width])
        return carry

    lax.fori_loop(low_ref[stream], me // GROUP + 1, step, 0)
    lane = lane_iota((rows, LANES))
    parts = {}
    for row, (heads, m, l, o) in enumerate(((SAME, ma, la, oa), (OTHER, mb, lb, ob))):
        total = l[...]
        flat = (o[...] / total).T
        lse_ref[0, row : row + 1, : total.shape[1]] = m[...] + jnp.log(total)
        for slot, h in enumerate(heads):
            parts[h] = flat[slot * rows : (slot + 1) * rows]
    for pair in range(HEADS // 2):
        both = jnp.where(lane < HD, parts[2 * pair], parts[2 * pair + 1])
        out_ref[0, :, pair * LANES : (pair + 1) * LANES] = both.astype(BF)


def attend(q, k_all, v_all, start_rows, low, me, spots):
    streams, rows, width = q.shape
    half = k_all[0].shape[0]
    a, b = len(SAME) * rows, len(OTHER) * rows
    tok = lambda w: pl.BlockSpec((1, rows, w), lambda s, *_: (s, 0, 0))
    two = pl.BlockSpec((1, 2, a), lambda s, *_: (s, 0, 0))
    return pl.pallas_call(
        forward_kernel,
        grid_spec=pltpu.PrefetchScalarGridSpec(
            num_scalar_prefetch=3,
            grid=(streams,),
            in_specs=[tok(width), *[pl.BlockSpec((half, 1, rows, KW), lambda s, *_: (0, s, 0, 0))] * 4, two],
            out_specs=[tok(width), two],
            scratch_shapes=[
                pltpu.VMEM((a, LANES), BF),
                pltpu.VMEM((b, LANES), BF),
                pltpu.VMEM((1, a), F32),
                pltpu.VMEM((1, a), F32),
                pltpu.VMEM((LANES, a), F32),
                pltpu.VMEM((1, b), F32),
                pltpu.VMEM((1, b), F32),
                pltpu.VMEM((LANES, b), F32),
                pltpu.VMEM((GROUP * rows, a), BF),
            ],
        ),
        out_shape=(
            jax.ShapeDtypeStruct((streams, rows, width), BF),
            jax.ShapeDtypeStruct((streams, 2, a), F32),
        ),
        compiler_params=params(),
        cost_estimate=cost(18),
        name="attend",
    )(low, me, spots, q, *k_all, *v_all, start_rows)


def three_parts(column):
    high = column.astype(BF)
    rest = column - high.astype(F32)
    middle = rest.astype(BF)
    return high, middle, (rest - middle.astype(F32)).astype(BF)


def put_column(scratch, at, column, rows):
    lane = lane_iota((rows, LANES))
    out = jnp.zeros((rows, LANES), F32)
    for i, piece in enumerate(three_parts(column)):
        out = jnp.where(lane == i, piece.astype(F32), out)
    scratch[at, LANES:] = out.astype(BF)


def backward_kernel(
    first, low_ref, me_ref, spot_ref, q_ref, k1_ref, k2_ref, v1_ref, v2_ref, start_ref, lse_ref, mixed_ref, grad_ref, cos_ref, sin_ref, dq_ref, dkk_ref,
    dks_ref, dvk_ref, dvs_ref, qa, qb, ga, gb, ta, tb, dk_all, dv_all, weights, grads,
):
    rows = q_ref.shape[1]
    stream = first + pl.program_id(0)
    me = me_ref[0]
    masked_heads(q_ref, SAME, qa, rows)
    masked_heads(q_ref, OTHER, qb, rows)
    masked_heads(grad_ref, SAME, ga, rows)
    masked_heads(grad_ref, OTHER, gb, rows)
    lane = lane_iota((rows, LANES))
    for heads, g in ((SAME, ga), (OTHER, gb)):
        for slot, h in enumerate(heads):
            at = slice(slot * rows, (slot + 1) * rows)
            cols = slice(h // 2 * LANES, h // 2 * LANES + LANES)
            keep = (lane >= HD) if h % 2 else (lane < HD)
            product = grad_ref[0, :, cols].astype(F32) * mixed_ref[0, :, cols].astype(F32)
            delta = jnp.sum(jnp.where(keep, product, 0.0), axis=-1, keepdims=True)
            put_column(g, at, -delta, rows)
    ta[...] = jnp.zeros_like(ta)
    tb[...] = jnp.zeros_like(tb)
    dk_all[...] = jnp.zeros_like(dk_all)
    dv_all[...] = jnp.zeros_like(dv_all)
    keys = GROUP * rows
    ones = (lane_iota((keys, LANES)) < 3).astype(F32).astype(BF)

    def step(j, carry):
        key = gathered(k1_ref, k2_ref, spot_ref, 0, j)
        value = gathered(v1_ref, v2_ref, spot_ref, 1, j)
        grad_keys = []
        grad_values = []
        for row, (q, g, t) in enumerate(((qa, ga, ta), (qb, gb, tb))):
            width = q.shape[0]
            k = swapped(key) if row else key
            v = jnp.concatenate([swapped(value) if row else value, ones], 1)
            for cols in chunks(width):
                s = nt(k, q[cols]) - lse_ref[0, row : row + 1, cols]
                p = jnp.exp(jnp.where(allowed_pairs(start_ref, j * keys, keys, cols), s, NEG))
                weights[:, cols] = p.astype(BF)
                grads[:, cols] = (p * nt(v, g[cols])).astype(BF)
            grad_values.append(nn(weights[:, :width], g[:, :LANES]))
            grad_keys.append(nn(grads[:, :width], q[...]))
            t[...] += nn(k.T, grads[:, :width])
        for out_ref, (same, other) in ((dk_all, grad_keys), (dv_all, grad_values)):
            total = (same + swapped(other)).astype(BF)
            out_ref[pl.ds(j * GROUP, GROUP)] = total.reshape(GROUP, rows, KW)
        return carry

    lax.fori_loop(low_ref[stream], me // GROUP + 1, step, 0)
    half = dkk_ref.shape[0]
    for which, (keep_ref, send_ref, out_ref) in enumerate(((dkk_ref, dks_ref, dk_all), (dvk_ref, dvs_ref, dv_all))):
        for spot in range(half):
            keep_ref[spot, 0] = out_ref[spot_ref[2 + which, spot]]
            send_ref[spot, 0] = out_ref[spot_ref[2 + which, half + spot]]
    parts = {}
    for heads, t in ((SAME, ta), (OTHER, tb)):
        flat = t[...].T
        for slot, h in enumerate(heads):
            parts[h] = flat[slot * rows : (slot + 1) * rows]
    cos = cos_ref[0]
    sin = sin_ref[0]
    for pair in range(HEADS // 2):
        both = jnp.where(lane < HD, parts[2 * pair], parts[2 * pair + 1]) * HD**-0.5
        dq_ref[0, :, pair * LANES : (pair + 1) * LANES] = (both * cos - half_swap(both) * sin).astype(BF)


def attend_back(first, streams, q, k_all, v_all, start_rows, low, me, spots, lse, mixed, grad, cos, sin):
    rows, width = q.shape[1:]
    half = k_all[0].shape[0]
    n = 2 * half
    a, b = len(SAME) * rows, len(OTHER) * rows
    tok = lambda w: pl.BlockSpec((1, rows, w), lambda s, *_: (s + first, 0, 0))
    two = pl.BlockSpec((1, 2, a), lambda s, *_: (s + first, 0, 0))
    key_spec = pl.BlockSpec((n // 2, 1, rows, KW), lambda s, *_: (0, s, 0, 0))
    return pl.pallas_call(
        functools.partial(backward_kernel, first),
        grid_spec=pltpu.PrefetchScalarGridSpec(
            num_scalar_prefetch=3,
            grid=(streams,),
            in_specs=[
                tok(width),
                *[pl.BlockSpec((half, 1, rows, KW), lambda s, *_: (0, s + first, 0, 0))] * 4,
                two,
                two,
                tok(width),
                tok(width),
                tok(LANES),
                tok(LANES),
            ],
            out_specs=[pl.BlockSpec((1, rows, width), lambda s, *_: (s, 0, 0)), *[key_spec] * 4],
            scratch_shapes=[
                pltpu.VMEM((a, LANES), BF),
                pltpu.VMEM((b, LANES), BF),
                pltpu.VMEM((a, 2 * LANES), BF),
                pltpu.VMEM((b, 2 * LANES), BF),
                pltpu.VMEM((LANES, a), F32),
                pltpu.VMEM((LANES, b), F32),
                *[pltpu.VMEM((n, rows, KW), BF)] * 2,
                *[pltpu.VMEM((GROUP * rows, a), BF)] * 2,
            ],
        ),
        out_shape=(
            jax.ShapeDtypeStruct((streams, rows, width), BF),
            *[jax.ShapeDtypeStruct((n // 2, streams, rows, KW), BF)] * 4,
        ),
        compiler_params=params(),
        cost_estimate=cost(8 * streams),
        name="attend_back",
    )(low, me, spots, q, *k_all, *v_all, start_rows, lse, mixed, grad, cos, sin)


TILE = 256


def mlp_kernel(
    valid, mine_ref, theirs_ref, sm_ref, st_ref, order_ref, wg_ref, wu_ref, wd_ref, om_ref, ot_ref, bm_ref, bt_ref,
    td_ref, gk_ref, gs_ref, uk_ref, us_ref, n_ref, s_ref, turned_ref,
):
    rows = mine_ref.shape[0]
    step = pl.program_id(0)
    sums = (om_ref, ot_ref, bm_ref, bt_ref)

    @pl.when(step == 0)
    def _():
        n_ref[:rows] = mine_ref[...]
        n_ref[rows:] = theirs_ref[...]
        s_ref[:rows] = sm_ref[...]
        s_ref[rows:] = st_ref[...]
        turned_ref[...] = nt(order_ref[...], n_ref[...]).astype(BF)
        for ref in sums:
            ref[...] = jnp.zeros_like(ref)

    normed = n_ref[...]
    seed = s_ref[...]
    left = valid - step * TILE
    inside = lambda w, dim: jnp.where(lax.broadcasted_iota(jnp.int32, w.shape, dim) < left, w, jnp.zeros_like(w))
    wg, wu, wd = inside(wg_ref[...], 1), inside(wu_ref[...], 1), inside(wd_ref[...], 0)
    gate = nn(normed, wg)
    up = nn(normed, wu)
    grad = nt(seed, wd)
    sig = 1.0 / (1.0 + jnp.exp(-gate))
    silu = gate * sig
    active = (silu * up).astype(BF)
    grad_up = (grad * silu).astype(BF)
    grad_gate = (grad * up * (sig * (1.0 + gate * (1.0 - sig)))).astype(BF)
    td_ref[...] = tn(active, seed).astype(BF)
    quarter = gk_ref.shape[0] // 2
    rows_of = lambda a, i: a[i * quarter : (i + 1) * quarter]
    for grad_pre, keep, send, quarters in ((grad_gate, gk_ref, gs_ref, (0, 1, 2, 3)), (grad_up, uk_ref, us_ref, (0, 2, 1, 3))):
        term = nn(turned_ref[...], grad_pre).astype(BF)
        for i in range(2):
            keep[i * quarter : (i + 1) * quarter] = rows_of(term, quarters[i])
            send[i * quarter : (i + 1) * quarter] = rows_of(term, quarters[2 + i])
    out = nn(active, wd)
    back = nt(grad_gate, wg) + nt(grad_up, wu)
    for ref, part in zip(sums, (out[:rows], out[rows:], back[:rows], back[rows:])):
        ref[...] += part


def fixed(*shape):
    return pl.BlockSpec(shape, lambda *_: (0,) * len(shape))


def shaped(dtype, *dims):
    return jax.ShapeDtypeStruct(dims, dtype)


def mlp(mine, theirs, seed_mine, seed_theirs, order, w_gate, w_up, w_d):
    rows, width = mine.shape
    half = w_gate.shape[1]
    cols = lambda size: pl.BlockSpec((size, TILE), lambda i: (0, i))
    down = pl.BlockSpec((TILE, width), lambda i: (i, 0))
    part = fixed(rows, width)
    return pl.pallas_call(
        functools.partial(mlp_kernel, half),
        grid=(pl.cdiv(half, TILE),),
        in_specs=[part] * 4 + [fixed(width, width)] + [cols(width)] * 2 + [down],
        out_specs=[part] * 4 + [down] + [cols(width // 2)] * 4,
        out_shape=[shaped(F32, rows, width)] * 4 + [shaped(BF, half, width)] + [shaped(BF, width // 2, half)] * 4,
        scratch_shapes=[pltpu.VMEM((2 * rows, width), BF)] * 2 + [pltpu.VMEM((width, 2 * rows), BF)],
        compiler_params=params(),
        cost_estimate=cost(40),
        name="mlp",
    )(mine, theirs, seed_mine, seed_theirs, order, w_gate, w_up, w_d)


def middle_kernel(bm_ref, bt_ref, middle_ref, seed_ref, g_ref, w_ref, gm_ref, gb_ref, gx_ref, gain_ref):
    @pl.when(pl.program_id(0) == 0)
    def _():
        gain_ref[...] = jnp.zeros_like(gain_ref)

    grad = bm_ref[...] + bt_ref[...]
    middle = middle_ref[...]
    inv = lax.rsqrt(jnp.mean(middle * middle, axis=-1, keepdims=True) + epsilon)
    unit = middle * inv
    scaled = grad * g_ref[...].astype(F32)
    grad_middle = seed_ref[...].astype(F32) + inv * (scaled - unit * jnp.mean(scaled * unit, axis=-1, keepdims=True))
    gm_ref[...] = grad_middle
    branch = grad_middle.astype(BF)
    gb_ref[...] = branch
    gx_ref[...] = nt(branch, w_ref[...]).astype(BF)
    gain_ref[...] += jnp.sum(grad * unit, axis=0, keepdims=True)


def middle_back(mine, theirs, middle, seed, gain, w_out):
    tokens, width = middle.shape
    rows = tokens // 4
    part = pl.BlockSpec((rows, width), lambda i: (i, 0))
    return pl.pallas_call(
        middle_kernel,
        grid=(4,),
        in_specs=[part] * 4 + [fixed(1, width), fixed(width, width)],
        out_specs=[part] * 3 + [fixed(1, width)],
        out_shape=[shaped(F32, tokens, width), shaped(BF, tokens, width), shaped(BF, tokens, width), shaped(F32, 1, width)],
        compiler_params=params(),
        cost_estimate=cost(5),
        name="middle_back",
    )(mine, theirs, middle, seed, gain, w_out)


def attention_terms_kernel(core_ref, normed_ref, mixed_ref, gq_ref, gb_ref, order_ref, sent_ref, kept_ref):
    first = core_ref[0] == 0
    order = order_ref[...]
    pick = lambda flag, a, b: jnp.where(jnp.broadcast_to(flag, a.shape), a[...], b[...])
    for out_ref, flag in ((sent_ref, first), (kept_ref, jnp.logical_not(first))):
        left = nt(order, pick(flag, normed_ref, mixed_ref)).astype(BF)
        out_ref[...] = nn(left, pick(flag, gq_ref, gb_ref)).astype(BF)


def attention_terms(core, normed, mixed, grad_q, grad_branch, order):
    width = normed.shape[1]
    whole = pl.BlockSpec(memory_space=pltpu.VMEM)
    return pl.pallas_call(
        attention_terms_kernel,
        in_specs=[pl.BlockSpec(memory_space=pltpu.SMEM)] + [whole] * 5,
        out_specs=[whole] * 2,
        out_shape=[shaped(BF, width, width)] * 2,
        compiler_params=params(),
        cost_estimate=cost(5),
        name="attention_terms",
    )(core, normed, mixed, grad_q, grad_branch, order)


def last_kernel(gkv_ref, gq_ref, w_ref, x_ref, g_ref, cos_ref, sin_ref, nt_ref, gm_ref, gain_ref, gi_ref, term_ref,
                sums_ref):
    grads = gkv_ref[...]
    keys = grads[:, :KW].astype(F32)
    keys = (keys * cos_ref[...] - half_swap(keys) * sin_ref[...]).astype(BF)
    grad_kv = jnp.concatenate([keys, grads[:, KW:]], 1)
    term_ref[...] = nn(nt_ref[...], grad_kv).astype(BF)
    grad = nt(gq_ref[...], w_ref[:, :QW]) + nt(grad_kv, w_ref[:, QW:])
    x = x_ref[...].astype(F32)
    inv = lax.rsqrt(jnp.mean(x * x, axis=-1, keepdims=True) + epsilon)
    unit = x * inv
    scaled = grad * g_ref[...].astype(F32)
    gi_ref[...] = gm_ref[...] + inv * (scaled - unit * jnp.mean(scaled * unit, axis=-1, keepdims=True))
    over = lambda a: jnp.sum(a.astype(F32), axis=0, keepdims=True)
    at = 0
    for row in (over(gq_ref[...]), over(grad_kv), over(grad * unit), gain_ref[...]):
        sums_ref[:, at : at + row.shape[1]] = row
        at += row.shape[1]


def last_back(grads, grad_q, w_qkv, x, gain, cos, sin, normed_t, grad_middle, gain_mlp_part):
    tokens, width = x.shape
    return pl.pallas_call(
        last_kernel,
        out_shape=[
            shaped(F32, tokens, width),
            shaped(BF, width, 2 * KW),
            shaped(F32, 1, QW + 2 * KW + 2 * width),
        ],
        compiler_params=params(),
        cost_estimate=cost(6),
        name="last_back",
    )(grads, grad_q, w_qkv, x, gain, cos, sin, normed_t, grad_middle, gain_mlp_part)


def after(a, *others):
    return lax.optimization_barrier((a, others))[0]


class Order:
    def __init__(self, token):
        self.token = token

    def enter(self, inputs):
        return lax.optimization_barrier((inputs, self.token))[0]

    def __call__(self, step, *inputs):
        self.token = step(*self.enter(inputs))
        return self.token


def other_core(a):
    return lax.ppermute(a, "dp", [(0, 1), (1, 0)])


def pair_up(a, axis, step):
    return lax.ppermute(a, axis, [(i, i ^ step) for i in range(lax.axis_size(axis))])


def total(terms):
    return functools.reduce(lambda a, b: a + b, [a.astype(F32) for a in terms]).astype(BF)


def add(a, b):
    return total((a, b))


Z, Y, X = SEQ
X_FIRST = ((X, 1), (Y, 1), (Z, 1), (Z, 2))
Y_FIRST = ((Y, 1), (X, 1), (Z, 1), (Z, 2))
Z_FIRST = ((Z, 1), (Y, 1), (X, 1), (Z, 2))
KEY_GATHER = ((Y, 1), (X, 1), (Z, 2), (Z, 1))
VALUE_GATHER = X_FIRST


def halving():
    return [lax.axis_size(axis) for axis in SEQ] == [4, 2, 2]


def my_bit(axis, step):
    return (lax.axis_index(axis) // step) % 2


def device_at(order, spot, relative):
    place = 0
    weight = {(X, 1): 1, (Y, 1): 2, (Z, 1): 4, (Z, 2): 8}
    for i, (axis, step) in enumerate(order):
        bit = (spot >> (len(order) - 1 - i)) & 1
        if relative:
            bit = bit ^ my_bit(axis, step)
        place = place + bit * weight[axis, step]
    return place


def spots_of_devices(order):
    n = lax.axis_size(SEQ)
    if not halving():
        return jnp.arange(n)
    spots = jnp.arange(n)
    return jnp.sum(jnp.where(device_at(order, spots, True)[:, None] == spots[None, :], spots[:, None], 0), 0)


def devices_at_spots(order):
    n = lax.axis_size(SEQ)
    return device_at(order, jnp.arange(n), True) if halving() else jnp.arange(n)


def row_order(order, width):
    n = lax.axis_size(SEQ)
    row = jnp.arange(width)
    source = row
    if halving():
        source = device_at(order, row // (width // n), True) * (width // n) + row % (width // n)
    return (source[:, None] == jnp.arange(width)[None, :]).astype(BF)


class Halving:
    def __init__(self, steps, arrays, rows, order=None, send=None):
        self.steps = list(steps)
        self.arrays = list(arrays)
        self.firsts = [0] * len(self.arrays)
        self.rows = rows
        if send is None:
            self.go(order)
        else:
            self.move(send)

    def halves(self):
        return 0, self.rows

    def move(self, send):
        self.arrays.append(pair_up(send, *self.steps.pop(0)))
        self.firsts.append(0)

    def sum(self, offset):
        cut = lambda a, first: lax.dynamic_slice_in_dim(a, first + offset, self.rows, 0)
        return total([cut(a, first) for a, first in zip(self.arrays, self.firsts)])

    def go(self, order):
        self.arrays = list(order.enter(self.arrays))
        if not self.steps:
            order.token = self.sum(0)
            return order.token
        self.rows //= 2
        kept, sent = self.halves()
        send = order.token = self.sum(sent)
        self.firsts = [first + kept for first in self.firsts]
        self.move(send)


class PlacedHalving(Halving):
    def halves(self):
        bit = my_bit(*self.steps[0])
        return bit * self.rows, (1 - bit) * self.rows


class PairHalving:
    def __init__(self, a_keep, a_send, b_keep, b_send, orders=(X_FIRST, Y_FIRST)):
        rows = a_keep.shape[0]
        self.pair = [
            Halving(orders[0][:2], [a_keep], rows, send=a_send),
            Halving(orders[1][:2], [b_keep], rows, send=b_send),
        ]
        self.last = orders[0][2:]
        self.count = 0

    def go(self, order, which=None):
        if which is not None:
            return self.pair[which].go(order)
        self.count += 1
        a, b = self.pair
        if self.count == 1:
            a.arrays, b.arrays = order.enter((list(a.arrays), list(b.arrays)))
            both = order.token = jnp.concatenate([a.sum(0), b.sum(0)], 1)
            half = both.shape[0] // 2
            self.rest = Halving(self.last, [both], half, send=both[half:])
        else:
            return self.rest.go(order)


def reduce_rows(a):
    return lax.psum_scatter(a, SEQ, scatter_dimension=0, tiled=True)


class Doubling:
    def __init__(self, order, a):
        self.steps = list(reversed(order))
        self.all = a[None]
        self.got = pair_up(self.all, *self.steps.pop(0))

    def go(self, order):
        if not self.steps:
            return self.all, self.got
        self.all = order(lambda a, b: jnp.concatenate([a, b], 0), self.all, self.got)
        self.got = pair_up(self.all, *self.steps.pop(0))


def to_owner(a, order):
    n = lax.axis_size(SEQ)
    holder = [device_at(order, spot, False) for spot in range(n)] if halving() else list(range(n))
    pairs = [(holder[spot] * 2 + core, core * n + spot) for spot in range(n) for core in range(2)]
    return lax.ppermute(a, (*SEQ, "dp"), pairs)


def sum_over_all(a):
    for axis in ("dp", *SEQ[::-1]):
        size = lax.axis_size(axis)
        step = 1
        while step < size:
            a = a + lax.ppermute(a, axis, [(i, i ^ step) for i in range(size)])
            step *= 2
    return a


def layout(lengths, offset, row_count):
    places = offset + jnp.arange(row_count, dtype=jnp.int32)
    slots = jnp.arange(lengths.shape[1])
    ends = jnp.sum(jnp.where(slots[:, None] <= slots[None, :], lengths[:, :, None], 0), axis=1)
    after = (places[None, :, None] >= ends[:, None, :]).astype(jnp.int32)
    begins = jnp.sum(after * lengths[:, None, :], axis=-1, dtype=jnp.int32)
    return (places, begins, places[None, :] < ends[:, -1:])


def shards(inputs, lengths, w_qkv, b_qkv, g_attn, w_out, g_mlp, w_gate_up, w_down, cotangent):
    streams, length, width = inputs.shape
    tokens = streams * length
    n = 1
    for axis in SEQ:
        n *= lax.axis_size(axis)
    me = lax.axis_index(SEQ)
    core = lax.axis_index("dp")
    offset = me * length
    places, begins, valid = layout(lengths, offset, length)
    frequency = rope_base ** (-(jnp.arange(HD // 2, dtype=F32) * (2.0 / HD)))
    lane_frequency = jnp.tile(frequency, LANES // (HD // 2))
    sign = jnp.where(jnp.arange(LANES) % HD < HD // 2, -1.0, 1.0)
    angle = (places[None, :] - begins).astype(F32).reshape(tokens, 1) * lane_frequency
    cos = jnp.cos(angle)
    sin = jnp.sin(angle) * sign

    x = inputs.reshape(tokens, width)
    small = jnp.concatenate([b_qkv, g_attn]).reshape(1, -1)
    normed, k, v = project_kv(x, w_qkv, small, cos, sin)
    k, v = k.reshape(streams, length, KW), v.reshape(streams, length, KW)
    half = FF // 2

    def small_inputs(begins):
        start_rows = jnp.stack(
            [
                jnp.tile(begins, (1, len(SAME))),
                jnp.tile(jnp.broadcast_to(places[None], begins.shape), (1, len(SAME))),
            ],
            1,
        )
        spots = jnp.stack(
            [*map(spots_of_devices, (KEY_GATHER, VALUE_GATHER)), *map(devices_at_spots, (Y_FIRST, X_FIRST))]
        ).astype(jnp.int32)
        return start_rows, spots, row_order(X_FIRST, width)

    cut_cols = lambda w, first: lax.dynamic_slice_in_dim(w, first + core * half, half, 1)
    cut_rows = lambda w: lax.dynamic_slice_in_dim(w, core * half, half, 0)
    fast = halving()
    order = Order(k)
    if fast:
        keys = Doubling(KEY_GATHER, k)
        values = Doubling(VALUE_GATHER, v)
        q = order(project_q, normed, w_qkv, small, cos, sin)
        keys.go(order), values.go(order)
        seed = order(lambda c: (c * valid[..., None].astype(BF)).reshape(tokens, width), cotangent)
        w_gate = order(functools.partial(cut_cols, first=0), w_gate_up)
        keys.go(order), values.go(order)
        w_up = order(functools.partial(cut_cols, first=FF), w_gate_up)
        w_d = order(cut_rows, w_down)
        keys.go(order), values.go(order)
        seed_theirs = other_core(seed)
        start_rows, spots, order_x = order(small_inputs, begins)
        normed_t = order(lambda a, b: nt(a, b).astype(BF), order_x, normed)
        k_all, v_all = keys.go(order), values.go(order)
    else:
        in_halves = lambda a: (a[: n // 2], a[n // 2 :])
        k_all, v_all = [in_halves(lax.all_gather(a, SEQ, axis=0)) for a in (k, v)]
        q = project_q(normed, w_qkv, small, cos, sin)
        seed = (cotangent * valid[..., None].astype(BF)).reshape(tokens, width)
        seed_theirs = other_core(seed)
        w_gate, w_up, w_d = cut_cols(w_gate_up, 0), cut_cols(w_gate_up, FF), cut_rows(w_down)
        start_rows, spots, order_x = small_inputs(begins)
        normed_t = nt(order_x, normed).astype(BF)
    low = begins[:, 0] // (GROUP * length)
    me_1 = jnp.reshape(me, (1,)).astype(jnp.int32)
    q = q.reshape(streams, length, QW)
    mixed, lse = attend(q, k_all, v_all, start_rows, low, me_1, spots)
    mixed_flat = mixed.reshape(tokens, QW)
    middle = x.astype(F32) + nn(mixed_flat, w_out)
    inv_mlp = lax.rsqrt(jnp.mean(middle * middle, axis=-1, keepdims=True) + epsilon)
    unit_mlp = middle * inv_mlp
    gain_mlp = g_mlp.astype(F32)
    normed_mlp = (unit_mlp * gain_mlp).astype(BF)
    normed_theirs = other_core(normed_mlp)
    out_mine, out_theirs, back_mine, back_theirs, term_down, keep_gate, send_gate, keep_up, send_up = mlp(
        normed_mlp, normed_theirs, seed, seed_theirs, order_x, w_gate, w_up, w_d
    )
    order = Order(back_mine)
    back_theirs = other_core(back_theirs)
    out_theirs = other_core(out_theirs)
    if fast:
        gate_up = PairHalving(keep_gate, send_gate, keep_up, send_up)
        down = PlacedHalving(Z_FIRST, [term_down], half, order)

    grad_middle, grad_branch, grad_mixed, gain_mlp_part = order(
        middle_back, back_mine, back_theirs, middle, seed, g_mlp.reshape(1, -1), w_out
    )
    grad_mixed = grad_mixed.reshape(streams, length, QW)

    cos_s = cos.reshape(streams, length, LANES)
    sin_s = sin.reshape(streams, length, LANES)
    back = lambda first, count: attend_back(
        first, count, q, k_all, v_all, start_rows, low, me_1, spots, lse, mixed, grad_mixed, cos_s, sin_s
    )

    core_1 = jnp.reshape(core, (1,)).astype(jnp.int32)
    gain_attn = g_attn.reshape(1, -1)

    def finish(mine, theirs, middle):
        return (middle + mine + theirs).astype(BF)

    def both_cores(mine, dim):
        theirs = other_core(mine)
        first = jnp.where(core == 0, mine, theirs)
        second = jnp.where(core == 0, theirs, mine)
        return jnp.concatenate([first, second], dim).astype(F32)

    if fast:
        per = streams // PARTS
        rows = (n // 2) * per * length
        grads_q = []
        at = {"down": down, "gu": gate_up}
        value = {}

        def back_step(which):
            grad_q, *grads = attend_back(
                per * which, per, q, k_all, v_all, start_rows, low, order.enter(me_1), spots, lse, mixed, grad_mixed, cos_s, sin_s
            )
            order.token = grad_q
            grads_q.append(grad_q.reshape(per * length, QW))
            at["keys", which] = PairHalving(*[g.reshape(rows, KW) for g in grads], orders=(Y_FIRST, X_FIRST))

        def terms_step():
            value["q"] = jnp.concatenate(grads_q, 0)
            sent, kept = order(attention_terms, core_1, normed, mixed_flat, value["q"], grad_branch, order_x)
            value["attn"] = kept, other_core(sent)

        def attn_step():
            value["attn"] = order(add, *value["attn"])
            at["attn"] = Halving(X_FIRST, [value["attn"]], width, order)

        def last_step():
            grads = jnp.concatenate([value[f"keys:{i}"] for i in range(PARTS)], 0)
            value["input"], term, sums = order(
                last_back, grads, value["q"], w_qkv, x, gain_attn, cos, sin, normed_t,
                grad_middle, gain_mlp_part,
            )
            block = width // n
            extra = jnp.pad(sums.astype(BF).reshape(-1, LANES), ((0, block - sums.size // LANES), (0, 0)))
            term = order(lambda t, e: jnp.concatenate([t, jnp.tile(e, (n, 1))], 1), term, extra)
            at["kv"] = Halving(X_FIRST, [term], width, order)

        def finish_step():
            value["output"] = order(finish, out_mine, out_theirs, middle)

        steps = {"ab": back_step, "terms": terms_step, "attn0": attn_step, "last": last_step}
        steps["finish"] = finish_step
        for name in PLAN:
            head, *rest = name.split(":")
            rest = [int(r) for r in rest]
            if head in steps:
                steps[head](*rest)
            elif head == "gu":
                value[name] = gate_up.go(order, *rest)
            elif head == "keys":
                value[name] = at[head, rest[0]].go(order, *rest[1:])
            else:
                value[name] = at[name].go(order)
        output, grad_input = value["output"], value["input"]
        rows_gate, rows_up = value["gu"][:, :half], value["gu"][:, half:]
        rows_down, rows_attn, rows_kv = value["down"], value["attn"], value["kv"]
        rows_kv = add(rows_kv, other_core(rows_kv))
        sums = rows_kv[:, 2 * KW :].astype(F32).reshape(-1)
    else:
        grad_q, *grads = back(0, streams)
        grad_q = grad_q.reshape(tokens, QW)
        sent, kept = attention_terms(core_1, normed, mixed_flat, grad_q, grad_branch, order_x)
        rows_attn = reduce_rows(add(kept, other_core(sent)))
        output = finish(out_mine, out_theirs, middle)
        grad_k, grad_v = [reduce_rows(jnp.concatenate(g, 0).reshape(n * tokens, KW)) for g in (grads[:2], grads[2:])]
        grad_kv = jnp.concatenate([grad_k, grad_v], 1)
        grad_input, term, sums = last_back(
            grad_kv, grad_q, w_qkv, x, gain_attn, cos, sin, normed_t, grad_middle,
            gain_mlp_part,
        )
        rows_kv = reduce_rows(term)
        rows_kv = add(rows_kv, other_core(rows_kv))
        sums = sum_over_all(sums.reshape(-1, LANES)).reshape(-1)
        rows_gate = reduce_rows(jnp.concatenate([keep_gate, send_gate], 0))
        cut_up = keep_up.shape[0] // 2
        rows_up = reduce_rows(jnp.concatenate([keep_up[:cut_up], send_up[:cut_up], keep_up[cut_up:], send_up[cut_up:]], 0))
        rows_down = reduce_rows(term_down)

    rows_down = to_owner(rows_down, Z_FIRST)
    rows_attn = both_cores(rows_attn, 1)
    rows_out, rows_q = rows_attn[:, :width], rows_attn[:, width:]
    small = [QW + 2 * KW, QW + 2 * KW + width, QW + 2 * KW + 2 * width]
    bias_grad, gain_attn_grad, gain_mlp_grad, _ = jnp.split(sums, small)
    return (
        output.reshape(streams, length, width),
        grad_input.reshape(streams, length, width),
        jnp.concatenate([rows_q, rows_kv[:, : 2 * KW].astype(F32)], 1),
        bias_grad,
        gain_attn_grad,
        rows_out,
        gain_mlp_grad,
        jnp.concatenate([both_cores(rows_gate, 1), both_cores(rows_up, 1)], 1),
        both_cores(rows_down, 0),
    )


PARTS = 1
PLAN = (
    "ab:0", "terms", "gu:0", "gu:1", "keys:0:0", "keys:0:1", "keys:0", "down", "attn0", "keys:0", "gu",
    "finish", "keys:0", "attn", "down", "last", "gu", "kv", "attn", "down", "kv", "attn", "kv", "gu", "down",
    "attn", "kv",
)


def solution(mesh):
    n = mesh.shape["seq"]
    sizes = {16: (4, 2, 2), 64: (4, 4, 4)}.get(n, (n, 1, 1))
    fine = Mesh(np.asarray(mesh.devices).reshape(*sizes, mesh.shape["dp"]), (*SEQ, "dp"))
    in_specs = (P("dp", SEQ, None), P("dp", None), P(), P(), P(), P(), P(), P(), P(), P("dp", SEQ, None))
    out_specs = (
        P("dp", SEQ, None), P("dp", SEQ, None), P(SEQ, None), P(), P(), P(SEQ, None), P(), P(SEQ, None), P(SEQ, None),
    )
    return jax.shard_map(shards, mesh=fine, in_specs=in_specs, out_specs=out_specs, check_vma=False)
```
